32 devices in a mesh: dp: 8 (over y, x, core), tensor: 4 (over z).
Axes of the slice: x: 2, y: 2, z: 4, core: 2. Of those that a mesh axis runs over, the one named last changes fastest.
Arguments:
- tokens: bfloat16 [8192, 1536], P('dp'), may hold values from -6 to 6
- block_order: int32 [1, 8], replicated, may hold values from 0 to 7, each once within a row
- attn_gain: float32 [1536], replicated, may hold values from 0.5 to 1.5
- w_query: bfloat16 [1536, 1536], P(None, 'tensor'), may hold values from -0.15625 to 0.15625
- w_key: bfloat16 [1536, 768], P(None, 'tensor'), may hold values from -0.15625 to 0.15625
- w_value: bfloat16 [1536, 768], P(None, 'tensor'), may hold values from -0.15625 to 0.15625
- w_out: bfloat16 [1536, 1536], P('tensor'), may hold values from -1.25 to 1.25
- mlp_gain: float32 [1536], replicated, may hold values from 0.5 to 1.5
- w_gate: bfloat16 [1536, 4096], P(None, 'tensor'), may hold values from -0.15625 to 0.15625
- w_up: bfloat16 [1536, 4096], P(None, 'tensor'), may hold values from -0.15625 to 0.15625
- w_down: bfloat16 [4096, 1536], P('tensor'), may hold values from -0.09375 to 0.09375
- cotangent: bfloat16 [8192, 1536], P('dp'), may hold values from -6 to 6
Outputs:
- activations: bfloat16 [8192, 1536], P('dp')
- grad_tokens: bfloat16 [8192, 1536], P('dp')
- grad_attn_gain: float32 [1536], replicated
- grad_query: float32 [1536, 1536], P(None, 'tensor')
- grad_key: float32 [1536, 768], P(None, 'tensor')
- grad_value: float32 [1536, 768], P(None, 'tensor')
- grad_out: float32 [1536, 1536], P('tensor')
- grad_mlp_gain: float32 [1536], replicated
- grad_gate: float32 [1536, 4096], P(None, 'tensor')
- grad_up: float32 [1536, 4096], P(None, 'tensor')
- grad_down: float32 [4096, 1536], P('tensor')
The draws below stay inside these ranges and needn't reach their ends.
Inputs may be any that keep to these rules, and one draw needn't show every extreme that they name: `block_order`: entry j of row g is the prompt block of 512 tokens held by the j-th device of group g; each row is a permutation.
All inputs are finite; a program needn't handle non-finite values.
Results may differ from the reference program's by a relative error of at most 0.02.
Values may be sent and summed in bfloat16 or wider, within the bound.
A program may use at most 192 MiB of HBM per device.

```python
import jax
import jax.numpy as jnp
from jax import lax

D = 1536
HEADS = 16
KV_HEADS = 8
HEAD_DIM = 96
FF = 4096
GROUP_DEVS = 8
PB = 512
CL = 512
TOK_DEV = 1024
PROMPT = 4096
GROUPS = 1
TOKENS = 8192
N_TENSOR = 4


def level_of(own_key, shape, cuts, low, high):
    factor_of, own = 1.0, jax.random.fold_in(own_key, 6)
    for position, shards_of in cuts:
        draws = jnp.exp(jax.random.uniform(jax.random.fold_in(own, position), (shards_of,), jnp.float32, low / len(cuts), high / len(cuts)))
        factor_of = factor_of * jnp.repeat(draws, shape[position] // shards_of).reshape([-1 if axis == position else 1 for axis in range(len(shape))])
    return factor_of


def gaussian(rng, dims, deviation, reach, split=(), kind=jnp.bfloat16):
    values = deviation * jax.random.normal(rng, dims, jnp.float32)
    if split:
        values = values * level_of(rng, dims, split, -0.22, 0.18)
    return jnp.clip(values, -reach, reach).astype(kind)


def setup_inputs(seed: int = 0) -> dict:
    streams_of = jax.random.split(jax.random.key(seed), 13)
    tokens = gaussian(streams_of[0], (TOKENS, D), 1.0, 6.0, ((0, 8),))
    block_order = jax.vmap(lambda own: jax.random.permutation(own, GROUP_DEVS))(jax.random.split(streams_of[1], GROUPS)).reshape((GROUPS, GROUP_DEVS)).astype(jnp.int32)
    attn_gain = jnp.clip(1.0 + 0.1 * jax.random.normal(streams_of[2], (D,), jnp.float32), 0.5, 1.5)
    w_query = gaussian(streams_of[3], (D, HEADS * HEAD_DIM), D ** -0.5, 0.15625, ((1, 4),))
    w_key = gaussian(streams_of[4], (D, KV_HEADS * HEAD_DIM), D ** -0.5, 0.15625, ((1, 4),))
    w_value = gaussian(streams_of[5], (D, KV_HEADS * HEAD_DIM), D ** -0.5, 0.15625, ((1, 4),))
    w_out = gaussian(streams_of[6], (HEADS * HEAD_DIM, D), (max(HEADS * HEAD_DIM // 64, 1)) ** -0.5, 1.25, ((0, 4),))
    mlp_gain = jnp.clip(1.0 + 0.1 * jax.random.normal(streams_of[7], (D,), jnp.float32), 0.5, 1.5)
    w_gate = gaussian(streams_of[8], (D, FF), D ** -0.5, 0.15625, ((1, 4),))
    w_up = gaussian(streams_of[9], (D, FF), D ** -0.5, 0.15625, ((1, 4),))
    w_down = gaussian(streams_of[10], (FF, D), FF ** -0.5, 0.09375, ((0, 4),))
    cotangent = gaussian(streams_of[11], (TOKENS, D), 1.0, 6.0, ((0, 8),))
    return dict(tokens=tokens, block_order=block_order, attn_gain=attn_gain, w_query=w_query, w_key=w_key, w_value=w_value, w_out=w_out, mlp_gain=mlp_gain, w_gate=w_gate, w_up=w_up, w_down=w_down, cotangent=cotangent)


@jax.custom_vjp
def low(v):
    return lax.optimization_barrier(v.astype(jnp.bfloat16)).astype(jnp.float32)

@jax.custom_vjp
def low_back(v):
    return v

def low_keep(v):
    return (low(v), None)

def low_pass(kept, grad):
    return (grad,)

def back_keep(v):
    return (v, None)

def back_low(kept, grad):
    return (low(grad),)
low.defvjp(low_keep, low_pass)
low_back.defvjp(back_keep, back_low)
EPSILON = 1e-05
ROTARY_BASE = 100000.0

def widen(former, latter):
    return jnp.dot(former, latter, precision=lax.Precision.HIGHEST, preferred_element_type=jnp.float32)

def turn(inputs, places):
    halfway = HEAD_DIM // 2
    frequency = ROTARY_BASE ** (-(jnp.arange(halfway, dtype=jnp.float32) * 2.0) / HEAD_DIM)
    angle = places.astype(jnp.float32)[:, None] * frequency[None, :]
    cosine_table = jnp.concatenate([jnp.cos(angle), jnp.cos(angle)], axis=-1)[:, None, :]
    sine_table = jnp.concatenate([jnp.sin(angle), jnp.sin(angle)], axis=-1)[:, None, :]
    turned = jnp.concatenate([-inputs[..., halfway:], inputs[..., :halfway]], axis=-1)
    return inputs * cosine_table + turned * sine_table

def attend(block):
    queries, key_block, value_block, query_places, key_places = block
    products = jnp.einsum('rqd,nd->rqn', queries, key_block, precision=lax.Precision.HIGHEST) * HEAD_DIM ** (-0.5)
    scores = low_back(products)
    visible = key_places[None, None, :] <= query_places[None, :, None]
    masked = jnp.where(visible, scores, -1e+30)
    summit = lax.optimization_barrier(jnp.max(masked, axis=-1, keepdims=True))
    powers = jnp.where(visible, jnp.exp(masked - summit), 0.0)
    weights = low(powers / lax.optimization_barrier(jnp.sum(powers, axis=-1, keepdims=True)))
    return jnp.einsum('rqn,nd->rqd', weights, value_block, precision=lax.Precision.HIGHEST)

def gather_keys(per_token):
    spread = per_token.reshape(GROUPS, GROUP_DEVS, TOK_DEV, KV_HEADS, HEAD_DIM)
    prompt_part = spread[:, :, :PB].reshape(GROUPS, 1, PROMPT, KV_HEADS, HEAD_DIM)
    joined = jnp.concatenate([jnp.broadcast_to(prompt_part, (GROUPS, GROUP_DEVS, PROMPT, KV_HEADS, HEAD_DIM)), spread[:, :, PB:]], axis=2)
    return joined.transpose(0, 1, 3, 2, 4).reshape(GROUPS * GROUP_DEVS * KV_HEADS, PROMPT + CL, HEAD_DIM)

def reference(tokens, block_order, attn_gain, w_query, w_key, w_value, w_out, mlp_gain, w_gate, w_up, w_down, cotangent):
    offsets = jnp.arange(PB, dtype=jnp.int32)
    tail_places = (PROMPT + jnp.arange(CL, dtype=jnp.int32)).astype(jnp.int32)
    prompt_places = (block_order[:, :, None] * PB + offsets[None, None, :]).astype(jnp.int32)
    tail_broad = jnp.broadcast_to(tail_places[None, None, :], (GROUPS, GROUP_DEVS, CL))
    query_places = jnp.concatenate([prompt_places, tail_broad], axis=2)
    key_places = jnp.concatenate([jnp.broadcast_to(prompt_places.reshape(GROUPS, 1, PROMPT), (GROUPS, GROUP_DEVS, PROMPT)), tail_broad], axis=2)
    places = query_places.reshape(TOKENS)
    query_lists = jnp.broadcast_to(query_places[:, :, None, :], (GROUPS, GROUP_DEVS, KV_HEADS, TOK_DEV)).reshape(-1, TOK_DEV)
    key_lists = jnp.broadcast_to(key_places[:, :, None, :], (GROUPS, GROUP_DEVS, KV_HEADS, PROMPT + CL)).reshape(-1, PROMPT + CL)
    repeat = HEADS // KV_HEADS
    head_cols = HEADS * HEAD_DIM // N_TENSOR
    unit_cols = FF // N_TENSOR

    def layer(inputs, attn_gain, w_query, w_key, w_value, w_out, mlp_gain, w_gate, w_up, w_down):
        normed = low(inputs * lax.rsqrt(lax.optimization_barrier(jnp.mean(inputs * inputs, axis=-1, keepdims=True)) + EPSILON) * attn_gain)
        queries = low(turn(low_back(widen(normed, w_query)).reshape(TOKENS, HEADS, HEAD_DIM), places))
        key_set = low(turn(low_back(widen(normed, w_key)).reshape(TOKENS, KV_HEADS, HEAD_DIM), places))
        value_set = low(low_back(widen(normed, w_value))).reshape(TOKENS, KV_HEADS, HEAD_DIM)
        query_blocks = queries.reshape(GROUPS, GROUP_DEVS, TOK_DEV, KV_HEADS, repeat, HEAD_DIM).transpose(0, 1, 3, 4, 2, 5).reshape(-1, repeat, TOK_DEV, HEAD_DIM)
        attended = lax.map(jax.checkpoint(attend), (query_blocks, gather_keys(key_set), gather_keys(value_set), query_lists, key_lists))
        attended = attended.reshape(GROUPS, GROUP_DEVS, KV_HEADS, repeat, TOK_DEV, HEAD_DIM).transpose(0, 1, 4, 2, 3, 5).reshape(TOKENS, HEADS * HEAD_DIM)
        attended = low(low_back(attended))
        attention = jnp.zeros((TOKENS, D), jnp.float32)
        for shard_index in range(N_TENSOR):
            lower = shard_index * head_cols
            attention = attention + low(widen(attended[:, lower:lower + head_cols], w_out[lower:lower + head_cols]))
        middle = inputs + low_back(attention)
        normed_two = low(middle * lax.rsqrt(lax.optimization_barrier(jnp.mean(middle * middle, axis=-1, keepdims=True)) + EPSILON) * mlp_gain)
        gate_pre = low_back(widen(normed_two, w_gate))
        up_pre = low_back(widen(normed_two, w_up))
        hidden = low(jax.nn.silu(gate_pre) * up_pre)
        feed_out = jnp.zeros((TOKENS, D), jnp.float32)
        for shard_index in range(N_TENSOR):
            lower = shard_index * unit_cols
            feed_out = feed_out + low(widen(hidden[:, lower:lower + unit_cols], w_down[lower:lower + unit_cols]))
        return middle + low_back(feed_out)
    params = (tokens.astype(jnp.float32), attn_gain, w_query.astype(jnp.float32), w_key.astype(jnp.float32), w_value.astype(jnp.float32), w_out.astype(jnp.float32), mlp_gain, w_gate.astype(jnp.float32), w_up.astype(jnp.float32), w_down.astype(jnp.float32))
    result, pullback = jax.vjp(layer, *params)
    grads = pullback(cotangent.astype(jnp.float32))
    return (result.astype(jnp.bfloat16), grads[0].astype(jnp.bfloat16), grads[1], grads[2], grads[3], grads[4], grads[5], grads[6], grads[7], grads[8], grads[9])
```

```python
import functools

import jax
import jax.numpy as jnp
from jax import lax
from jax.experimental import pallas as pl
from jax.experimental.pallas import tpu as pltpu
from jax.sharding import PartitionSpec as P

HEAD_DIM = 96
GROUP_DEVS = 8
PB = 512
CL = 512
EPSILON = 1e-05
ROTARY_BASE = 100000.0
LOG2E = 1.4426950408889634
NEG = -1e30
MESH = pl.DeviceIdType.MESH
VM = pltpu.VMEM
F32 = jnp.float32
BF16 = jnp.bfloat16
NT = (((1,), (1,)), ((), ()))


def dot(a, b):
    return jnp.dot(a, b, preferred_element_type=F32)


def dot_nt(a, b):
    return lax.dot_general(a, b, NT, preferred_element_type=F32)


def dot_tn(a, b):
    return lax.dot_general(a, b, (((0,), (0,)), ((), ())), preferred_element_type=F32)


def causal(s):
    key = lax.broadcasted_iota(jnp.int32, s.shape, 0)
    query = lax.broadcasted_iota(jnp.int32, s.shape, 1)
    return jnp.where(key <= query, s, NEG)


def greet(targets):
    barrier = pltpu.get_barrier_semaphore()
    for target in targets:
        pl.semaphore_signal(barrier, inc=1, device_id=target, device_id_type=MESH)
    pl.semaphore_wait(barrier, len(targets))


def remote(src, dst, send, recv, target):
    return pltpu.make_async_remote_copy(
        src_ref=src, dst_ref=dst, send_sem=send, recv_sem=recv, device_id=target, device_id_type=MESH
    )


def forward_kernel(
    nz, q_ref, kv_ref, bias_ref, att, kv_all, lse_ref, acc, top, total, ktok, gs, gr, zs, zr
):
    heads = q_ref.shape[0]
    kvh = heads // 2
    d, z = lax.axis_index("dp"), lax.axis_index("tensor")
    peer = lambda m: (jnp.bitwise_xor(d, m), z)
    greet(
        [peer(1), peer(2), peer(4), peer(6)]
        + [(d, lax.rem(z + 1, nz)), (d, lax.rem(z + nz - 1, nz))]
    )
    own = kv_ref.at[:, :, pl.ds(0, PB)]
    firsts = [remote(own, kv_all.at[m], gs.at[m], gr.at[m], peer(m)) for m in (1, 2, 4, 6)]
    for copy in firsts:
        copy.start()
    kv_all[0] = kv_ref[:, :, 0:PB]
    for h in range(kvh):
        ktok[8, h] = kv_ref[h, :, PB : PB + CL].T
        ktok[0, h] = kv_ref[h, :, 0:PB].T
    acc[...] = jnp.zeros_like(acc)
    top[...] = jnp.full_like(top, NEG)
    total[...] = jnp.zeros_like(total)

    def block(head, half, key, value, mask, bias):
        cols = pl.ds(half * PB, PB)
        s = dot(key, q_ref[head, :, cols])
        if mask:
            s = causal(s)
        if bias is not None:
            s = s + bias
        old = top[head, :, cols]
        new = jnp.maximum(old, jnp.max(s, axis=0, keepdims=True))
        p = jnp.exp2(s - new)
        shrink = jnp.exp2(old - new)
        total[head, :, cols] = total[head, :, cols] * shrink + jnp.sum(p, axis=0, keepdims=True)
        acc[head, :, cols] = acc[head, :, cols] * shrink + dot(value, p.astype(BF16))
        top[head, :, cols] = new

    def slot_step(slot, half, mask=False, bias=None):
        for head in range(heads):
            block(head, half, ktok[slot, head // 2], kv_all[slot, kvh + head // 2], mask, bias)

    slot_step(0, 1)
    for head in range(heads):
        block(head, 1, ktok[8, head // 2], kv_ref[kvh + head // 2, :, PB : PB + CL], True, None)

    def arrive(m):
        remote(kv_all.at[m], kv_all.at[m], gs.at[m], gr.at[m], peer(1)).wait_recv()

    def hand_on(m):
        return remote(kv_all.at[m], kv_all.at[m + 1], gs.at[m + 1], gr.at[m + 1], peer(1))

    def tail_slot(m, carry):
        arrive(m)

        @pl.when(lax.rem(m, 2) == 0)
        def _():
            hand_on(m).start()

        for h in range(kvh):
            ktok[m, h] = kv_all[m, h].T
        slot_step(m, 1)
        return carry

    tail_slot(1, 0)
    slot_step(0, 0, mask=True)
    slot_step(1, 0, bias=bias_ref[1])
    lax.fori_loop(2, GROUP_DEVS, tail_slot, 0)

    rows = heads * HEAD_DIM

    def finish(half):
        cols = pl.ds(half * PB, PB)
        for head in range(heads):
            att[z, pl.ds(head * HEAD_DIM, HEAD_DIM), cols] = (
                acc[head, :, cols] / total[head, :, cols]
            ).astype(BF16)
            lse_ref[head, :, cols] = top[head, :, cols] + jnp.log2(total[head, :, cols])

    def piece(index, half):
        return att.at[index, :, pl.ds(half * PB, PB)]

    def z_send(right, half, s):
        index, target = (z - s, z + 1) if right else (z + s, z - 1)
        there = (z - s >= 0) & (z < nz - 1) if right else (z + s < nz) & (z > 0)
        where = piece(index, half)
        return there, remote(
            where, where, zs.at[half, int(right), s], zr.at[half, int(right), s], (d, target)
        )

    def z_arrive(right, half, s):
        index = z - 1 - s if right else z + 1 + s
        there = index >= 0 if right else index < nz
        where = piece(index, half)

        @pl.when(there)
        def _():
            remote(
                where, where, zs.at[half, int(right), s], zr.at[half, int(right), s], (d, z)
            ).wait_recv()

    def z_start(half, s):
        for right in (True, False):
            if s > 0:
                z_arrive(right, half, s - 1)
            there, copy = z_send(right, half, s)
            pl.when(there)(copy.start)

    def z_finish(half):
        for right in (True, False):
            z_arrive(right, half, nz - 2)
            for s in range(nz - 1):
                there, copy = z_send(right, half, s)
                pl.when(there)(copy.wait_send)

    def prompt_slot(m, carry):
        slot_step(m, 0, bias=bias_ref[m])
        return carry

    finish(1)
    z_start(1, 0)
    lax.fori_loop(2, 6, prompt_slot, 0)
    z_start(1, 1)
    lax.fori_loop(6, GROUP_DEVS, prompt_slot, 0)
    finish(0)
    z_start(0, 0)
    for s in range(2, nz - 1):
        z_start(1, s)
    for s in range(1, nz - 1):
        z_start(0, s)
    z_finish(1)
    z_finish(0)
    for copy in firsts:
        copy.wait_send()
    for m in (2, 4, 6):
        hand_on(m).wait_send()


def forward_attention(nz, q, kv, bias):
    heads, tokens = q.shape[0], q.shape[2]
    kvh = heads // 2
    return pl.pallas_call(
        functools.partial(forward_kernel, nz),
        out_shape=(
            jax.ShapeDtypeStruct((nz, heads * HEAD_DIM, tokens), BF16),
            jax.ShapeDtypeStruct((GROUP_DEVS, 2 * kvh, HEAD_DIM, PB), BF16),
            jax.ShapeDtypeStruct((heads, 1, tokens), F32),
        ),
        in_specs=[
            pl.BlockSpec(memory_space=VM),
            pl.BlockSpec(memory_space=VM),
            pl.BlockSpec(memory_space=pltpu.SMEM),
        ],
        out_specs=(pl.BlockSpec(memory_space=VM),) * 3,
        scratch_shapes=[
            VM((heads, HEAD_DIM, tokens), F32),
            VM((heads, 1, tokens), F32),
            VM((heads, 1, tokens), F32),
            VM((GROUP_DEVS + 1, kvh, PB, HEAD_DIM), BF16),
            pltpu.SemaphoreType.DMA((GROUP_DEVS,)),
            pltpu.SemaphoreType.DMA((GROUP_DEVS,)),
            pltpu.SemaphoreType.DMA((2, 2, nz - 1)),
            pltpu.SemaphoreType.DMA((2, 2, nz - 1)),
        ],
        compiler_params=pltpu.CompilerParams(
            collective_id=0, has_side_effects=True, vmem_limit_bytes=48 << 20
        ),
        cost_estimate=pl.CostEstimate(
            flops=40_000_000_000, bytes_accessed=12_000_000, transcendentals=19_000_000
        ),
        name="forward_attention",
    )(q, kv, bias)


def backward_kernel(
    q_ref, kv_ref, kv_all, do_ref, bias_ref, lse_ref, inner_ref, dq, dkv, dkv_tail, ktok, vtok
):
    heads = q_ref.shape[0]
    kvh = heads // 2
    dq[...] = jnp.zeros_like(dq)

    def block(head, half, keyt, slot, mask, bias):
        h = head // 2
        cols = pl.ds(half * PB, PB)
        s = dot(ktok[slot, h], q_ref[head, :, cols])
        if mask:
            s = causal(s)
        shift = lse_ref[head, :, cols]
        if bias is not None:
            shift = shift - bias
        p = jnp.exp2(s - shift)
        dp = dot(vtok[slot, h], do_ref[head, :, cols])
        ds = (p * (dp - inner_ref[head, :, cols])).astype(BF16)
        dq[head, :, cols] += dot(keyt, ds)
        dv = dot_nt(do_ref[head, :, cols], p.astype(BF16))
        dk = dot_nt(q_ref[head, :, cols], ds)
        return dk, dv

    def total(parts):
        out = parts[0]
        for part in parts[1:]:
            out = out + part
        return out

    for h in range(kvh):
        ktok[1, h] = kv_ref[h, :, PB : PB + CL].T
        vtok[1, h] = kv_ref[kvh + h, :, PB : PB + CL].T
    for h in range(kvh):
        pairs = [
            block(2 * h + r, 1, kv_ref[h, :, PB : PB + CL], 1, True, None) for r in range(2)
        ]
        dkv_tail[h] = total([p[0] for p in pairs]) * (1.0 / LOG2E)
        dkv_tail[kvh + h] = total([p[1] for p in pairs])

    def slot_step(m, first):
        for h in range(kvh):
            ktok[0, h] = kv_all[m, h].T
            vtok[0, h] = kv_all[m, kvh + h].T
        for h in range(kvh):
            pairs = []
            for r in range(2):
                pairs.append(block(2 * h + r, 1, kv_all[m, h], 0, False, None))
                pairs.append(
                    block(2 * h + r, 0, kv_all[m, h], 0, first, None if first else bias_ref[m])
                )
            dkv[m, h] = (total([p[0] for p in pairs]) * (1.0 / LOG2E)).astype(BF16)
            dkv[m, kvh + h] = total([p[1] for p in pairs]).astype(BF16)

    slot_step(0, True)

    def step(m, carry):
        slot_step(m, False)
        return carry

    lax.fori_loop(1, GROUP_DEVS, step, 0)


def backward_attention(q, kv, kv_all, do, bias, lse, inner):
    heads, tokens = q.shape[0], q.shape[2]
    kvh = heads // 2
    return pl.pallas_call(
        backward_kernel,
        out_shape=(
            jax.ShapeDtypeStruct((heads, HEAD_DIM, tokens), F32),
            jax.ShapeDtypeStruct((GROUP_DEVS, 2 * kvh, HEAD_DIM, PB), BF16),
            jax.ShapeDtypeStruct((2 * kvh, HEAD_DIM, CL), F32),
        ),
        in_specs=[pl.BlockSpec(memory_space=VM)] * 4
        + [pl.BlockSpec(memory_space=pltpu.SMEM)]
        + [pl.BlockSpec(memory_space=VM)] * 2,
        out_specs=(pl.BlockSpec(memory_space=VM),) * 3,
        scratch_shapes=[VM((2, kvh, PB, HEAD_DIM), BF16), VM((2, kvh, PB, HEAD_DIM), BF16)],
        compiler_params=pltpu.CompilerParams(vmem_limit_bytes=48 << 20),
        cost_estimate=pl.CostEstimate(
            flops=60_000_000_000, bytes_accessed=12_000_000, transcendentals=19_000_000
        ),
        name="backward_attention",
    )(q, kv, kv_all, do, bias, lse, inner)


def keys_home_kernel(part, out, near, far, ns, nr, fs, fr):
    d, z = lax.axis_index("dp"), lax.axis_index("tensor")
    peer = lambda m: (jnp.bitwise_xor(d, m), z)
    greet([peer(1), peer(2), peer(4), peer(6)])
    order = (2, 4, 6, 0)
    nears = [
        remote(part.at[m + 1], near.at[m // 2], ns.at[m // 2], nr.at[m // 2], peer(1))
        for m in order
    ]
    for copy in nears:
        copy.start()
    fars = []
    for i, m in enumerate(order):
        nears[i].wait_recv()
        merged = part[m].astype(F32) + near[m // 2].astype(F32)
        if m == 0:
            out[...] = merged
        else:
            near[m // 2] = merged.astype(BF16)
            copy = remote(near.at[m // 2], far.at[m // 2], fs.at[m // 2], fr.at[m // 2], peer(m))
            copy.start()
            fars.append((copy, m))
    for copy, m in fars:
        copy.wait_recv()
        out[...] += far[m // 2].astype(F32)
    for copy in nears:
        copy.wait_send()
    for copy, _ in fars:
        copy.wait_send()


def keys_home(part):
    shape = part.shape[1:]
    return pl.pallas_call(
        keys_home_kernel,
        out_shape=jax.ShapeDtypeStruct(shape, F32),
        in_specs=[pl.BlockSpec(memory_space=VM)],
        out_specs=pl.BlockSpec(memory_space=VM),
        scratch_shapes=[VM((4,) + shape, BF16), VM((4,) + shape, BF16)]
        + [pltpu.SemaphoreType.DMA((4,))] * 4,
        compiler_params=pltpu.CompilerParams(
            collective_id=1, has_side_effects=True, vmem_limit_bytes=24 << 20
        ),
        name="keys_home",
    )(part)


def line_sum_kernel(nz, chunk, part, out, held, rs, rr, bs, br):
    d, z = lax.axis_index("dp"), lax.axis_index("tensor")
    greet([(d, lax.rem(z + 1, nz)), (d, lax.rem(z + nz - 1, nz))])
    half = part.shape[0] // 2
    count = half // chunk
    last = nz - 1

    def step(s, carry):
        for way in range(2):
            place = z if way == 0 else last - z
            onward = z + 1 if way == 0 else z - 1
            back = z - 1 if way == 0 else z + 1

            def rows(c):
                return pl.ds(pl.multiple_of(way * half + c * chunk, chunk), chunk)

            def forth(c):
                return remote(
                    held.at[rows(c)], held.at[rows(c)], rs.at[way, c], rr.at[way, c], (d, onward)
                )

            def home(c):
                return remote(
                    out.at[rows(c)], out.at[rows(c)], bs.at[way, c], br.at[way, c], (d, back)
                )

            c = s - place
            live = (c >= 0) & (c < count)

            @pl.when(live & (place == 0))
            def _():
                remote(
                    part.at[rows(c)], held.at[rows(c)], rs.at[way, c], rr.at[way, c], (d, onward)
                ).start()

            @pl.when(live & (place > 0) & (place < last))
            def _():
                forth(c).wait_recv()
                held[rows(c)] = (held[rows(c)].astype(F32) + part[rows(c)].astype(F32)).astype(BF16)
                forth(c).start()

            @pl.when(live & (place == last))
            def _():
                forth(c).wait_recv()
                out[rows(c)] = (held[rows(c)].astype(F32) + part[rows(c)].astype(F32)).astype(BF16)
                home(c).start()

            b = s - (2 * last - place)
            back_live = (b >= 0) & (b < count) & (place < last)

            @pl.when(back_live)
            def _():
                home(b).wait_recv()

            @pl.when(back_live & (place > 0))
            def _():
                home(b).start()

        return carry

    lax.fori_loop(0, count + 2 * last, step, 0)

    def drain(c, carry):
        for way in range(2):
            place = z if way == 0 else last - z
            where = pl.ds(pl.multiple_of(way * half + c * chunk, chunk), chunk)

            @pl.when(place < last)
            def _():
                remote(
                    held.at[where], held.at[where], rs.at[way, c], rr.at[way, c], (d, z)
                ).wait_send()

            @pl.when(place > 0)
            def _():
                remote(out.at[where], out.at[where], bs.at[way, c], br.at[way, c], (d, z)).wait_send()

        return carry

    lax.fori_loop(0, count, drain, 0)


def line_sum(nz, part, ident, chunk=16):
    count = part.shape[0] // 2 // chunk
    return pl.pallas_call(
        functools.partial(line_sum_kernel, nz, chunk),
        out_shape=jax.ShapeDtypeStruct(part.shape, BF16),
        in_specs=[pl.BlockSpec(memory_space=VM)],
        out_specs=pl.BlockSpec(memory_space=VM),
        scratch_shapes=[VM(part.shape, BF16)] + [pltpu.SemaphoreType.DMA((2, count))] * 4,
        compiler_params=pltpu.CompilerParams(
            collective_id=ident, has_side_effects=True, vmem_limit_bytes=24 << 20
        ),
        name="line_sum",
    )(part)


def rms_inverse(inputs):
    return lax.rsqrt(jnp.mean(inputs * inputs, axis=-1, keepdims=True) + EPSILON)


def norm_back(inputs, inverse, gain, upstream):
    inner = upstream * gain
    through = inverse * inner - inputs * inverse**3 * jnp.mean(
        inner * inputs, axis=-1, keepdims=True
    )
    return (through, jnp.sum(upstream * inputs * inverse, axis=0))


def rotate(u, cosine, sine):
    half = HEAD_DIM // 2
    lower, upper = u[:, :half], u[:, half:]
    return jnp.concatenate(
        [lower * cosine - upper * sine, upper * cosine + lower * sine], axis=1
    )


def everywhere(share, axis_size, dimension):
    summed = lax.psum_scatter(share.astype(BF16), "dp", scatter_dimension=dimension, tiled=True)
    return lax.all_gather(summed, "dp", axis=dimension, tiled=True).astype(F32)


def shards(
    nz,
    tokens,
    block_order,
    attn_gain,
    w_query,
    w_key,
    w_value,
    w_out,
    mlp_gain,
    w_gate,
    w_up,
    w_down,
    cotangent,
):
    device = lax.axis_index("dp")
    n_dp = lax.axis_size("dp")
    member = device % GROUP_DEVS
    order_row = lax.dynamic_index_in_dim(block_order, device // GROUP_DEVS, 0, keepdims=False)
    by_slot = order_row[jnp.bitwise_xor(jnp.arange(GROUP_DEVS), member)]
    own_block = by_slot[0]
    bias = jnp.where(by_slot <= own_block, 0.0, NEG).astype(F32)
    offsets = jnp.arange(PB, dtype=jnp.int32)
    places = jnp.concatenate([own_block * PB + offsets, GROUP_DEVS * PB + offsets])
    halfway = HEAD_DIM // 2
    frequency = ROTARY_BASE ** (-(jnp.arange(halfway, dtype=F32) * 2.0) / HEAD_DIM)
    angle = frequency[:, None] * places.astype(F32)[None, :]
    cosine, sine = jnp.cos(angle)[None], jnp.sin(angle)[None]

    rows = w_out.shape[0] // n_dp
    w_piece = lax.dynamic_slice_in_dim(w_out, device * rows, rows, 0)
    w_out_all = lax.all_gather(w_piece, ("tensor", "dp"), axis=0, tiled=True)

    count = tokens.shape[0]
    factor = HEAD_DIM ** (-0.5)
    inputs = tokens.astype(F32)
    inverse_one = rms_inverse(inputs)
    normed = (inputs * inverse_one * attn_gain).astype(BF16)

    def project(weight):
        out = lax.dot_general(
            weight, normed, (((0,), (1,)), ((), ())), preferred_element_type=F32
        )
        return out.reshape(-1, HEAD_DIM, count)

    queries = (rotate(project(w_query), cosine, sine) * (factor * LOG2E)).astype(BF16)
    keys = rotate(project(w_key), cosine, sine).astype(BF16)
    values = project(w_value).astype(BF16)
    kv = jnp.concatenate([keys, values], axis=0)
    heads, kvh = queries.shape[0], keys.shape[0]

    att_all, kv_all, lse = forward_attention(nz, queries, kv, bias)
    attended = lax.dynamic_index_in_dim(att_all, lax.axis_index("tensor"), 0, keepdims=False)
    attention = dot_tn(att_all.reshape(-1, count), w_out_all)
    middle = inputs + attention
    inverse_two = rms_inverse(middle)
    normed_two = (middle * inverse_two * mlp_gain).astype(BF16)
    gate_pre = dot(normed_two, w_gate)
    up_pre = dot(normed_two, w_up)
    sigmoid_gate = jax.nn.sigmoid(gate_pre)
    hidden = (gate_pre * sigmoid_gate * up_pre).astype(BF16)
    grad_hidden = dot_nt(cotangent, w_down)
    grad_gate_low = (
        grad_hidden * up_pre * sigmoid_gate * (1.0 + gate_pre * (1.0 - sigmoid_gate))
    ).astype(BF16)
    grad_up_low = (grad_hidden * gate_pre * sigmoid_gate).astype(BF16)
    partial_two = (dot_nt(grad_gate_low, w_gate) + dot_nt(grad_up_low, w_up)).astype(BF16)
    grad_normed_two = line_sum(nz, partial_two, 2).astype(F32)
    feed_out = lax.psum(dot(hidden, w_down).astype(BF16), "tensor").astype(F32)
    activations = (middle + feed_out).astype(BF16)
    grad_w_gate_up = jnp.concatenate(
        [dot_tn(normed_two, grad_gate_low), dot_tn(normed_two, grad_up_low)], axis=1
    )
    grad_w_down = dot_tn(hidden, cotangent)
    upstream = cotangent.astype(F32)
    through_two, grad_gain_two = norm_back(middle, inverse_two, mlp_gain, grad_normed_two)
    grad_middle = upstream + through_two
    grad_attention = grad_middle.astype(BF16)
    grad_w_out = dot(attended, grad_attention)
    grad_attended = dot_nt(w_out, grad_attention).astype(BF16)
    row_inner = jnp.sum(
        (grad_attended.astype(F32) * attended.astype(F32)).reshape(heads, HEAD_DIM, count),
        axis=1,
        keepdims=True,
    )
    grad_queries, grad_kv_part, grad_kv_tail = backward_attention(
        queries,
        kv,
        kv_all,
        grad_attended.reshape(heads, HEAD_DIM, count),
        bias,
        lse,
        row_inner,
    )
    grad_kv_prompt = keys_home(grad_kv_part)
    grad_kv = jnp.concatenate([grad_kv_prompt, grad_kv_tail], axis=2)
    grad_query_low = rotate(grad_queries * factor, cosine, -sine).astype(BF16).reshape(-1, count)
    grad_key_low = rotate(grad_kv[:kvh], cosine, -sine).astype(BF16).reshape(-1, count)
    grad_value_low = grad_kv[kvh:].astype(BF16).reshape(-1, count)

    def back(grad, weight):
        return lax.dot_general(grad, weight, (((0,), (1,)), ((), ())), preferred_element_type=F32)

    partial_one = (
        back(grad_query_low, w_query) + back(grad_key_low, w_key) + back(grad_value_low, w_value)
    ).astype(BF16)
    grad_normed = line_sum(nz, partial_one, 3).astype(F32)
    grads_low = jnp.concatenate([grad_query_low, grad_key_low, grad_value_low], axis=0)
    grad_w_qkv = dot_tn(normed, grads_low.T)
    through_one, grad_gain_one = norm_back(inputs, inverse_one, attn_gain, grad_normed)
    grad_tokens = (grad_middle + through_one).astype(BF16)
    gains = lax.psum(jnp.stack([grad_gain_one, grad_gain_two]), "dp")
    gate_up = everywhere(grad_w_gate_up, n_dp, 0)
    down = everywhere(grad_w_down, n_dp, 0)
    out = everywhere(grad_w_out, n_dp, 0)
    qkv = everywhere(grad_w_qkv, n_dp, 0)
    nq, nk = w_query.shape[1], w_key.shape[1]
    nf = w_gate.shape[1]
    return (
        activations,
        grad_tokens,
        gains[0],
        qkv[:, :nq],
        qkv[:, nq : nq + nk],
        qkv[:, nq + nk :],
        out,
        gains[1],
        gate_up[:, :nf],
        gate_up[:, nf:],
        down,
    )


def solution(mesh):
    in_specs = (
        P("dp", None),
        P(),
        P(),
        P(None, "tensor"),
        P(None, "tensor"),
        P(None, "tensor"),
        P("tensor", None),
        P(),
        P(None, "tensor"),
        P(None, "tensor"),
        P("tensor", None),
        P("dp", None),
    )
    out_specs = (
        P("dp", None),
        P("dp", None),
        P(),
        P(None, "tensor"),
        P(None, "tensor"),
        P(None, "tensor"),
        P("tensor", None),
        P(),
        P(None, "tensor"),
        P(None, "tensor"),
        P("tensor", None),
    )
    return jax.shard_map(
        functools.partial(shards, mesh.shape["tensor"]),
        mesh=mesh,
        in_specs=in_specs,
        out_specs=out_specs,
        check_vma=False,
    )
```

```python
import functools

import jax
import jax.numpy as jnp
from jax import lax
from jax.experimental import pallas as pl
from jax.experimental.pallas import tpu as pltpu
from jax.sharding import PartitionSpec as P

HEAD_DIM = 96
GROUP_DEVS = 8
PB = 512
CL = 512
EPSILON = 1e-05
ROTARY_BASE = 100000.0
LOG2E = 1.4426950408889634
NEG = -1e30
MESH = pl.DeviceIdType.MESH
VM = pltpu.VMEM
F32 = jnp.float32
BF16 = jnp.bfloat16
NT = (((1,), (1,)), ((), ()))


def dot(a, b):
    return jnp.dot(a, b, preferred_element_type=F32)


def dot_nt(a, b):
    return lax.dot_general(a, b, NT, preferred_element_type=F32)


def dot_tn(a, b):
    return lax.dot_general(a, b, (((0,), (0,)), ((), ())), preferred_element_type=F32)


def causal(s):
    key = lax.broadcasted_iota(jnp.int32, s.shape, 0)
    query = lax.broadcasted_iota(jnp.int32, s.shape, 1)
    return jnp.where(key <= query, s, NEG)


def greet(targets):
    barrier = pltpu.get_barrier_semaphore()
    for target in targets:
        pl.semaphore_signal(barrier, inc=1, device_id=target, device_id_type=MESH)
    pl.semaphore_wait(barrier, len(targets))


def remote(src, dst, send, recv, target):
    return pltpu.make_async_remote_copy(
        src_ref=src, dst_ref=dst, send_sem=send, recv_sem=recv, device_id=target, device_id_type=MESH
    )


def forward_kernel(
    nz, q_ref, kv_ref, bias_ref, att, kv_all, lse_ref, acc, top, total, ktok, gs, gr, zs, zr
):
    heads = q_ref.shape[0]
    kvh = heads // 2
    d, z = lax.axis_index("dp"), lax.axis_index("tensor")
    peer = lambda m: (jnp.bitwise_xor(d, m), z)
    greet(
        [peer(1), peer(2), peer(4), peer(6)]
        + [(d, lax.rem(z + 1, nz)), (d, lax.rem(z + nz - 1, nz))]
    )
    own = kv_ref.at[:, :, pl.ds(0, PB)]
    firsts = [remote(own, kv_all.at[m], gs.at[m], gr.at[m], peer(m)) for m in (1, 2, 4, 6)]
    for copy in firsts:
        copy.start()
    kv_all[0] = kv_ref[:, :, 0:PB]
    for h in range(kvh):
        ktok[8, h] = kv_ref[h, :, PB : PB + CL].T
        ktok[0, h] = kv_ref[h, :, 0:PB].T
    acc[...] = jnp.zeros_like(acc)
    top[...] = jnp.full_like(top, NEG)
    total[...] = jnp.zeros_like(total)

    def block(head, half, key, value, mask, bias):
        cols = pl.ds(half * PB, PB)
        s = dot(key, q_ref[head, :, cols])
        if mask:
            s = causal(s)
        if bias is not None:
            s = s + bias
        old = top[head, :, cols]
        new = jnp.maximum(old, jnp.max(s, axis=0, keepdims=True))
        p = jnp.exp2(s - new)
        shrink = jnp.exp2(old - new)
        total[head, :, cols] = total[head, :, cols] * shrink + jnp.sum(p, axis=0, keepdims=True)
        acc[head, :, cols] = acc[head, :, cols] * shrink + dot(value, p.astype(BF16))
        top[head, :, cols] = new

    def slot_step(slot, half, mask=False, bias=None):
        for head in range(heads):
            block(head, half, ktok[slot, head // 2], kv_all[slot, kvh + head // 2], mask, bias)

    slot_step(0, 1)
    for head in range(heads):
        block(head, 1, ktok[8, head // 2], kv_ref[kvh + head // 2, :, PB : PB + CL], True, None)

    def arrive(m):
        remote(kv_all.at[m], kv_all.at[m], gs.at[m], gr.at[m], peer(1)).wait_recv()

    def hand_on(m):
        return remote(kv_all.at[m], kv_all.at[m + 1], gs.at[m + 1], gr.at[m + 1], peer(1))

    def tail_slot(m, carry):
        arrive(m)

        @pl.when(lax.rem(m, 2) == 0)
        def _():
            hand_on(m).start()

        for h in range(kvh):
            ktok[m, h] = kv_all[m, h].T
        slot_step(m, 1)
        return carry

    tail_slot(1, 0)
    slot_step(0, 0, mask=True)
    slot_step(1, 0, bias=bias_ref[1])
    lax.fori_loop(2, GROUP_DEVS, tail_slot, 0)

    rows = heads * HEAD_DIM

    def finish(half):
        cols = pl.ds(half * PB, PB)
        for head in range(heads):
            att[z, pl.ds(head * HEAD_DIM, HEAD_DIM), cols] = (
                acc[head, :, cols] / total[head, :, cols]
            ).astype(BF16)
            lse_ref[head, :, cols] = top[head, :, cols] + jnp.log2(total[head, :, cols])

    def piece(index, half):
        return att.at[index, :, pl.ds(half * PB, PB)]

    def z_send(right, half, s):
        index, target = (z - s, z + 1) if right else (z + s, z - 1)
        there = (z - s >= 0) & (z < nz - 1) if right else (z + s < nz) & (z > 0)
        where = piece(index, half)
        return there, remote(
            where, where, zs.at[half, int(right), s], zr.at[half, int(right), s], (d, target)
        )

    def z_arrive(right, half, s):
        index = z - 1 - s if right else z + 1 + s
        there = index >= 0 if right else index < nz
        where = piece(index, half)

        @pl.when(there)
        def _():
            remote(
                where, where, zs.at[half, int(right), s], zr.at[half, int(right), s], (d, z)
            ).wait_recv()

    def z_start(half, s):
        for right in (True, False):
            if s > 0:
                z_arrive(right, half, s - 1)
            there, copy = z_send(right, half, s)
            pl.when(there)(copy.start)

    def z_finish(half):
        for right in (True, False):
            z_arrive(right, half, nz - 2)
            for s in range(nz - 1):
                there, copy = z_send(right, half, s)
                pl.when(there)(copy.wait_send)

    def prompt_slot(m, carry):
        slot_step(m, 0, bias=bias_ref[m])
        return carry

    finish(1)
    z_start(1, 0)
    lax.fori_loop(2, 6, prompt_slot, 0)
    z_start(1, 1)
    lax.fori_loop(6, GROUP_DEVS, prompt_slot, 0)
    finish(0)
    z_start(0, 0)
    for s in range(2, nz - 1):
        z_start(1, s)
    for s in range(1, nz - 1):
        z_start(0, s)
    z_finish(1)
    z_finish(0)
    for copy in firsts:
        copy.wait_send()
    for m in (2, 4, 6):
        hand_on(m).wait_send()


def forward_attention(nz, q, kv, bias):
    heads, tokens = q.shape[0], q.shape[2]
    kvh = heads // 2
    return pl.pallas_call(
        functools.partial(forward_kernel, nz),
        out_shape=(
            jax.ShapeDtypeStruct((nz, heads * HEAD_DIM, tokens), BF16),
            jax.ShapeDtypeStruct((GROUP_DEVS, 2 * kvh, HEAD_DIM, PB), BF16),
            jax.ShapeDtypeStruct((heads, 1, tokens), F32),
        ),
        in_specs=[
            pl.BlockSpec(memory_space=VM),
            pl.BlockSpec(memory_space=VM),
            pl.BlockSpec(memory_space=pltpu.SMEM),
        ],
        out_specs=(pl.BlockSpec(memory_space=VM),) * 3,
        scratch_shapes=[
            VM((heads, HEAD_DIM, tokens), F32),
            VM((heads, 1, tokens), F32),
            VM((heads, 1, tokens), F32),
            VM((GROUP_DEVS + 1, kvh, PB, HEAD_DIM), BF16),
            pltpu.SemaphoreType.DMA((GROUP_DEVS,)),
            pltpu.SemaphoreType.DMA((GROUP_DEVS,)),
            pltpu.SemaphoreType.DMA((2, 2, nz - 1)),
            pltpu.SemaphoreType.DMA((2, 2, nz - 1)),
        ],
        compiler_params=pltpu.CompilerParams(
            collective_id=0, has_side_effects=True, vmem_limit_bytes=48 << 20
        ),
        cost_estimate=pl.CostEstimate(
            flops=40_000_000_000, bytes_accessed=12_000_000, transcendentals=19_000_000
        ),
        name="forward_attention",
    )(q, kv, bias)


class Line:
    def __init__(self, nz, chunk, part, out, held, sems):
        self.d, self.z = lax.axis_index("dp"), lax.axis_index("tensor")
        self.chunk, self.part, self.out, self.held = chunk, part, out, held
        self.ss, self.rr, self.fs, self.fr = sems
        self.count = part.shape[0] // chunk
        self.root, self.last = nz // 2 - 1, nz - 1

    def rows(self, c):
        return pl.ds(pl.multiple_of(c * self.chunk, self.chunk), self.chunk)

    def toward(self, c, side, src):
        rows = self.rows(c)
        target = self.z + 1 if side == 0 else self.z - 1
        return remote(
            src.at[rows],
            (self.out if side == 0 else self.held).at[rows],
            self.ss.at[side, c],
            self.rr.at[side, c],
            (self.d, target),
        )

    def final(self, c, side):
        rows = self.rows(c)
        target = self.z - 1 if side == 0 else self.z + 1
        return remote(
            self.out.at[rows], self.out.at[rows], self.fs.at[side, c], self.fr.at[c], (self.d, target)
        )

    def mine(self, c, side):
        rows = self.rows(c)
        arrived = (self.out if side == 0 else self.held)[rows]
        return arrived.astype(F32) + self.part[rows].astype(F32)

    def issue(self, c):
        @pl.when(self.z == 0)
        def _():
            self.toward(c, 0, self.part).start()

        @pl.when(self.z == self.last)
        def _():
            self.toward(c, 1, self.part).start()

    def service(self, c):
        @pl.when((self.z > self.root) & (self.z < self.last))
        def _():
            rows = self.rows(c)
            self.toward(c, 1, self.held).wait_recv()
            self.held[rows] = self.mine(c, 1).astype(BF16)
            self.toward(c, 1, self.held).start()

    def ready(self, c):
        @pl.when(self.z != self.root)
        def _():
            self.final(c, 1).wait_recv()

        @pl.when((self.z > self.root) & (self.z < self.last))
        def _():
            self.final(c, 1).start()

        @pl.when(self.z == self.root)
        def _():
            rows = self.rows(c)
            self.toward(c, 0, self.out).wait_recv()
            self.toward(c, 1, self.held).wait_recv()
            self.out[rows] = (self.mine(c, 0) + self.held[rows].astype(F32)).astype(BF16)
            self.final(c, 0).start()
            self.final(c, 1).start()

    def drain(self):
        def body(c, carry):
            @pl.when(self.z < self.root + 1)
            def _():
                @pl.when(self.z == 0)
                def _():
                    self.toward(c, 0, self.part).wait_send()

                @pl.when(self.z == self.root)
                def _():
                    self.final(c, 0).wait_send()
                    self.final(c, 1).wait_send()

            @pl.when(self.z > self.root)
            def _():
                self.toward(c, 1, self.part).wait_send()

                @pl.when(self.z < self.last)
                def _():
                    self.final(c, 1).wait_send()

            return carry

        lax.fori_loop(0, self.count, body, 0)


def line_scratch(shape, chunk):
    count = shape[0] // chunk
    return [VM(shape, BF16)] + [pltpu.SemaphoreType.DMA((2, count))] * 3 + [
        pltpu.SemaphoreType.DMA((count,))
    ]


def neighbours(nz):
    d, z = lax.axis_index("dp"), lax.axis_index("tensor")
    return [(d, lax.rem(z + 1, nz)), (d, lax.rem(z + nz - 1, nz))]


def plane(masks):
    d, z = lax.axis_index("dp"), lax.axis_index("tensor")
    return [(jnp.bitwise_xor(d, m), z) for m in masks]


def loop(start, stop, body):
    def step(i, carry):
        body(i)
        return carry

    lax.fori_loop(start, stop, step, 0)


def fold_rows(values):
    return jnp.sum(values.reshape(values.shape[0] // 8, 8, values.shape[1]), axis=0)


class PlaneSum:
    def __init__(self, part, out, near, far, sems):
        self.d, self.z = lax.axis_index("dp"), lax.axis_index("tensor")
        member = lax.rem(self.d, GROUP_DEVS)
        self.chip, self.core = member // 2, lax.rem(member, 2)
        self.part, self.out, self.near, self.far, self.sems = part, out, near, far, sems
        self.height = part.shape[0] // GROUP_DEVS

    def rows(self, chip, core):
        return pl.ds(pl.multiple_of((chip * 2 + core) * self.height, self.height), self.height)

    def target(self, mask):
        return (jnp.bitwise_xor(self.d, mask), self.z)

    def copy(self, kind, i, src, dst, mask):
        return remote(
            src, dst, self.sems.at[2 * kind, i], self.sems.at[2 * kind + 1, i], self.target(mask)
        )

    def to_core(self, i):
        return self.copy(0, i, self.part.at[self.rows(i, 1 - self.core)], self.near.at[i], 1)

    def to_chip(self, k):
        return self.copy(1, k, self.near.at[jnp.bitwise_xor(self.chip, k)], self.far.at[k], 2 * k)

    def home(self, k):
        mine = self.out.at[self.rows(self.chip, self.core)]
        return self.copy(2, k, mine, mine, 2 * k)

    def share(self, k):
        piece = self.out.at[self.rows(jnp.bitwise_xor(self.chip, k), self.core)]
        return self.copy(3, k, piece, piece, 1)

    def start(self):
        for i in range(4):
            self.to_core(i).start()

    def between(self):
        for i in range(4):
            self.to_core(i).wait_recv()
            mine = self.part[self.rows(i, self.core)].astype(F32)
            self.near[i] = (mine + self.near[i].astype(F32)).astype(BF16)
        for k in (1, 2, 3):
            self.to_chip(k).start()

    def back(self):
        result = self.near[self.chip].astype(F32)
        for k in (1, 2, 3):
            self.to_chip(k).wait_recv()
            result = result + self.far[k].astype(F32)
        self.out[self.rows(self.chip, self.core)] = result.astype(BF16)
        for k in (1, 2, 3):
            self.home(k).start()
        self.share(0).start()

    def spread(self):
        for k in (1, 2, 3):
            self.home(k).wait_recv()
            self.share(k).start()

    def finish(self):
        for k in range(4):
            self.share(k).wait()
            self.to_core(k).wait_send()
        for k in (1, 2, 3):
            self.home(k).wait_send()
            self.to_chip(k).wait_send()


def plane_scratch(shape):
    piece = (4, shape[0] // GROUP_DEVS, shape[1])
    return [VM(piece, BF16), VM(piece, BF16), pltpu.SemaphoreType.DMA((8, 4))]


def last_kernel(
    nz, chunk, part, weights, x_ref, ga_ref, gain_ref, gain_two, gt, gains, summed,
    total, accum, box, held, ss, rr, fs, fr, bs, br, near, far, sems,
):
    d = lax.axis_index("dp")
    member = lax.rem(d, GROUP_DEVS)
    masks = range(1, GROUP_DEVS)
    greet(neighbours(nz) + plane(masks))
    line = Line(nz, chunk, part, total, held, (ss, rr, fs, fr))
    plane_sum = PlaneSum(weights, summed, near, far, sems)
    loop(0, line.count, line.issue)
    plane_sum.start()
    accum[...] = jnp.zeros_like(accum)
    gain = gain_ref[...]
    lag = 2

    def body(s):
        @pl.when(s < line.count)
        def _():
            line.service(s)

        @pl.when(s >= lag)
        def _():
            c = s - lag
            line.ready(c)
            rows = line.rows(c)
            x = x_ref[rows].astype(F32)
            inverse = lax.rsqrt(jnp.mean(x * x, axis=-1, keepdims=True) + EPSILON)
            upstream = total[rows].astype(F32)
            inner = upstream * gain
            through = inverse * inner - x * inverse**3 * jnp.mean(
                inner * x, axis=-1, keepdims=True
            )
            gt[rows] = (ga_ref[rows].astype(F32) + through).astype(BF16)
            accum[...] += fold_rows(upstream * x * inverse)

    marks = [0, line.count // 8, line.count // 2, line.count - line.count // 8, line.count + lag]
    loop(marks[0], marks[1], body)
    plane_sum.between()
    loop(marks[1], marks[2], body)
    plane_sum.back()
    loop(marks[2], marks[3], body)
    plane_sum.spread()
    loop(marks[3], marks[4], body)
    box[member, 0:1] = jnp.sum(accum[...], axis=0, keepdims=True)
    box[member, 1:2] = gain_two[...]
    copies = [
        remote(box.at[member], box.at[member], bs.at[m], br.at[m], target)
        for m, target in zip(masks, plane(masks))
    ]
    for copy in copies:
        copy.start()
    line.drain()
    plane_sum.finish()
    for copy in copies:
        copy.wait()
    result = box[0]
    for m in masks:
        result = result + box[m]
    gains[...] = result


def last_stage(nz, part, weights, x, ga, gain, gain_two, chunk=64):
    width = part.shape[1]
    return pl.pallas_call(
        functools.partial(last_kernel, nz, chunk),
        out_shape=(
            jax.ShapeDtypeStruct(part.shape, BF16),
            jax.ShapeDtypeStruct((2, width), F32),
            jax.ShapeDtypeStruct(weights.shape, BF16),
        ),
        in_specs=[pl.BlockSpec(memory_space=VM)] * 6,
        out_specs=(pl.BlockSpec(memory_space=VM),) * 3,
        scratch_shapes=[
            VM(part.shape, BF16),
            VM((8, width), F32),
            VM((GROUP_DEVS, 2, width), F32),
        ]
        + line_scratch(part.shape, chunk)
        + [pltpu.SemaphoreType.DMA((GROUP_DEVS,))] * 2
        + plane_scratch(weights.shape),
        compiler_params=pltpu.CompilerParams(
            collective_id=3, has_side_effects=True, vmem_limit_bytes=48 << 20
        ),
        cost_estimate=pl.CostEstimate(
            flops=100_000_000_000, bytes_accessed=24_000_000, transcendentals=0
        ),
        name="last_stage",
    )(part, weights, x, ga, gain, gain_two)


def backward_kernel(
    nz, chunk, q_ref, kv_ref, kv_all, do_ref, bias_ref, lse_ref, inner_ref, feed, mid_ref,
    dq, dkv_home, dkv_tail, act,
    dkv, near, far, ktok, vtok, total, held, ss, rr, fs, fr, ns, nr, ps, pr,
):
    heads = q_ref.shape[0]
    kvh = heads // 2
    greet(neighbours(nz) + plane((1, 2, 4, 6)))
    line = Line(nz, chunk, feed, total, held, (ss, rr, fs, fr))
    loop(0, line.count, line.issue)
    lag = 3

    def background(s):
        @pl.when(s < line.count)
        def _():
            line.service(s)

        @pl.when((s >= lag) & (s < line.count + lag))
        def _():
            line.ready(s - lag)
            rows = line.rows(s - lag)
            act[rows] = (mid_ref[rows].astype(F32) + total[rows].astype(F32)).astype(BF16)

    dq[...] = jnp.zeros_like(dq)

    def block(head, half, keyt, slot, mask, bias):
        h = head // 2
        cols = pl.ds(half * PB, PB)
        s = dot(ktok[slot, h], q_ref[head, :, cols])
        if mask:
            s = causal(s)
        shift = lse_ref[head, :, cols]
        if bias is not None:
            shift = shift - bias
        p = jnp.exp2(s - shift)
        dp = dot(vtok[slot, h], do_ref[head, :, cols])
        ds = (p * (dp - inner_ref[head, :, cols])).astype(BF16)
        dq[head, :, cols] += dot(keyt, ds)
        dv = dot_nt(do_ref[head, :, cols], p.astype(BF16))
        dk = dot_nt(q_ref[head, :, cols], ds)
        return dk, dv

    def total_of(parts):
        out = parts[0]
        for part in parts[1:]:
            out = out + part
        return out

    for h in range(kvh):
        ktok[1, h] = kv_ref[h, :, PB : PB + CL].T
        vtok[1, h] = kv_ref[kvh + h, :, PB : PB + CL].T
    for h in range(kvh):
        pairs = [
            block(2 * h + r, 1, kv_ref[h, :, PB : PB + CL], 1, True, None) for r in range(2)
        ]
        dkv_tail[h] = total_of([p[0] for p in pairs]) * (1.0 / LOG2E)
        dkv_tail[kvh + h] = total_of([p[1] for p in pairs])

    def slot_step(m, first, tick):
        for h in range(kvh):
            ktok[0, h] = kv_all[m, h].T
            vtok[0, h] = kv_all[m, kvh + h].T
        for h in range(kvh):
            background(tick * 2 + h)
            pairs = []
            for r in range(2):
                pairs.append(block(2 * h + r, 1, kv_all[m, h], 0, False, None))
                pairs.append(
                    block(2 * h + r, 0, kv_all[m, h], 0, first, None if first else bias_ref[m])
                )
            dkv[m, h] = (total_of([p[0] for p in pairs]) * (1.0 / LOG2E)).astype(BF16)
            dkv[m, kvh + h] = total_of([p[1] for p in pairs]).astype(BF16)

    def to_near(i):
        return remote(dkv.at[2 * i + 1], near.at[i], ns.at[i], nr.at[i], plane((1,))[0])

    def to_far(i):
        return remote(near.at[i], far.at[i], ps.at[i], pr.at[i], plane((2 * i,))[0])

    def odd(i):
        slot_step(2 * i + 1, False, i)
        to_near(i).start()

    def even(i):
        slot_step(2 * i, False, i + 3)
        to_near(i).wait_recv()
        near[i] = (dkv[2 * i].astype(F32) + near[i].astype(F32)).astype(BF16)
        to_far(i).start()

    quarter = GROUP_DEVS // 2
    loop(0, quarter, odd)
    loop(1, quarter, even)
    slot_step(0, True, GROUP_DEVS - 1)
    to_near(0).wait_recv()
    dkv_home[...] = dkv[0].astype(F32) + near[0].astype(F32)
    loop(2 * GROUP_DEVS, line.count + lag, background)
    for i in range(1, quarter):
        to_far(i).wait_recv()
        dkv_home[...] += far[i].astype(F32)
    for i in range(quarter):
        to_near(i).wait_send()
    for i in range(1, quarter):
        to_far(i).wait_send()
    line.drain()


def backward_attention(nz, q, kv, kv_all, do, bias, lse, inner, feed, middle, chunk=64):
    heads, tokens = q.shape[0], q.shape[2]
    kvh = heads // 2
    slot = (2 * kvh, HEAD_DIM, PB)
    return pl.pallas_call(
        functools.partial(backward_kernel, nz, chunk),
        out_shape=(
            jax.ShapeDtypeStruct((heads, HEAD_DIM, tokens), F32),
            jax.ShapeDtypeStruct(slot, F32),
            jax.ShapeDtypeStruct((2 * kvh, HEAD_DIM, CL), F32),
            jax.ShapeDtypeStruct(feed.shape, BF16),
        ),
        in_specs=[pl.BlockSpec(memory_space=VM)] * 4
        + [pl.BlockSpec(memory_space=pltpu.SMEM)]
        + [pl.BlockSpec(memory_space=VM)] * 4,
        out_specs=(pl.BlockSpec(memory_space=VM),) * 4,
        scratch_shapes=[
            VM((GROUP_DEVS,) + slot, BF16),
            VM((GROUP_DEVS // 2,) + slot, BF16),
            VM((GROUP_DEVS // 2,) + slot, BF16),
            VM((2, kvh, PB, HEAD_DIM), BF16),
            VM((2, kvh, PB, HEAD_DIM), BF16),
            VM(feed.shape, BF16),
        ]
        + line_scratch(feed.shape, chunk)
        + [pltpu.SemaphoreType.DMA((GROUP_DEVS // 2,))] * 4,
        compiler_params=pltpu.CompilerParams(
            collective_id=1, has_side_effects=True, vmem_limit_bytes=50 << 20
        ),
        cost_estimate=pl.CostEstimate(
            flops=200_000_000_000, bytes_accessed=24_000_000, transcendentals=19_000_000
        ),
        name="backward_attention",
    )(q, kv, kv_all, do, bias, lse, inner, feed, middle)


def middle_kernel(
    nz, chunk, att_hbm, wo_hbm, x_hbm, wg_hbm, wu_hbm, wd_hbm, cot_hbm, gain_ref,
    ga, mid, feed, gatt, inner_out, gwo, gain_two, gffn,
    att, wo, wg, wu, wd, cot, mid32, nt2, hidden, gg, gu, part, total, accum, stage, load, store,
    held, ss, rr, fs, fr,
):
    z = lax.axis_index("tensor")
    pairs = ((x_hbm, mid), (att_hbm, att), (wo_hbm, wo), (wg_hbm, wg), (wu_hbm, wu), (cot_hbm, cot), (wd_hbm, wd))
    loads = [pltpu.make_async_copy(src, dst, load.at[i]) for i, (src, dst) in enumerate(pairs)]
    for copy in loads:
        copy.start()
    greet(neighbours(nz))
    tokens, width = mid.shape
    ff = wg.shape[1]
    own = gatt.shape[0]
    heads = own // HEAD_DIM
    group = 256
    per = group // chunk
    tile = 512
    gain = gain_ref[...]
    accum[...] = jnp.zeros_like(accum)
    line = Line(nz, chunk, part, total, held, (ss, rr, fs, fr))
    mine = pl.ds(pl.multiple_of(z * own, own), own)
    lag = 3

    def settle(c):
        rows = line.rows(c)
        m = mid[rows].astype(F32)
        inverse = lax.rsqrt(jnp.mean(m * m, axis=-1, keepdims=True) + EPSILON)
        upstream = total[rows].astype(F32)
        inner = upstream * gain
        through = inverse * inner - m * inverse**3 * jnp.mean(inner * m, axis=-1, keepdims=True)
        ga[rows] = (cot[rows].astype(F32) + through).astype(BF16)
        accum[...] += fold_rows(upstream * m * inverse)

        @pl.when(lax.rem(c, per) == per - 1)
        def _():
            block = pl.ds(pl.multiple_of((c // per) * group, group), group)
            back = dot_nt(wo[mine], ga[block])
            gatt[:, block] = back.astype(BF16)
            for head in range(heads):
                some = pl.ds(head * HEAD_DIM, HEAD_DIM)
                there = att[pl.ds(pl.multiple_of(z * own + head * HEAD_DIM, 32), HEAD_DIM), block]
                inner_out[head, :, block] = jnp.sum(
                    gatt[some, block].astype(F32) * there.astype(F32), axis=0, keepdims=True
                )

    def tick(s):
        @pl.when((s >= 0) & (s < line.count))
        def _():
            line.service(s)

        @pl.when((s >= lag) & (s < line.count + lag))
        def _():
            line.ready(s - lag)
            settle(s - lag)

    for copy in loads[:3]:
        copy.wait()

    def forward(j):
        rows = pl.ds(pl.multiple_of(j * group, group), group)
        a = att[:, rows].T
        for t in range(width // tile):
            cols = pl.ds(t * tile, tile)
            mid32[:, cols] = mid[rows, cols].astype(F32) + dot(a, wo[:, cols])
        m = mid32[...]
        mid[rows] = m.astype(BF16)
        inverse = lax.rsqrt(jnp.mean(m * m, axis=-1, keepdims=True) + EPSILON)
        nt2[rows] = (m * inverse * gain).astype(BF16)

        @pl.when(j == 0)
        def _():
            for copy in loads[3:]:
                copy.wait()

        tick(2 * j - 3)
        for t in range(ff // tile):
            cols = pl.ds(t * tile, tile)
            gate = dot(nt2[rows], wg[:, cols])
            up = dot(nt2[rows], wu[:, cols])
            back = dot_nt(cot[rows], wd[cols])
            sig = jax.nn.sigmoid(gate)
            silu = gate * sig
            hidden[rows, cols] = (silu * up).astype(BF16)
            gu[rows, cols] = (back * silu).astype(BF16)
            gg[rows, cols] = (back * up * (sig * (1.0 + gate * (1.0 - sig)))).astype(BF16)
        for t in range(width // tile):
            cols = pl.ds(t * tile, tile)
            part[rows, cols] = (dot_nt(gg[rows], wg[cols]) + dot_nt(gu[rows], wu[cols])).astype(BF16)
        loop(j * per, j * per + per, line.issue)
        for t in range(width // tile):
            cols = pl.ds(t * tile, tile)
            feed[rows, cols] = dot(hidden[rows], wd[:, cols]).astype(BF16)
        tick(2 * j - 2)

    steps = tokens // group
    loop(0, steps, forward)
    done = 2 * steps - 3
    slabs = width // group

    def put(t):
        return pltpu.make_async_copy(
            stage.at[lax.rem(t, 2)],
            gffn.at[pl.ds(pl.multiple_of(t * group, group), group)],
            store.at[lax.rem(t, 2)],
        )

    def weights(t):
        @pl.when(t >= 2)
        def _():
            put(t - 2).wait()

        slot = lax.rem(t, 2)
        cols = pl.ds(pl.multiple_of(t * group, group), group)
        a = nt2[:, cols].T
        stage[slot, :, 0:ff] = dot(a, gg[...]).astype(BF16)
        stage[slot, :, ff : 2 * ff] = dot(a, gu[...]).astype(BF16)
        stage[slot, :, 2 * ff : 3 * ff] = dot(cot[:, cols].T, hidden[...]).astype(BF16)
        put(t).start()

        @pl.when(lax.rem(t, 2) == 1)
        def _():
            tick(done + t // 2)

    loop(0, slabs, weights)
    loop(done + slabs // 2, line.count + lag, tick)
    for t in range(width // tile):
        cols = pl.ds(t * tile, tile)
        gwo[:, cols] = dot(att[mine], ga[:, cols]).astype(BF16)
    gain_two[...] = jnp.sum(accum[...], axis=0, keepdims=True)
    for t in (slabs - 2, slabs - 1):
        put(t).wait()
    line.drain()


def middle_stage(nz, att_all, w_out_all, x, w_gate, w_up, w_down, cot, gain, chunk=64):
    tokens, width = x.shape
    ff = w_gate.shape[1]
    own = w_out_all.shape[0] // nz
    heads = own // HEAD_DIM
    group = 256
    wide = jax.ShapeDtypeStruct((tokens, width), BF16)
    return pl.pallas_call(
        functools.partial(middle_kernel, nz, chunk),
        out_shape=(
            wide,
            wide,
            wide,
            jax.ShapeDtypeStruct((own, tokens), BF16),
            jax.ShapeDtypeStruct((heads, 1, tokens), F32),
            jax.ShapeDtypeStruct((own, width), BF16),
            jax.ShapeDtypeStruct((1, width), F32),
            jax.ShapeDtypeStruct((width, 3 * ff), BF16),
        ),
        in_specs=[pl.BlockSpec(memory_space=pl.ANY)] * 7 + [pl.BlockSpec(memory_space=VM)],
        out_specs=(pl.BlockSpec(memory_space=VM),) * 7 + (pl.BlockSpec(memory_space=pl.ANY),),
        scratch_shapes=[
            VM(w_out_all.shape[:1] + (tokens,), BF16),
            VM(w_out_all.shape, BF16),
            VM((width, ff), BF16),
            VM((width, ff), BF16),
            VM((ff, width), BF16),
            VM((tokens, width), BF16),
            VM((group, width), F32),
            VM((tokens, width), BF16),
            VM((tokens, ff), BF16),
            VM((tokens, ff), BF16),
            VM((tokens, ff), BF16),
            VM((tokens, width), BF16),
            VM((tokens, width), BF16),
            VM((8, width), F32),
            VM((2, group, 3 * ff), BF16),
            pltpu.SemaphoreType.DMA((7,)),
            pltpu.SemaphoreType.DMA((2,)),
        ]
        + line_scratch((tokens, width), chunk),
        compiler_params=pltpu.CompilerParams(
            collective_id=2, has_side_effects=True, vmem_limit_bytes=60 << 20
        ),
        cost_estimate=pl.CostEstimate(
            flops=100_000_000_000, bytes_accessed=50_000_000, transcendentals=1_000_000
        ),
        name="middle_stage",
    )(att_all, w_out_all, x, w_gate, w_up, w_down, cot, gain)


def rms_inverse(inputs):
    return lax.rsqrt(jnp.mean(inputs * inputs, axis=-1, keepdims=True) + EPSILON)


def rotate(u, cosine, sine):
    half = HEAD_DIM // 2
    lower, upper = u[:, :half], u[:, half:]
    return jnp.concatenate(
        [lower * cosine - upper * sine, upper * cosine + lower * sine], axis=1
    )


def shards(
    nz,
    tokens,
    block_order,
    attn_gain,
    w_query,
    w_key,
    w_value,
    w_out,
    mlp_gain,
    w_gate,
    w_up,
    w_down,
    cotangent,
):
    device = lax.axis_index("dp")
    n_dp = lax.axis_size("dp")
    member = device % GROUP_DEVS
    order_row = lax.dynamic_index_in_dim(block_order, device // GROUP_DEVS, 0, keepdims=False)
    by_slot = order_row[jnp.bitwise_xor(jnp.arange(GROUP_DEVS), member)]
    own_block = by_slot[0]
    bias = jnp.where(by_slot <= own_block, 0.0, NEG).astype(F32)
    offsets = jnp.arange(PB, dtype=jnp.int32)
    places = jnp.concatenate([own_block * PB + offsets, GROUP_DEVS * PB + offsets])
    halfway = HEAD_DIM // 2
    frequency = ROTARY_BASE ** (-(jnp.arange(halfway, dtype=F32) * 2.0) / HEAD_DIM)
    angle = frequency[:, None] * places.astype(F32)[None, :]
    cosine, sine = jnp.cos(angle)[None], jnp.sin(angle)[None]

    rows = w_out.shape[0] // n_dp
    w_piece = lax.dynamic_slice_in_dim(w_out, device * rows, rows, 0)
    w_out_all = lax.all_gather(w_piece, ("tensor", "dp"), axis=0, tiled=True)

    count = tokens.shape[0]
    factor = HEAD_DIM ** (-0.5)
    inputs = tokens.astype(F32)
    inverse_one = rms_inverse(inputs)
    normed = (inputs * inverse_one * attn_gain).astype(BF16)

    def project(weight):
        out = lax.dot_general(
            weight, normed, (((0,), (1,)), ((), ())), preferred_element_type=F32
        )
        return out.reshape(-1, HEAD_DIM, count)

    queries = (rotate(project(w_query), cosine, sine) * (factor * LOG2E)).astype(BF16)
    keys = rotate(project(w_key), cosine, sine).astype(BF16)
    values = project(w_value).astype(BF16)
    kv = jnp.concatenate([keys, values], axis=0)
    heads, kvh = queries.shape[0], keys.shape[0]

    att_all, kv_all, lse = forward_attention(nz, queries, kv, bias)
    grad_attention, middle, feed_part, grad_attended, row_inner, grad_w_out, grad_gain_two, grad_ffn = (
        middle_stage(
            nz,
            att_all.reshape(-1, count),
            w_out_all,
            tokens,
            w_gate,
            w_up,
            w_down,
            cotangent,
            mlp_gain[None],
        )
    )
    grad_ffn = lax.psum_scatter(grad_ffn, "dp", scatter_dimension=0, tiled=True)
    grad_queries, grad_kv_prompt, grad_kv_tail, activations = backward_attention(
        nz,
        queries,
        kv,
        kv_all,
        grad_attended.reshape(heads, HEAD_DIM, count),
        bias,
        lse,
        row_inner,
        feed_part,
        middle,
    )
    grad_kv = jnp.concatenate([grad_kv_prompt, grad_kv_tail], axis=2)
    grad_query_low = rotate(grad_queries * factor, cosine, -sine).astype(BF16).reshape(-1, count)
    grad_key_low = rotate(grad_kv[:kvh], cosine, -sine).astype(BF16).reshape(-1, count)
    grad_value_low = grad_kv[kvh:].astype(BF16).reshape(-1, count)

    def back(grad, weight):
        return lax.dot_general(grad, weight, (((0,), (1,)), ((), ())), preferred_element_type=F32)

    partial_one = (
        back(grad_query_low, w_query) + back(grad_key_low, w_key) + back(grad_value_low, w_value)
    ).astype(BF16)
    grads_low = jnp.concatenate([grad_query_low, grad_key_low, grad_value_low], axis=0)
    grad_attn = jnp.concatenate(
        [dot(grads_low, normed).astype(BF16), grad_w_out], axis=0
    )
    partial_one, grad_ffn = lax.optimization_barrier((partial_one, grad_ffn))
    grad_ffn = lax.all_gather(grad_ffn, "dp", axis=0, tiled=True)
    grad_tokens, gains, grad_attn = last_stage(
        nz, partial_one, grad_attn, tokens, grad_attention, attn_gain[None], grad_gain_two
    )
    if n_dp > GROUP_DEVS:
        gains = lax.psum(gains, "dp") * (1.0 / GROUP_DEVS)
        grad_attn = lax.psum(grad_attn.astype(F32), "dp") * (1.0 / GROUP_DEVS)
    nq, nk, nf = w_query.shape[1], w_key.shape[1], w_gate.shape[1]

    def wide(values):
        return values.astype(F32)

    return (
        activations,
        grad_tokens,
        gains[0],
        wide(grad_attn[:nq].T),
        wide(grad_attn[nq : nq + nk].T),
        wide(grad_attn[nq + nk : nq + 2 * nk].T),
        wide(grad_attn[nq + 2 * nk :]),
        gains[1],
        wide(grad_ffn[:, :nf]),
        wide(grad_ffn[:, nf : 2 * nf]),
        wide(grad_ffn[:, 2 * nf :].T),
    )


def solution(mesh):
    in_specs = (
        P("dp", None),
        P(),
        P(),
        P(None, "tensor"),
        P(None, "tensor"),
        P(None, "tensor"),
        P("tensor", None),
        P(),
        P(None, "tensor"),
        P(None, "tensor"),
        P("tensor", None),
        P("dp", None),
    )
    out_specs = (
        P("dp", None),
        P("dp", None),
        P(),
        P(None, "tensor"),
        P(None, "tensor"),
        P(None, "tensor"),
        P("tensor", None),
        P(),
        P(None, "tensor"),
        P(None, "tensor"),
        P("tensor", None),
    )
    return jax.shard_map(
        functools.partial(shards, mesh.shape["tensor"]),
        mesh=mesh,
        in_specs=in_specs,
        out_specs=out_specs,
        check_vma=False,
    )
```

```python
import functools

import jax
import jax.numpy as jnp
from jax import lax
from jax.experimental import pallas as pl
from jax.experimental.pallas import tpu as pltpu
from jax.sharding import PartitionSpec as P

HEAD_DIM = 96
GROUP_DEVS = 8
PB = 512
CL = 512
EPSILON = 1e-05
ROTARY_BASE = 100000.0
LOG2E = 1.4426950408889634
NEG = -1e30
MESH = pl.DeviceIdType.MESH
VM = pltpu.VMEM
F32 = jnp.float32
BF16 = jnp.bfloat16
NT = (((1,), (1,)), ((), ()))


def dot(a, b):
    return jnp.dot(a, b, preferred_element_type=F32)


def dot_nt(a, b):
    return lax.dot_general(a, b, NT, preferred_element_type=F32)


def dot_tn(a, b):
    return lax.dot_general(a, b, (((0,), (0,)), ((), ())), preferred_element_type=F32)


def causal(s):
    key = lax.broadcasted_iota(jnp.int32, s.shape, 0)
    query = lax.broadcasted_iota(jnp.int32, s.shape, 1)
    return jnp.where(key <= query, s, NEG)


def greet(targets):
    barrier = pltpu.get_barrier_semaphore()
    for target in targets:
        pl.semaphore_signal(barrier, inc=1, device_id=target, device_id_type=MESH)
    pl.semaphore_wait(barrier, len(targets))


def remote(src, dst, send, recv, target):
    return pltpu.make_async_remote_copy(
        src_ref=src, dst_ref=dst, send_sem=send, recv_sem=recv, device_id=target, device_id_type=MESH
    )


class Line:
    def __init__(self, nz, chunk, part, out, held, sems):
        self.d, self.z = lax.axis_index("dp"), lax.axis_index("tensor")
        self.chunk, self.part, self.out, self.held = chunk, part, out, held
        self.ss, self.rr, self.fs, self.fr = sems
        self.count = part.shape[0] // chunk
        self.root, self.last = nz // 2 - 1, nz - 1

    def rows(self, c):
        return pl.ds(pl.multiple_of(c * self.chunk, self.chunk), self.chunk)

    def batch(self, i, n):
        return pl.ds(pl.multiple_of(i * self.chunk * n, self.chunk * n), self.chunk * n)

    def toward(self, c, side, src):
        rows = self.rows(c)
        target = self.z + 1 if side == 0 else self.z - 1
        return remote(
            src.at[rows],
            (self.out if side == 0 else self.held).at[rows],
            self.ss.at[side, c],
            self.rr.at[side, c],
            (self.d, target),
        )

    def final(self, c, side):
        rows = self.rows(c)
        target = self.z - 1 if side == 0 else self.z + 1
        return remote(
            self.out.at[rows], self.out.at[rows], self.fs.at[side, c], self.fr.at[c], (self.d, target)
        )

    def mine(self, c, side):
        rows = self.rows(c)
        arrived = (self.out if side == 0 else self.held)[rows]
        return arrived.astype(F32) + self.part[rows].astype(F32)

    def issue(self, c):
        @pl.when(self.z == 0)
        def _():
            self.toward(c, 0, self.part).start()

        @pl.when(self.z == self.last)
        def _():
            self.toward(c, 1, self.part).start()

    def service(self, c):
        @pl.when((self.z > self.root) & (self.z < self.last))
        def _():
            rows = self.rows(c)
            self.toward(c, 1, self.held).wait_recv()
            self.held[rows] = self.mine(c, 1).astype(BF16)
            self.toward(c, 1, self.held).start()

    def ready(self, c):
        @pl.when(self.z != self.root)
        def _():
            self.final(c, 1).wait_recv()

        @pl.when((self.z > self.root) & (self.z < self.last))
        def _():
            self.final(c, 1).start()

        @pl.when(self.z == self.root)
        def _():
            rows = self.rows(c)
            self.toward(c, 0, self.out).wait_recv()
            self.toward(c, 1, self.held).wait_recv()
            self.out[rows] = (self.mine(c, 0) + self.held[rows].astype(F32)).astype(BF16)
            self.final(c, 0).start()
            self.final(c, 1).start()

    def drain(self):
        def body(c, carry):
            @pl.when(self.z < self.root + 1)
            def _():
                @pl.when(self.z == 0)
                def _():
                    self.toward(c, 0, self.part).wait_send()

                @pl.when(self.z == self.root)
                def _():
                    self.final(c, 0).wait_send()
                    self.final(c, 1).wait_send()

            @pl.when(self.z > self.root)
            def _():
                self.toward(c, 1, self.part).wait_send()

                @pl.when(self.z < self.last)
                def _():
                    self.final(c, 1).wait_send()

            return carry

        lax.fori_loop(0, self.count, body, 0)


def line_scratch(shape, chunk):
    count = shape[0] // chunk
    return [VM(shape, BF16)] + [pltpu.SemaphoreType.DMA((2, count))] * 3 + [
        pltpu.SemaphoreType.DMA((count,))
    ]


def neighbours(nz):
    d, z = lax.axis_index("dp"), lax.axis_index("tensor")
    return [(d, lax.rem(z + 1, nz)), (d, lax.rem(z + nz - 1, nz))]


def plane(masks):
    d, z = lax.axis_index("dp"), lax.axis_index("tensor")
    return [(jnp.bitwise_xor(d, m), z) for m in masks]


def loop(start, stop, body):
    def step(i, carry):
        body(i)
        return carry

    lax.fori_loop(start, stop, step, 0)


def fold_rows(values):
    return jnp.sum(values.reshape(values.shape[0] // 8, 8, values.shape[1]), axis=0)


class Plane:
    def __init__(self, height, width, sems):
        self.d, self.z = lax.axis_index("dp"), lax.axis_index("tensor")
        member = lax.rem(self.d, GROUP_DEVS)
        self.core = lax.rem(member, 2)
        self.chip = member // 2
        self.bit = (lax.rem(self.chip, 2), self.chip // 2)
        self.height, self.half, self.sems = height, width // 2, sems

    def rows(self, chip, core):
        return pl.ds(pl.multiple_of((chip * 2 + core) * self.height, 16), self.height)

    def cols(self, colour):
        return pl.ds(colour * self.half, self.half)

    def at(self, first, x, y):
        return x + 2 * y if first == 0 else y + 2 * x

    def copy(self, i, src, dst, mask):
        return remote(
            src, dst, self.sems.at[0, i], self.sems.at[1, i], (jnp.bitwise_xor(self.d, mask), self.z)
        )


class PlaneReduce(Plane):
    def __init__(self, src, mine, near, far, last, sems):
        super().__init__(near.shape[1], near.shape[2], sems)
        self.src, self.mine, self.near, self.far, self.last = src, mine, near, far, last

    def to_core(self, i):
        return self.copy(i, self.src.at[self.rows(i, 1 - self.core)], self.near.at[i], 1)

    def fetch(self, i):
        rows = self.src.at[self.rows(i, self.core)]
        return pltpu.make_async_copy(rows, self.mine.at[i], self.sems.at[0, 10 + i])

    def first(self, colour, k):
        i = self.at(colour, 1 - self.bit[colour], k)
        piece = self.near.at[i, :, self.cols(colour)]
        return self.copy(4 + 2 * colour + k, piece, self.far.at[colour, k], 2 << colour)

    def second(self, colour):
        i = self.at(colour, self.bit[colour], 1 - self.bit[1 - colour])
        piece = self.near.at[i, :, self.cols(colour)]
        return self.copy(8 + colour, piece, self.last.at[colour], 4 >> colour)

    def start(self):
        for i in range(4):
            self.to_core(i).start()
            if self.mine is not None:
                self.fetch(i).start()

    def after_core(self):
        for i in range(4):
            self.to_core(i).wait_recv()
            if self.mine is not None:
                self.fetch(i).wait()
                own = self.mine[i]
            else:
                own = self.src[self.rows(i, self.core)]
            self.near[i] = (own.astype(F32) + self.near[i].astype(F32)).astype(BF16)
        for colour in range(2):
            for k in range(2):
                self.first(colour, k).start()

    def after_first(self):
        for colour in range(2):
            for k in range(2):
                self.first(colour, k).wait_recv()
                i = self.at(colour, self.bit[colour], k)
                cols = self.cols(colour)
                self.near[i, :, cols] = (
                    self.near[i, :, cols].astype(F32) + self.far[colour, k].astype(F32)
                ).astype(BF16)
        for colour in range(2):
            self.second(colour).start()

    def result(self, out):
        for colour in range(2):
            self.second(colour).wait_recv()
            cols = self.cols(colour)
            out[:, cols] = (
                self.near[self.chip, :, cols].astype(F32) + self.last[colour].astype(F32)
            ).astype(BF16)

    def finish(self):
        for i in range(4):
            self.to_core(i).wait_send()
        for colour in range(2):
            self.second(colour).wait_send()
            for k in range(2):
                self.first(colour, k).wait_send()


def reduce_scratch(height, width, fetched):
    piece = [VM((4, height, width), BF16)]
    return (
        (piece if fetched else [])
        + piece
        + [
            VM((2, 2, height, width // 2), BF16),
            VM((2, height, width // 2), BF16),
            pltpu.SemaphoreType.DMA((2, 14)),
        ]
    )


class PlaneGather(Plane):
    def __init__(self, piece, out, sems):
        super().__init__(piece.shape[0], piece.shape[1], sems)
        self.piece, self.out = piece, out

    def place(self, dx, dy, colour):
        chip = jnp.bitwise_xor(self.chip, dx + 2 * dy)
        return self.out.at[self.rows(chip, self.core), self.cols(colour)]

    def keep(self):
        own = self.out.at[self.rows(self.chip, self.core)]
        return pltpu.make_async_copy(self.piece, own, self.sems.at[0, 10])

    def first(self, colour):
        dst = self.place(0, 0, colour)
        return self.copy(colour, self.piece.at[:, self.cols(colour)], dst, 4 >> colour)

    def second(self, colour, k):
        there = self.place(0, k, colour) if colour == 0 else self.place(k, 0, colour)
        src = self.piece.at[:, self.cols(colour)] if k == 0 else there
        return self.copy(2 + 2 * colour + k, src, there, 2 << colour)

    def share(self, k):
        rows = self.out.at[self.rows(jnp.bitwise_xor(self.chip, k), self.core)]
        return self.copy(6 + k, self.piece if k == 0 else rows, rows, 1)

    def start(self):
        self.keep().start()
        for colour in range(2):
            self.first(colour).start()
            self.second(colour, 0).start()
        self.share(0).start()

    def after_first(self):
        for colour in range(2):
            self.first(colour).wait_recv()
            self.second(colour, 1).start()

    def after_second(self):
        for colour in range(2):
            for k in range(2):
                self.second(colour, k).wait_recv()
        for k in (1, 2, 3):
            self.share(k).start()

    def finish(self):
        self.keep().wait()
        for k in range(4):
            self.share(k).wait()
        for colour in range(2):
            self.first(colour).wait_send()
            for k in range(2):
                self.second(colour, k).wait_send()


def last_kernel(
    nz, chunk, part, weights, x_ref, ga_ref, gain_ref, gain_two, ffn_piece, gt, gains, summed, ffn,
    total, accum, box, attn_piece, held, ss, rr, fs, fr, bs, br, near, far, far_last, reduce_sems,
    gather_sems, ffn_sems,
):
    d = lax.axis_index("dp")
    member = lax.rem(d, GROUP_DEVS)
    masks = range(1, GROUP_DEVS)
    greet(neighbours(nz) + plane(masks))
    line = Line(nz, chunk, part, total, held, (ss, rr, fs, fr))
    reduce = PlaneReduce(weights, None, near, far, far_last, reduce_sems)
    gather = PlaneGather(attn_piece, summed, gather_sems)
    gather_ffn = PlaneGather(ffn_piece, ffn, ffn_sems)
    loop(0, line.count, line.issue)
    reduce.start()
    gather_ffn.start()
    accum[...] = jnp.zeros_like(accum)
    gain = gain_ref[...]
    lag = 10
    batch = 4

    def body(s):
        @pl.when(s < line.count)
        def _():
            line.service(s)

        @pl.when(s >= lag)
        def _():
            line.ready(s - lag)

        @pl.when((s >= lag) & (lax.rem(s - lag, batch) == batch - 1))
        def _():
            rows = line.batch((s - lag) // batch, batch)
            x = x_ref[rows].astype(F32)
            inverse = lax.rsqrt(jnp.mean(x * x, axis=-1, keepdims=True) + EPSILON)
            upstream = total[rows].astype(F32)
            inner = upstream * gain
            through = inverse * inner - x * inverse**3 * jnp.mean(
                inner * x, axis=-1, keepdims=True
            )
            gt[rows] = (ga_ref[rows].astype(F32) + through).astype(BF16)
            accum[...] += fold_rows(upstream * x * inverse)

        @pl.when(s == 5)
        def _():
            reduce.after_core()

        @pl.when(s == 24)
        def _():
            gather_ffn.after_first()

        @pl.when(s == 36)
        def _():
            reduce.after_first()

        @pl.when(s == 50)
        def _():
            reduce.result(attn_piece)
            gather.start()

        @pl.when(s == 56)
        def _():
            gather_ffn.after_second()

        @pl.when(s == 64)
        def _():
            gather.after_first()

    loop(0, line.count + lag, body)
    box[member, 0:1] = jnp.sum(accum[...], axis=0, keepdims=True)
    box[member, 1:2] = gain_two[...]
    copies = [
        remote(box.at[member], box.at[member], bs.at[m], br.at[m], target)
        for m, target in zip(masks, plane(masks))
    ]
    for copy in copies:
        copy.start()
    gather.after_second()
    line.drain()
    reduce.finish()
    gather_ffn.finish()
    gather.finish()
    for copy in copies:
        copy.wait()
    result = box[0]
    for m in masks:
        result = result + box[m]
    gains[...] = result


def last_stage(nz, part, weights, x, ga, gain, gain_two, ffn_piece, chunk=16):
    width = part.shape[1]
    height = weights.shape[0] // GROUP_DEVS
    return pl.pallas_call(
        functools.partial(last_kernel, nz, chunk),
        out_shape=(
            jax.ShapeDtypeStruct(part.shape, BF16),
            jax.ShapeDtypeStruct((2, width), F32),
            jax.ShapeDtypeStruct(weights.shape, BF16),
            jax.ShapeDtypeStruct((ffn_piece.shape[0] * GROUP_DEVS, ffn_piece.shape[1]), BF16),
        ),
        in_specs=[pl.BlockSpec(memory_space=VM)] * 7,
        out_specs=(pl.BlockSpec(memory_space=VM),) * 2 + (pl.BlockSpec(memory_space=pl.ANY),) * 2,
        scratch_shapes=[
            VM(part.shape, BF16),
            VM((8, width), F32),
            VM((GROUP_DEVS, 2, width), F32),
            VM((height, width), BF16),
        ]
        + line_scratch(part.shape, chunk)
        + [pltpu.SemaphoreType.DMA((GROUP_DEVS,))] * 2
        + reduce_scratch(height, width, False)
        + [pltpu.SemaphoreType.DMA((2, 11))] * 2,
        compiler_params=pltpu.CompilerParams(
            collective_id=3, has_side_effects=True, vmem_limit_bytes=48 << 20
        ),
        cost_estimate=pl.CostEstimate(
            flops=100_000_000_000, bytes_accessed=24_000_000, transcendentals=0
        ),
        name="last_stage",
    )(part, weights, x, ga, gain, gain_two, ffn_piece)


class LineGather:
    def __init__(self, nz, place, send, recv):
        self.d, self.z = lax.axis_index("dp"), lax.axis_index("tensor")
        self.nz, self.place, self.send, self.recv = nz, place, send, recv

    def step(self, right, s):
        index, target = (self.z - s, self.z + 1) if right else (self.z + s, self.z - 1)
        there = (index >= 0) & (index < self.nz) & (target >= 0) & (target < self.nz)
        where = self.place(index)
        way = int(right)
        return there, remote(where, where, self.send.at[way, s], self.recv.at[way, s], (self.d, target))

    def arrive(self, right, s):
        index = self.z - 1 - s if right else self.z + 1 + s
        where = self.place(index)
        way = int(right)

        @pl.when((index >= 0) & (index < self.nz))
        def _():
            remote(
                where, where, self.send.at[way, s], self.recv.at[way, s], (self.d, self.z)
            ).wait_recv()

    def start(self, s):
        for right in (True, False):
            if s > 0:
                self.arrive(right, s - 1)
            there, copy = self.step(right, s)
            pl.when(there)(copy.start)

    def last(self):
        for right in (True, False):
            self.arrive(right, self.nz - 2)

    def drain(self):
        for right in (True, False):
            for s in range(self.nz - 1):
                there, copy = self.step(right, s)
                pl.when(there)(copy.wait_send)


def forward_kernel(
    nz, q_ref, kv_ref, wo_ref, bias_ref, att, kv_all, lse_ref, wo_all, acc, top, total, ktok, mine,
    gs, gr, zs, zr, ws, wr, wp, load,
):
    heads = q_ref.shape[0]
    kvh = heads // 2
    d, z = lax.axis_index("dp"), lax.axis_index("tensor")
    some = mine.shape[0] // nz
    member = lax.rem(d, GROUP_DEVS)

    def own_place(index):
        return mine.at[pl.ds(pl.multiple_of(index * some, 16), some)]

    first_rows = pltpu.make_async_copy(
        wo_ref.at[pl.ds(pl.multiple_of(member * some, 16), some)], own_place(z), load.at[0]
    )
    first_rows.start()
    greet(plane((1, 2, 4, 6)) + neighbours(nz))
    own = kv_ref.at[:, :, pl.ds(0, PB)]
    firsts = [
        remote(own, kv_all.at[m], gs.at[m], gr.at[m], target)
        for m, target in zip((1, 2, 4, 6), plane((1, 2, 4, 6)))
    ]
    for copy in firsts:
        copy.start()
    w_line = LineGather(nz, own_place, ws, wr)
    w_plane = PlaneGather(mine, wo_all, wp)
    first_rows.wait()
    w_line.start(0)
    kv_all[0] = kv_ref[:, :, 0:PB]
    for h in range(kvh):
        ktok[8, h] = kv_ref[h, :, PB : PB + CL].T
        ktok[0, h] = kv_ref[h, :, 0:PB].T
    acc[...] = jnp.zeros_like(acc)
    top[...] = jnp.full_like(top, NEG)
    total[...] = jnp.zeros_like(total)

    def block(head, half, key, value, mask, bias):
        cols = pl.ds(half * PB, PB)
        s = dot(key, q_ref[head, :, cols])
        if mask:
            s = causal(s)
        old = top[head, :, cols]
        high = jnp.max(s, axis=0, keepdims=True)
        new = jnp.maximum(old, high if bias is None else high + bias)
        p = jnp.exp2(s - (new if bias is None else new - bias))
        shrink = jnp.exp2(old - new)
        total[head, :, cols] = total[head, :, cols] * shrink + jnp.sum(p, axis=0, keepdims=True)
        acc[head, :, cols] = acc[head, :, cols] * shrink + dot(value, p.astype(BF16))
        top[head, :, cols] = new

    def slot_step(slot, half, mask=False, bias=None):
        for head in range(heads):
            block(head, half, ktok[slot, head // 2], kv_all[slot, kvh + head // 2], mask, bias)

    for head in range(heads):
        block(head, 1, ktok[8, head // 2], kv_ref[kvh + head // 2, :, PB : PB + CL], True, None)

    def arrive(m):
        remote(kv_all.at[m], kv_all.at[m], gs.at[m], gr.at[m], (d, z)).wait_recv()

    def hand_on(m):
        return remote(kv_all.at[m], kv_all.at[m + 1], gs.at[m + 1], gr.at[m + 1], plane((1,))[0])

    def tail_slot(m):
        @pl.when(m > 0)
        def _():
            arrive(m)
            for h in range(kvh):
                ktok[m, h] = kv_all[m, h].T

        @pl.when((m > 0) & (lax.rem(m, 2) == 0))
        def _():
            hand_on(m).start()

        for s in range(1, nz - 1):

            @pl.when(m == 2 * s)
            def _():
                w_line.start(s)

        @pl.when(m == GROUP_DEVS - 1)
        def _():
            w_line.last()
            w_plane.start()

        slot_step(m, 1)

    loop(0, GROUP_DEVS, tail_slot)

    def finish(half):
        cols = pl.ds(half * PB, PB)
        for head in range(heads):
            att[z, pl.ds(head * HEAD_DIM, HEAD_DIM), cols] = (
                acc[head, :, cols] / total[head, :, cols]
            ).astype(BF16)
            lse_ref[head, :, cols] = top[head, :, cols] + jnp.log2(total[head, :, cols])

    lines = [
        LineGather(
            nz,
            lambda index, half=half: att.at[index, :, pl.ds(half * PB, PB)],
            zs.at[half],
            zr.at[half],
        )
        for half in range(2)
    ]
    finish(1)
    lines[1].start(0)
    slot_step(0, 0, mask=True)

    def prompt_slot(m):
        slot_step(m, 0, bias=bias_ref[m])

        @pl.when(m == 4)
        def _():
            w_plane.after_first()
            lines[1].start(1)

    loop(1, GROUP_DEVS, prompt_slot)
    finish(0)
    lines[0].start(0)
    w_plane.after_second()
    for s in range(2, nz - 1):
        lines[1].start(s)
    for s in range(1, nz - 1):
        lines[0].start(s)
    for line in lines:
        line.last()
    for line in lines + [w_line]:
        line.drain()
    w_plane.finish()
    for copy in firsts:
        copy.wait_send()
    for m in (2, 4, 6):
        hand_on(m).wait_send()


def forward_attention(nz, q, kv, w_out, bias):
    heads, tokens = q.shape[0], q.shape[2]
    kvh = heads // 2
    own, width = w_out.shape
    return pl.pallas_call(
        functools.partial(forward_kernel, nz),
        out_shape=(
            jax.ShapeDtypeStruct((nz, heads * HEAD_DIM, tokens), BF16),
            jax.ShapeDtypeStruct((GROUP_DEVS, 2 * kvh, HEAD_DIM, PB), BF16),
            jax.ShapeDtypeStruct((heads, 1, tokens), F32),
            jax.ShapeDtypeStruct((nz * own, width), BF16),
        ),
        in_specs=[
            pl.BlockSpec(memory_space=VM),
            pl.BlockSpec(memory_space=VM),
            pl.BlockSpec(memory_space=pl.ANY),
            pl.BlockSpec(memory_space=pltpu.SMEM),
        ],
        out_specs=(pl.BlockSpec(memory_space=VM),) * 3 + (pl.BlockSpec(memory_space=pl.ANY),),
        scratch_shapes=[
            VM((heads, HEAD_DIM, tokens), F32),
            VM((heads, 1, tokens), F32),
            VM((heads, 1, tokens), F32),
            VM((GROUP_DEVS + 1, kvh, PB, HEAD_DIM), BF16),
            VM((nz * own // GROUP_DEVS, width), BF16),
            pltpu.SemaphoreType.DMA((GROUP_DEVS,)),
            pltpu.SemaphoreType.DMA((GROUP_DEVS,)),
            pltpu.SemaphoreType.DMA((2, 2, nz - 1)),
            pltpu.SemaphoreType.DMA((2, 2, nz - 1)),
            pltpu.SemaphoreType.DMA((2, nz - 1)),
            pltpu.SemaphoreType.DMA((2, nz - 1)),
            pltpu.SemaphoreType.DMA((2, 11)),
            pltpu.SemaphoreType.DMA((1,)),
        ],
        compiler_params=pltpu.CompilerParams(
            collective_id=0, has_side_effects=True, vmem_limit_bytes=48 << 20
        ),
        cost_estimate=pl.CostEstimate(
            flops=40_000_000_000, bytes_accessed=12_000_000, transcendentals=19_000_000
        ),
        name="forward_attention",
    )(q, kv, w_out, bias)


def backward_kernel(
    nz, chunk, q_ref, kv_ref, kv_all, do_ref, bias_ref, lse_ref, inner_ref, feed, mid_ref, ffn,
    dq, dkv_home, dkv_tail, act, ffn_piece,
    dkv, near, far, ktok, vtok, total, held, ss, rr, fs, fr, ns, nr, ps, pr,
    f_mine, f_near, f_far, f_last, f_sems,
):
    heads = q_ref.shape[0]
    kvh = heads // 2
    greet(neighbours(nz) + plane((1, 2, 4, 6)))
    line = Line(nz, chunk, feed, total, held, (ss, rr, fs, fr))
    reduce = PlaneReduce(ffn, f_mine, f_near, f_far, f_last, f_sems)
    loop(0, line.count, line.issue)
    reduce.start()
    lag = 12
    ply = 4

    def ripple(s):
        @pl.when(s < line.count)
        def _():
            line.service(s)

        @pl.when(s >= lag)
        def _():
            line.ready(s - lag)

        @pl.when((s >= lag) & (lax.rem(s - lag, ply) == ply - 1))
        def _():
            rows = line.batch((s - lag) // ply, ply)
            act[rows] = (mid_ref[rows].astype(F32) + total[rows].astype(F32)).astype(BF16)

    def background(s):
        @pl.when(s == 3)
        def _():
            reduce.after_core()

        @pl.when(s == 12)
        def _():
            reduce.after_first()

        loop(s * ply, s * ply + ply, ripple)

    dq[...] = jnp.zeros_like(dq)

    def block(head, half, keyt, slot, mask, bias):
        h = head // 2
        cols = pl.ds(half * PB, PB)
        s = dot(ktok[slot, h], q_ref[head, :, cols])
        if mask:
            s = causal(s)
        shift = lse_ref[head, :, cols]
        if bias is not None:
            shift = shift - bias
        p = jnp.exp2(s - shift)
        dp = dot(vtok[slot, h], do_ref[head, :, cols])
        ds = (p * (dp - inner_ref[head, :, cols])).astype(BF16)
        dq[head, :, cols] += dot(keyt, ds)
        dv = dot_nt(do_ref[head, :, cols], p.astype(BF16))
        dk = dot_nt(q_ref[head, :, cols], ds)
        return dk, dv

    def total_of(parts):
        out = parts[0]
        for part in parts[1:]:
            out = out + part
        return out

    for h in range(kvh):
        ktok[1, h] = kv_ref[h, :, PB : PB + CL].T
        vtok[1, h] = kv_ref[kvh + h, :, PB : PB + CL].T
    for h in range(kvh):
        pairs = [
            block(2 * h + r, 1, kv_ref[h, :, PB : PB + CL], 1, True, None) for r in range(2)
        ]
        dkv_tail[h] = total_of([p[0] for p in pairs]) * (1.0 / LOG2E)
        dkv_tail[kvh + h] = total_of([p[1] for p in pairs])

    def slot_step(m, first, tick):
        for h in range(kvh):
            ktok[0, h] = kv_all[m, h].T
            vtok[0, h] = kv_all[m, kvh + h].T
        for h in range(kvh):
            background(tick * 2 + h)
            pairs = []
            for r in range(2):
                pairs.append(block(2 * h + r, 1, kv_all[m, h], 0, False, None))
                pairs.append(
                    block(2 * h + r, 0, kv_all[m, h], 0, first, None if first else bias_ref[m])
                )
            dkv[m, h] = (total_of([p[0] for p in pairs]) * (1.0 / LOG2E)).astype(BF16)
            dkv[m, kvh + h] = total_of([p[1] for p in pairs]).astype(BF16)

    def to_near(i):
        return remote(dkv.at[2 * i + 1], near.at[i], ns.at[i], nr.at[i], plane((1,))[0])

    def to_far(i):
        return remote(near.at[i], far.at[i], ps.at[i], pr.at[i], plane((2 * i,))[0])

    def odd(i):
        slot_step(2 * i + 1, False, i)
        to_near(i).start()

    def even(i):
        slot_step(2 * i, False, i + 3)
        to_near(i).wait_recv()
        near[i] = (dkv[2 * i].astype(F32) + near[i].astype(F32)).astype(BF16)
        to_far(i).start()

    quarter = GROUP_DEVS // 2
    loop(0, quarter, odd)
    loop(1, quarter, even)
    slot_step(0, True, GROUP_DEVS - 1)
    to_near(0).wait_recv()
    dkv_home[...] = dkv[0].astype(F32) + near[0].astype(F32)
    loop(2 * GROUP_DEVS * ply, line.count + lag, ripple)
    reduce.result(ffn_piece)
    for i in range(1, quarter):
        to_far(i).wait_recv()
        dkv_home[...] += far[i].astype(F32)
    reduce.finish()
    for i in range(quarter):
        to_near(i).wait_send()
    for i in range(1, quarter):
        to_far(i).wait_send()
    line.drain()


def backward_attention(
    nz, q, kv, kv_all, do, bias, lse, inner, feed, middle, ffn, chunk=16
):
    heads, tokens = q.shape[0], q.shape[2]
    kvh = heads // 2
    slot = (2 * kvh, HEAD_DIM, PB)
    return pl.pallas_call(
        functools.partial(backward_kernel, nz, chunk),
        out_shape=(
            jax.ShapeDtypeStruct((heads, HEAD_DIM, tokens), F32),
            jax.ShapeDtypeStruct(slot, F32),
            jax.ShapeDtypeStruct((2 * kvh, HEAD_DIM, CL), F32),
            jax.ShapeDtypeStruct(feed.shape, BF16),
            jax.ShapeDtypeStruct((ffn.shape[0] // GROUP_DEVS, ffn.shape[1]), BF16),
        ),
        in_specs=[pl.BlockSpec(memory_space=VM)] * 4
        + [pl.BlockSpec(memory_space=pltpu.SMEM)]
        + [pl.BlockSpec(memory_space=VM)] * 4
        + [pl.BlockSpec(memory_space=pl.ANY)],
        out_specs=(pl.BlockSpec(memory_space=VM),) * 5,
        scratch_shapes=[
            VM((GROUP_DEVS,) + slot, BF16),
            VM((GROUP_DEVS // 2,) + slot, BF16),
            VM((GROUP_DEVS // 2,) + slot, BF16),
            VM((2, kvh, PB, HEAD_DIM), BF16),
            VM((2, kvh, PB, HEAD_DIM), BF16),
            VM(feed.shape, BF16),
        ]
        + line_scratch(feed.shape, chunk)
        + [pltpu.SemaphoreType.DMA((GROUP_DEVS // 2,))] * 4
        + reduce_scratch(ffn.shape[0] // GROUP_DEVS, ffn.shape[1], True),
        compiler_params=pltpu.CompilerParams(
            collective_id=1, has_side_effects=True, vmem_limit_bytes=56 << 20
        ),
        cost_estimate=pl.CostEstimate(
            flops=200_000_000_000, bytes_accessed=24_000_000, transcendentals=19_000_000
        ),
        name="backward_attention",
    )(q, kv, kv_all, do, bias, lse, inner, feed, middle, ffn)


def middle_kernel(
    nz, chunk, att_hbm, wo_hbm, x_hbm, wg_hbm, wu_hbm, wd_hbm, cot_hbm, gain_ref,
    ga, mid, feed, gatt, inner_out, gwo, gain_two, gffn,
    att, wo, wg, wu, wd, cot, mid32, nt2, hidden, gg, gu, part, total, accum, stage, load, store,
    held, ss, rr, fs, fr,
):
    z = lax.axis_index("tensor")
    pairs = ((x_hbm, mid), (att_hbm, att), (wg_hbm, wg), (wu_hbm, wu), (cot_hbm, cot), (wd_hbm, wd))
    loads = [pltpu.make_async_copy(src, dst, load.at[i]) for i, (src, dst) in enumerate(pairs)]
    own = gatt.shape[0]
    some = own // GROUP_DEVS

    def wo_rows(i):
        src = pl.ds(pl.multiple_of(i * some, 16), some)
        dst = pl.ds(pl.multiple_of(lax.rem(i, nz) * own + i // nz * some, 16), some)
        pltpu.make_async_copy(wo_hbm.at[src], wo.at[dst], load.at[len(pairs)]).start()

    for copy in loads[:2]:
        copy.start()
    loop(0, nz * GROUP_DEVS, wo_rows)
    for copy in loads[2:]:
        copy.start()
    greet(neighbours(nz))
    tokens, width = mid.shape
    ff = wg.shape[1]
    heads = own // HEAD_DIM
    group = 256
    per = group // chunk
    ply = 4
    quarters = per // ply
    tile = 512
    gain = gain_ref[...]
    accum[...] = jnp.zeros_like(accum)
    line = Line(nz, chunk, part, total, held, (ss, rr, fs, fr))
    mine = pl.ds(pl.multiple_of(z * own, own), own)
    lag = 12

    def settle(c):
        rows = line.batch(c, ply)
        m = mid[rows].astype(F32)
        inverse = lax.rsqrt(jnp.mean(m * m, axis=-1, keepdims=True) + EPSILON)
        upstream = total[rows].astype(F32)
        inner = upstream * gain
        through = inverse * inner - m * inverse**3 * jnp.mean(inner * m, axis=-1, keepdims=True)
        ga[rows] = (cot[rows].astype(F32) + through).astype(BF16)
        accum[...] += fold_rows(upstream * m * inverse)

        @pl.when(lax.rem(c, quarters) == quarters - 1)
        def _():
            block = pl.ds(pl.multiple_of((c // quarters) * group, group), group)
            back = dot_nt(wo[mine], ga[block])
            gatt[:, block] = back.astype(BF16)
            for head in range(heads):
                some = pl.ds(head * HEAD_DIM, HEAD_DIM)
                there = att[pl.ds(pl.multiple_of(z * own + head * HEAD_DIM, 32), HEAD_DIM), block]
                inner_out[head, :, block] = jnp.sum(
                    gatt[some, block].astype(F32) * there.astype(F32), axis=0, keepdims=True
                )

    def ripple(s):
        @pl.when(s < line.count)
        def _():
            line.service(s)

        @pl.when(s >= lag)
        def _():
            line.ready(s - lag)

        @pl.when((s >= lag) & (lax.rem(s - lag, ply) == ply - 1))
        def _():
            settle((s - lag) // ply)

    def tick(s):
        @pl.when(s >= 0)
        def _():
            loop(s * ply, s * ply + ply, ripple)

    for copy in loads[:2]:
        copy.wait()
    pltpu.make_async_copy(wo_hbm, wo, load.at[len(pairs)]).wait()

    def forward(j):
        rows = pl.ds(pl.multiple_of(j * group, group), group)
        a = att[:, rows].T
        for t in range(width // tile):
            cols = pl.ds(t * tile, tile)
            mid32[:, cols] = mid[rows, cols].astype(F32) + dot(a, wo[:, cols])
        m = mid32[...]
        mid[rows] = m.astype(BF16)
        inverse = lax.rsqrt(jnp.mean(m * m, axis=-1, keepdims=True) + EPSILON)
        nt2[rows] = (m * inverse * gain).astype(BF16)

        @pl.when(j == 0)
        def _():
            for copy in loads[2:]:
                copy.wait()

        tick(2 * j - 3)
        for t in range(ff // tile):
            cols = pl.ds(t * tile, tile)
            gate = dot(nt2[rows], wg[:, cols])
            up = dot(nt2[rows], wu[:, cols])
            back = dot_nt(cot[rows], wd[cols])
            sig = jax.nn.sigmoid(gate)
            silu = gate * sig
            hidden[rows, cols] = (silu * up).astype(BF16)
            gu[rows, cols] = (back * silu).astype(BF16)
            gg[rows, cols] = (back * up * (sig * (1.0 + gate * (1.0 - sig)))).astype(BF16)
        for t in range(width // tile):
            cols = pl.ds(t * tile, tile)
            part[rows, cols] = (dot_nt(gg[rows], wg[cols]) + dot_nt(gu[rows], wu[cols])).astype(BF16)
        loop(j * per, j * per + per, line.issue)
        for t in range(width // tile):
            cols = pl.ds(t * tile, tile)
            feed[rows, cols] = dot(hidden[rows], wd[:, cols]).astype(BF16)
        tick(2 * j - 2)

    steps = tokens // group
    loop(0, steps, forward)
    done = 2 * steps - 3
    slabs = width // group

    def put(t):
        return pltpu.make_async_copy(
            stage.at[lax.rem(t, 2)],
            gffn.at[pl.ds(pl.multiple_of(t * group, group), group)],
            store.at[lax.rem(t, 2)],
        )

    def weights(t):
        @pl.when(t >= 2)
        def _():
            put(t - 2).wait()

        slot = lax.rem(t, 2)
        cols = pl.ds(pl.multiple_of(t * group, group), group)
        a = nt2[:, cols].T
        stage[slot, :, 0:ff] = dot(a, gg[...]).astype(BF16)
        stage[slot, :, ff : 2 * ff] = dot(a, gu[...]).astype(BF16)
        stage[slot, :, 2 * ff : 3 * ff] = dot(cot[:, cols].T, hidden[...]).astype(BF16)
        put(t).start()

        @pl.when(lax.rem(t, 2) == 1)
        def _():
            tick(done + t // 2)

    loop(0, slabs, weights)
    loop((done + slabs // 2) * ply, line.count + lag, ripple)
    for t in range(width // tile):
        cols = pl.ds(t * tile, tile)
        gwo[:, cols] = dot(att[mine], ga[:, cols]).astype(BF16)
    gain_two[...] = jnp.sum(accum[...], axis=0, keepdims=True)
    for t in (slabs - 2, slabs - 1):
        put(t).wait()
    line.drain()


def middle_stage(nz, att_all, w_out_all, x, w_gate, w_up, w_down, cot, gain, chunk=16):
    tokens, width = x.shape
    ff = w_gate.shape[1]
    own = w_out_all.shape[0] // nz
    heads = own // HEAD_DIM
    group = 256
    wide = jax.ShapeDtypeStruct((tokens, width), BF16)
    return pl.pallas_call(
        functools.partial(middle_kernel, nz, chunk),
        out_shape=(
            wide,
            wide,
            wide,
            jax.ShapeDtypeStruct((own, tokens), BF16),
            jax.ShapeDtypeStruct((heads, 1, tokens), F32),
            jax.ShapeDtypeStruct((own, width), BF16),
            jax.ShapeDtypeStruct((1, width), F32),
            jax.ShapeDtypeStruct((width, 3 * ff), BF16),
        ),
        in_specs=[pl.BlockSpec(memory_space=pl.ANY)] * 7 + [pl.BlockSpec(memory_space=VM)],
        out_specs=(pl.BlockSpec(memory_space=VM),) * 7 + (pl.BlockSpec(memory_space=pl.ANY),),
        scratch_shapes=[
            VM(w_out_all.shape[:1] + (tokens,), BF16),
            VM(w_out_all.shape, BF16),
            VM((width, ff), BF16),
            VM((width, ff), BF16),
            VM((ff, width), BF16),
            VM((tokens, width), BF16),
            VM((group, width), F32),
            VM((tokens, width), BF16),
            VM((tokens, ff), BF16),
            VM((tokens, ff), BF16),
            VM((tokens, ff), BF16),
            VM((tokens, width), BF16),
            VM((tokens, width), BF16),
            VM((8, width), F32),
            VM((2, group, 3 * ff), BF16),
            pltpu.SemaphoreType.DMA((7,)),
            pltpu.SemaphoreType.DMA((2,)),
        ]
        + line_scratch((tokens, width), chunk),
        compiler_params=pltpu.CompilerParams(
            collective_id=2, has_side_effects=True, vmem_limit_bytes=60 << 20
        ),
        cost_estimate=pl.CostEstimate(
            flops=100_000_000_000, bytes_accessed=50_000_000, transcendentals=1_000_000
        ),
        name="middle_stage",
    )(att_all, w_out_all, x, w_gate, w_up, w_down, cot, gain)


def finish_kernel(nq, nk, ffn, attn, gt, act, gate, up, down, q, k, v, o, gt_out, act_out):
    ff = gate.shape[1]
    gate[...] = ffn[:, 0:ff].astype(F32)
    up[...] = ffn[:, ff : 2 * ff].astype(F32)
    down[...] = ffn[:, 2 * ff : 3 * ff].astype(F32).T
    q[...] = attn[0:nq].astype(F32).T
    k[...] = attn[nq : nq + nk].astype(F32)
    v[...] = attn[nq + nk : nq + 2 * nk].astype(F32)
    o[...] = attn[nq + 2 * nk :].astype(F32)
    gt_out[...] = gt[...]
    act_out[...] = act[...]


def finish(ffn, attn, gt, act, nq, nk):
    width, ff = ffn.shape[0], ffn.shape[1] // 3
    tokens, own = gt.shape[0], attn.shape[0] - nq - 2 * nk
    tile = 256
    wide = lambda *shape: jax.ShapeDtypeStruct(shape, F32)
    down = lambda rows: pl.BlockSpec((tile, rows), lambda i: (i, 0))
    side = lambda rows: pl.BlockSpec((rows, tile), lambda i: (0, i))
    return pl.pallas_call(
        functools.partial(finish_kernel, nq, nk),
        grid=(width // tile,),
        out_shape=(
            wide(width, ff),
            wide(width, ff),
            wide(ff, width),
            wide(width, nq),
            wide(nk, width),
            wide(nk, width),
            wide(own, width),
            jax.ShapeDtypeStruct(gt.shape, gt.dtype),
            jax.ShapeDtypeStruct(act.shape, act.dtype),
        ),
        in_specs=[down(3 * ff), side(attn.shape[0]), side(tokens), side(tokens)],
        out_specs=(
            down(ff),
            down(ff),
            side(ff),
            down(nq),
            side(nk),
            side(nk),
            side(own),
            side(tokens),
            side(tokens),
        ),
        compiler_params=pltpu.CompilerParams(vmem_limit_bytes=40 << 20),
        name="finish",
    )(ffn, attn, gt, act)


def rms_inverse(inputs):
    return lax.rsqrt(jnp.mean(inputs * inputs, axis=-1, keepdims=True) + EPSILON)


def rotate(u, cosine, sine):
    half = HEAD_DIM // 2
    lower, upper = u[:, :half], u[:, half:]
    return jnp.concatenate(
        [lower * cosine - upper * sine, upper * cosine + lower * sine], axis=1
    )


def shards(
    nz,
    tokens,
    block_order,
    attn_gain,
    w_query,
    w_key,
    w_value,
    w_out,
    mlp_gain,
    w_gate,
    w_up,
    w_down,
    cotangent,
):
    device = lax.axis_index("dp")
    n_dp = lax.axis_size("dp")
    member = device % GROUP_DEVS
    order_row = lax.dynamic_index_in_dim(block_order, device // GROUP_DEVS, 0, keepdims=False)
    by_slot = order_row[jnp.bitwise_xor(jnp.arange(GROUP_DEVS), member)]
    own_block = by_slot[0]
    bias = jnp.where(by_slot <= own_block, 0.0, NEG).astype(F32)
    offsets = jnp.arange(PB, dtype=jnp.int32)
    places = jnp.concatenate([own_block * PB + offsets, GROUP_DEVS * PB + offsets])
    halfway = HEAD_DIM // 2
    frequency = ROTARY_BASE ** (-(jnp.arange(halfway, dtype=F32) * 2.0) / HEAD_DIM)
    angle = frequency[:, None] * places.astype(F32)[None, :]
    cosine, sine = jnp.cos(angle)[None], jnp.sin(angle)[None]

    count = tokens.shape[0]
    factor = HEAD_DIM ** (-0.5)
    inputs = tokens.astype(F32)
    inverse_one = rms_inverse(inputs)
    normed = (inputs * inverse_one * attn_gain).astype(BF16)

    def project(weight):
        out = lax.dot_general(
            weight, normed, (((0,), (1,)), ((), ())), preferred_element_type=F32
        )
        return out.reshape(-1, HEAD_DIM, count)

    queries = (rotate(project(w_query), cosine, sine) * (factor * LOG2E)).astype(BF16)
    keys = rotate(project(w_key), cosine, sine).astype(BF16)
    values = project(w_value).astype(BF16)
    kv = jnp.concatenate([keys, values], axis=0)
    heads, kvh = queries.shape[0], keys.shape[0]

    att_all, kv_all, lse, w_out_all = forward_attention(nz, queries, kv, w_out, bias)
    grad_attention, middle, feed_part, grad_attended, row_inner, grad_w_out, grad_gain_two, grad_ffn = (
        middle_stage(
            nz,
            att_all.reshape(-1, count),
            w_out_all,
            tokens,
            w_gate,
            w_up,
            w_down,
            cotangent,
            mlp_gain[None],
        )
    )
    grad_queries, grad_kv_prompt, grad_kv_tail, activations, ffn_piece = backward_attention(
        nz,
        queries,
        kv,
        kv_all,
        grad_attended.reshape(heads, HEAD_DIM, count),
        bias,
        lse,
        row_inner,
        feed_part,
        middle,
        grad_ffn,
    )
    grad_kv = jnp.concatenate([grad_kv_prompt, grad_kv_tail], axis=2)
    grad_query_low = rotate(grad_queries * factor, cosine, -sine).astype(BF16).reshape(-1, count)
    grad_key_low = rotate(grad_kv[:kvh], cosine, -sine).astype(BF16).reshape(-1, count)
    grad_value_low = grad_kv[kvh:].astype(BF16).reshape(-1, count)

    def back(grad, weight):
        return lax.dot_general(grad, weight, (((0,), (1,)), ((), ())), preferred_element_type=F32)

    partial_one = (
        back(grad_query_low, w_query) + back(grad_key_low, w_key) + back(grad_value_low, w_value)
    ).astype(BF16)
    grads_low = jnp.concatenate([grad_query_low, grad_key_low, grad_value_low], axis=0)
    grad_attn = jnp.concatenate(
        [dot(grads_low, normed).astype(BF16), grad_w_out], axis=0
    )
    grad_tokens, gains, grad_attn, grad_ffn = last_stage(
        nz,
        partial_one,
        grad_attn,
        tokens,
        grad_attention,
        attn_gain[None],
        grad_gain_two,
        ffn_piece,
    )
    if n_dp > GROUP_DEVS:
        gains = lax.psum(gains, "dp") * (1.0 / GROUP_DEVS)
        grad_attn = lax.psum(grad_attn.astype(F32), "dp") * (1.0 / GROUP_DEVS)
        grad_ffn = lax.psum(grad_ffn.astype(F32), "dp") * (1.0 / GROUP_DEVS)
    nq, nk = w_query.shape[1], w_key.shape[1]

    gate, up, down, query, key, value, out, grad_tokens, activations = finish(
        grad_ffn, grad_attn, grad_tokens, activations, nq, nk
    )
    return (
        activations,
        grad_tokens,
        gains[0],
        query,
        key.T,
        value.T,
        out,
        gains[1],
        gate,
        up,
        down,
    )


def solution(mesh):
    in_specs = (
        P("dp", None),
        P(),
        P(),
        P(None, "tensor"),
        P(None, "tensor"),
        P(None, "tensor"),
        P("tensor", None),
        P(),
        P(None, "tensor"),
        P(None, "tensor"),
        P("tensor", None),
        P("dp", None),
    )
    out_specs = (
        P("dp", None),
        P("dp", None),
        P(),
        P(None, "tensor"),
        P(None, "tensor"),
        P(None, "tensor"),
        P("tensor", None),
        P(),
        P(None, "tensor"),
        P(None, "tensor"),
        P("tensor", None),
    )
    return jax.shard_map(
        functools.partial(shards, mesh.shape["tensor"]),
        mesh=mesh,
        in_specs=in_specs,
        out_specs=out_specs,
        check_vma=False,
    )
```

```python
import functools

import jax
import jax.numpy as jnp
from jax import lax
from jax.experimental import pallas as pl
from jax.experimental.pallas import tpu as pltpu
from jax.sharding import PartitionSpec as P

HEAD_DIM = 96
GROUP_DEVS = 8
PB = 512
CL = 512
EPSILON = 1e-05
ROTARY_BASE = 100000.0
LOG2E = 1.4426950408889634
NEG = -1e30
MESH = pl.DeviceIdType.MESH
VM = pltpu.VMEM
F32 = jnp.float32
BF16 = jnp.bfloat16
NT = (((1,), (1,)), ((), ()))


def dot(a, b):
    return jnp.dot(a, b, preferred_element_type=F32)


def dot_nt(a, b):
    return lax.dot_general(a, b, NT, preferred_element_type=F32)


def dot_tn(a, b):
    return lax.dot_general(a, b, (((0,), (0,)), ((), ())), preferred_element_type=F32)


def causal(s):
    key = lax.broadcasted_iota(jnp.int32, s.shape, 0)
    query = lax.broadcasted_iota(jnp.int32, s.shape, 1)
    return jnp.where(key <= query, s, NEG)


def greet(targets):
    barrier = pltpu.get_barrier_semaphore()
    for target in targets:
        pl.semaphore_signal(barrier, inc=1, device_id=target, device_id_type=MESH)
    pl.semaphore_wait(barrier, len(targets))


def remote(src, dst, send, recv, target):
    return pltpu.make_async_remote_copy(
        src_ref=src, dst_ref=dst, send_sem=send, recv_sem=recv, device_id=target, device_id_type=MESH
    )


class Line:
    def __init__(self, nz, chunk, part, out, held, sems, shift=0):
        self.d, self.z = lax.axis_index("dp"), lax.axis_index("tensor")
        self.shift = shift
        self.chunk, self.part, self.out, self.held = chunk, part, out, held
        self.ss, self.rr, self.fs, self.fr = sems
        self.count = part.shape[0] // chunk
        self.root, self.last = nz // 2 - 1, nz - 1

    def rows(self, c):
        if self.shift:
            c = lax.rem(c + self.shift, self.count)
        return pl.ds(pl.multiple_of(c * self.chunk, self.chunk), self.chunk)

    def batch(self, i, n):
        if self.shift:
            i = lax.rem(i + self.shift // n, self.count // n)
        return pl.ds(pl.multiple_of(i * self.chunk * n, self.chunk * n), self.chunk * n)

    def toward(self, c, side, src):
        rows = self.rows(c)
        target = self.z + 1 if side == 0 else self.z - 1
        return remote(
            src.at[rows],
            (self.out if side == 0 else self.held).at[rows],
            self.ss.at[side, c],
            self.rr.at[side, c],
            (self.d, target),
        )

    def final(self, c, side):
        rows = self.rows(c)
        target = self.z - 1 if side == 0 else self.z + 1
        return remote(
            self.out.at[rows], self.out.at[rows], self.fs.at[side, c], self.fr.at[c], (self.d, target)
        )

    def mine(self, c, side):
        rows = self.rows(c)
        arrived = (self.out if side == 0 else self.held)[rows]
        return arrived.astype(F32) + self.part[rows].astype(F32)

    def issue(self, c):
        @pl.when(self.z == 0)
        def _():
            self.toward(c, 0, self.part).start()

        @pl.when(self.z == self.last)
        def _():
            self.toward(c, 1, self.part).start()

    def service(self, c):
        @pl.when((self.z > self.root) & (self.z < self.last))
        def _():
            rows = self.rows(c)
            self.toward(c, 1, self.held).wait_recv()
            self.held[rows] = self.mine(c, 1).astype(BF16)
            self.toward(c, 1, self.held).start()

    def ready(self, c):
        @pl.when(self.z != self.root)
        def _():
            self.final(c, 1).wait_recv()

        @pl.when((self.z > self.root) & (self.z < self.last))
        def _():
            self.final(c, 1).start()

        @pl.when(self.z == self.root)
        def _():
            rows = self.rows(c)
            self.toward(c, 0, self.out).wait_recv()
            self.toward(c, 1, self.held).wait_recv()
            self.out[rows] = (self.mine(c, 0) + self.held[rows].astype(F32)).astype(BF16)
            self.final(c, 0).start()
            self.final(c, 1).start()

    def drain(self):
        def body(c, carry):
            @pl.when(self.z < self.root + 1)
            def _():
                @pl.when(self.z == 0)
                def _():
                    self.toward(c, 0, self.part).wait_send()

                @pl.when(self.z == self.root)
                def _():
                    self.final(c, 0).wait_send()
                    self.final(c, 1).wait_send()

            @pl.when(self.z > self.root)
            def _():
                self.toward(c, 1, self.part).wait_send()

                @pl.when(self.z < self.last)
                def _():
                    self.final(c, 1).wait_send()

            return carry

        lax.fori_loop(0, self.count, body, 0)


def line_scratch(shape, chunk):
    count = shape[0] // chunk
    return [VM(shape, BF16)] + [pltpu.SemaphoreType.DMA((2, count))] * 3 + [
        pltpu.SemaphoreType.DMA((count,))
    ]


def neighbours(nz):
    d, z = lax.axis_index("dp"), lax.axis_index("tensor")
    return [(d, lax.rem(z + 1, nz)), (d, lax.rem(z + nz - 1, nz))]


def plane(masks):
    d, z = lax.axis_index("dp"), lax.axis_index("tensor")
    return [(jnp.bitwise_xor(d, m), z) for m in masks]


def loop(start, stop, body):
    def step(i, carry):
        body(i)
        return carry

    lax.fori_loop(start, stop, step, 0)


def fold_rows(values):
    return jnp.sum(values.reshape(values.shape[0] // 8, 8, values.shape[1]), axis=0)


class Plane:
    def __init__(self, height, width, sems):
        self.d, self.z = lax.axis_index("dp"), lax.axis_index("tensor")
        member = lax.rem(self.d, GROUP_DEVS)
        self.core = lax.rem(member, 2)
        self.chip = member // 2
        self.bit = (lax.rem(self.chip, 2), self.chip // 2)
        self.height, self.half, self.sems = height, width // 2, sems

    def rows(self, chip, core):
        return pl.ds(pl.multiple_of((chip * 2 + core) * self.height, 16), self.height)

    def cols(self, colour):
        return pl.ds(colour * self.half, self.half)

    def at(self, first, x, y):
        return x + 2 * y if first == 0 else y + 2 * x

    def copy(self, i, src, dst, mask):
        return remote(
            src, dst, self.sems.at[0, i], self.sems.at[1, i], (jnp.bitwise_xor(self.d, mask), self.z)
        )


class PlaneReduce(Plane):
    def __init__(self, src, mine, near, far, last, sems):
        super().__init__(src.shape[0] // GROUP_DEVS, src.shape[1], sems)
        self.src, self.mine, self.near, self.far, self.last = src, mine, near, far, last

    def to_core(self, i):
        return self.copy(i, self.src.at[self.rows(i, 1 - self.core)], self.near(i), 1)

    def fetch(self, i):
        rows = self.src.at[self.rows(i, self.core)]
        return pltpu.make_async_copy(rows, self.mine, self.sems.at[0, 10])

    def part_of(self, i, colour):
        return self.near(i).at[:, self.cols(colour)]

    def first(self, colour, k):
        i = self.at(colour, 1 - self.bit[colour], k)
        return self.copy(
            4 + 2 * colour + k, self.part_of(i, colour), self.far(colour, k), 2 << colour
        )

    def second(self, colour):
        i = self.at(colour, self.bit[colour], 1 - self.bit[1 - colour])
        return self.copy(8 + colour, self.part_of(i, colour), self.last(colour), 4 >> colour)

    def start(self):
        for i in range(4):
            self.to_core(i).start()
        if self.mine is not None:
            self.fetch(0).start()

    def after_core(self):
        for i in range(4):
            self.to_core(i).wait_recv()
            if self.mine is not None:
                self.fetch(i).wait()
                own = self.mine[...]
            else:
                own = self.src[self.rows(i, self.core)]
            near = self.near(i)
            near[...] = (own.astype(F32) + near[...].astype(F32)).astype(BF16)
            if self.mine is not None and i < 3:
                self.fetch(i + 1).start()
        for colour in range(2):
            for k in range(2):
                self.first(colour, k).start()

    def after_first(self):
        for colour in range(2):
            for k in range(2):
                self.first(colour, k).wait_recv()
                mine = self.part_of(self.at(colour, self.bit[colour], k), colour)
                mine[...] = (
                    mine[...].astype(F32) + self.far(colour, k)[...].astype(F32)
                ).astype(BF16)
        for colour in range(2):
            self.second(colour).start()

    def result(self, out):
        for colour in range(2):
            self.second(colour).wait_recv()
            out[:, self.cols(colour)] = (
                self.part_of(self.chip, colour)[...].astype(F32)
                + self.last(colour)[...].astype(F32)
            ).astype(BF16)

    def finish(self):
        for i in range(4):
            self.to_core(i).wait_send()
        for colour in range(2):
            self.second(colour).wait_send()
            for k in range(2):
                self.first(colour, k).wait_send()


class PlaneGather(Plane):
    def __init__(self, piece, out, sems):
        super().__init__(piece.shape[0], piece.shape[1], sems)
        self.piece, self.out = piece, out

    def place(self, dx, dy, colour):
        chip = jnp.bitwise_xor(self.chip, dx + 2 * dy)
        return self.out.at[self.rows(chip, self.core), self.cols(colour)]

    def keep(self):
        own = self.out.at[self.rows(self.chip, self.core)]
        return pltpu.make_async_copy(self.piece, own, self.sems.at[0, 10])

    def first(self, colour):
        dst = self.place(0, 0, colour)
        return self.copy(colour, self.piece.at[:, self.cols(colour)], dst, 4 >> colour)

    def second(self, colour, k):
        there = self.place(0, k, colour) if colour == 0 else self.place(k, 0, colour)
        src = self.piece.at[:, self.cols(colour)] if k == 0 else there
        return self.copy(2 + 2 * colour + k, src, there, 2 << colour)

    def share(self, k):
        rows = self.out.at[self.rows(jnp.bitwise_xor(self.chip, k), self.core)]
        return self.copy(6 + k, self.piece if k == 0 else rows, rows, 1)

    def start(self):
        self.keep().start()
        for colour in range(2):
            self.first(colour).start()
        self.share(0).start()

    def after_first(self):
        for colour in range(2):
            self.second(colour, 0).start()
            self.first(colour).wait_recv()
            self.second(colour, 1).start()

    def after_second(self):
        for colour in range(2):
            for k in range(2):
                self.second(colour, k).wait_recv()
        for k in (1, 2, 3):
            self.share(k).start()

    def finish(self):
        self.keep().wait()
        for k in range(4):
            self.share(k).wait()
        for colour in range(2):
            self.first(colour).wait_send()
            for k in range(2):
                self.second(colour, k).wait_send()


class LineGather:
    def __init__(self, nz, place, send, recv):
        self.d, self.z = lax.axis_index("dp"), lax.axis_index("tensor")
        self.nz, self.place, self.send, self.recv = nz, place, send, recv

    def step(self, right, s):
        index, target = (self.z - s, self.z + 1) if right else (self.z + s, self.z - 1)
        there = (index >= 0) & (index < self.nz) & (target >= 0) & (target < self.nz)
        where = self.place(index)
        way = int(right)
        return there, remote(where, where, self.send.at[way, s], self.recv.at[way, s], (self.d, target))

    def arrive(self, right, s):
        index = self.z - 1 - s if right else self.z + 1 + s
        where = self.place(index)
        way = int(right)

        @pl.when((index >= 0) & (index < self.nz))
        def _():
            remote(
                where, where, self.send.at[way, s], self.recv.at[way, s], (self.d, self.z)
            ).wait_recv()

    def start(self, s):
        for right in (True, False):
            if s > 0:
                self.arrive(right, s - 1)
            there, copy = self.step(right, s)
            pl.when(there)(copy.start)

    def last(self):
        for right in (True, False):
            self.arrive(right, self.nz - 2)

    def drain(self):
        for right in (True, False):
            for s in range(self.nz - 1):
                there, copy = self.step(right, s)
                pl.when(there)(copy.wait_send)


def forward_kernel(
    nz, q_ref, kv_ref, wo_ref, bias_ref, att, kv_all, lse_ref, wo_all, acc, top, total, ktok, mine,
    gs, gr, zs, zr, ws, wr, wp, load,
):
    heads = q_ref.shape[0]
    kvh = heads // 2
    d, z = lax.axis_index("dp"), lax.axis_index("tensor")
    some = mine.shape[0] // nz
    member = lax.rem(d, GROUP_DEVS)

    def own_place(index):
        return mine.at[pl.ds(pl.multiple_of(index * some, 16), some)]

    first_rows = pltpu.make_async_copy(
        wo_ref.at[pl.ds(pl.multiple_of(member * some, 16), some)], own_place(z), load.at[0]
    )
    first_rows.start()
    greet(plane((1, 2, 4, 6)) + neighbours(nz))
    own = kv_ref.at[:, :, pl.ds(0, PB)]
    firsts = [
        remote(own, kv_all.at[m], gs.at[m], gr.at[m], target)
        for m, target in zip((1, 2, 4, 6), plane((1, 2, 4, 6)))
    ]
    for copy in firsts:
        copy.start()
    w_line = LineGather(nz, own_place, ws, wr)
    w_plane = PlaneGather(mine, wo_all, wp)
    first_rows.wait()
    w_line.start(0)
    kv_all[0] = kv_ref[:, :, 0:PB]
    for h in range(kvh):
        ktok[8, h] = kv_ref[h, :, PB : PB + CL].T
        ktok[0, h] = kv_ref[h, :, 0:PB].T
    acc[...] = jnp.zeros_like(acc)
    top[...] = jnp.full_like(top, NEG)
    total[...] = jnp.zeros_like(total)

    def block(head, half, key, value, mask, bias):
        cols = pl.ds(half * PB, PB)
        s = dot(key, q_ref[head, :, cols])
        if mask:
            s = causal(s)
        old = top[head, :, cols]
        high = jnp.max(s, axis=0, keepdims=True)
        new = jnp.maximum(old, high if bias is None else high + bias)
        p = jnp.exp2(s - (new if bias is None else new - bias))
        shrink = jnp.exp2(old - new)
        total[head, :, cols] = total[head, :, cols] * shrink + jnp.sum(p, axis=0, keepdims=True)
        acc[head, :, cols] = acc[head, :, cols] * shrink + dot(value, p.astype(BF16))
        top[head, :, cols] = new

    def slot_step(slot, half, mask=False, bias=None):
        for head in range(heads):
            block(head, half, ktok[slot, head // 2], kv_all[slot, kvh + head // 2], mask, bias)

    for head in range(heads):
        block(head, 1, ktok[8, head // 2], kv_ref[kvh + head // 2, :, PB : PB + CL], True, None)

    def arrive(m):
        remote(kv_all.at[m], kv_all.at[m], gs.at[m], gr.at[m], (d, z)).wait_recv()

    def hand_on(m):
        return remote(kv_all.at[m], kv_all.at[m + 1], gs.at[m + 1], gr.at[m + 1], plane((1,))[0])

    def tail_slot(m):
        @pl.when(m > 0)
        def _():
            arrive(m)
            for h in range(kvh):
                ktok[m, h] = kv_all[m, h].T

        @pl.when((m > 0) & (lax.rem(m, 2) == 0))
        def _():
            hand_on(m).start()

        for s in range(1, nz - 1):

            @pl.when(m == 2 * s)
            def _():
                w_line.start(s)

        @pl.when(m == GROUP_DEVS - 1)
        def _():
            w_line.last()
            w_plane.start()

        slot_step(m, 1)

    loop(0, GROUP_DEVS, tail_slot)

    def finish(half):
        cols = pl.ds(half * PB, PB)
        for head in range(heads):
            att[z, pl.ds(head * HEAD_DIM, HEAD_DIM), cols] = (
                acc[head, :, cols] / total[head, :, cols]
            ).astype(BF16)
            lse_ref[head, :, cols] = top[head, :, cols] + jnp.log2(total[head, :, cols])

    lines = [
        LineGather(
            nz,
            lambda index, half=half: att.at[index, :, pl.ds(half * PB, PB)],
            zs.at[half],
            zr.at[half],
        )
        for half in range(2)
    ]
    finish(1)
    lines[1].start(0)
    slot_step(0, 0, mask=True)

    def prompt_slot(m):
        slot_step(m, 0, bias=bias_ref[m])

        @pl.when(m == 4)
        def _():
            w_plane.after_first()
            lines[1].start(1)

    loop(1, GROUP_DEVS, prompt_slot)
    finish(0)
    lines[0].start(0)
    w_plane.after_second()
    for s in range(2, nz - 1):
        lines[1].start(s)
    for s in range(1, nz - 1):
        lines[0].start(s)
    for line in lines:
        line.last()
    for line in lines + [w_line]:
        line.drain()
    w_plane.finish()
    for copy in firsts:
        copy.wait_send()
    for m in (2, 4, 6):
        hand_on(m).wait_send()


def forward_attention(nz, q, kv, w_out, bias):
    heads, tokens = q.shape[0], q.shape[2]
    kvh = heads // 2
    own, width = w_out.shape
    return pl.pallas_call(
        functools.partial(forward_kernel, nz),
        out_shape=(
            jax.ShapeDtypeStruct((nz, heads * HEAD_DIM, tokens), BF16),
            jax.ShapeDtypeStruct((GROUP_DEVS, 2 * kvh, HEAD_DIM, PB), BF16),
            jax.ShapeDtypeStruct((heads, 1, tokens), F32),
            jax.ShapeDtypeStruct((nz * own, width), BF16),
        ),
        in_specs=[
            pl.BlockSpec(memory_space=VM),
            pl.BlockSpec(memory_space=VM),
            pl.BlockSpec(memory_space=pl.ANY),
            pl.BlockSpec(memory_space=pltpu.SMEM),
        ],
        out_specs=(pl.BlockSpec(memory_space=VM),) * 3 + (pl.BlockSpec(memory_space=pl.ANY),),
        scratch_shapes=[
            VM((heads, HEAD_DIM, tokens), F32),
            VM((heads, 1, tokens), F32),
            VM((heads, 1, tokens), F32),
            VM((GROUP_DEVS + 1, kvh, PB, HEAD_DIM), BF16),
            VM((nz * own // GROUP_DEVS, width), BF16),
            pltpu.SemaphoreType.DMA((GROUP_DEVS,)),
            pltpu.SemaphoreType.DMA((GROUP_DEVS,)),
            pltpu.SemaphoreType.DMA((2, 2, nz - 1)),
            pltpu.SemaphoreType.DMA((2, 2, nz - 1)),
            pltpu.SemaphoreType.DMA((2, nz - 1)),
            pltpu.SemaphoreType.DMA((2, nz - 1)),
            pltpu.SemaphoreType.DMA((2, 11)),
            pltpu.SemaphoreType.DMA((1,)),
        ],
        compiler_params=pltpu.CompilerParams(
            collective_id=0, has_side_effects=True, vmem_limit_bytes=48 << 20
        ),
        cost_estimate=pl.CostEstimate(
            flops=40_000_000_000, bytes_accessed=12_000_000, transcendentals=19_000_000
        ),
        name="forward_attention",
    )(q, kv, w_out, bias)


class Stream:
    def __init__(self, rows, count, ins, out):
        self.rows, self.count, self.ins, self.out = rows, count, ins, out

    def load(self, i):
        slot = lax.rem(i, 2)
        return [
            pltpu.make_async_copy(src.at[self.rows(i)], buf.at[slot], sem.at[slot])
            for src, buf, sem in self.ins
        ]

    def store(self, i):
        dst, buf, sem = self.out
        slot = lax.rem(i, 2)
        return pltpu.make_async_copy(buf.at[slot], dst.at[self.rows(i)], sem.at[slot])

    def prime(self):
        for i in range(2):
            for copy in self.load(i):
                copy.start()

    def take(self, i):
        for copy in self.load(i):
            copy.wait()

        @pl.when(i >= 2)
        def _():
            self.store(i - 2).wait()

    def give(self, i):
        self.store(i).start()

        @pl.when(i + 2 < self.count)
        def _():
            for copy in self.load(i + 2):
                copy.start()

    def flush(self):
        for i in range(self.count - 2, self.count):
            self.store(i).wait()


def tail_kernel(
    nz, chunk, q_ref, kv_ref, do_ref, bias_ref, lse_ref, inner_ref, feed, cos_ref, sin_ref,
    gain_ref, gain_two, kv_all, mid_hbm, ffn_hbm, normed_hbm, x_hbm, ga_hbm, wq_hbm, wk_hbm, wv_hbm,
    gwo_hbm,
    act, gt, gains, summed, ffn_sum,
    kvs, wq, wk, wv, dq, dkv, near, far, ktok, vtok, low, total, held, f_piece, part, total_one, held_one, weights, a_near, a_far, a_last, a_piece, tile_in,
    mid_in, act_out, x_in, ga_in, gt_out, accum, box,
    ss, rr, fs, fr, ss1, rr1, fs1, fr1, ns, nr, ps, pr, a_sems, ag_sems, fg_sems, bs, br,
    loads, kv_sem, m_sem, act_sem, x_sem, g_sem, gt_sem,
):
    heads = q_ref.shape[0]
    kvh = heads // 2
    d, z = lax.axis_index("dp"), lax.axis_index("tensor")
    member = lax.rem(d, GROUP_DEVS)
    masks = range(1, GROUP_DEVS)
    nq = heads * HEAD_DIM
    nkv = kvh * HEAD_DIM
    tokens, width = feed.shape
    pairs = (
        (wq_hbm, wq),
        (wk_hbm, wk),
        (wv_hbm, wv),
        (gwo_hbm, weights.at[pl.ds(nq + 2 * nkv, gwo_hbm.shape[0])]),
    )
    fetches = [pltpu.make_async_copy(src, dst, loads.at[i]) for i, (src, dst) in enumerate(pairs)]

    def kv_load(t):
        slot = lax.rem(2 * t + 1 + t // 4, GROUP_DEVS)
        return pltpu.make_async_copy(
            kv_all.at[slot], kvs.at[lax.rem(t, 2)], kv_sem.at[lax.rem(t, 2)]
        )

    kv_load(0).start()
    first_piece = pltpu.make_async_copy(ffn_hbm, f_piece, loads.at[len(pairs)])
    first_piece.start()
    batch = 4
    line = Line(nz, chunk, feed, total, held, (ss, rr, fs, fr))
    line_one = Line(
        nz, chunk, part, total_one, held_one, (ss1, rr1, fs1, fr1), shift=tokens // chunk // 2
    )
    batches = line.count // batch
    acts = Stream(
        lambda i: line.batch(i, batch), batches, [(mid_hbm, mid_in, m_sem)], (act, act_out, act_sem)
    )
    outs = Stream(
        lambda i: line_one.batch(i, batch),
        batches,
        [(x_hbm, x_in, x_sem), (ga_hbm, ga_in, g_sem)],
        (gt, gt_out, gt_sem),
    )
    acts.prime()
    greet(neighbours(nz) + plane(masks))
    reduce_attn = PlaneReduce(
        weights,
        None,
        lambda i: a_near.at[i],
        lambda c, k: a_far.at[c, k],
        lambda c: a_last.at[c],
        a_sems,
    )
    gather_attn = PlaneGather(a_piece, summed, ag_sems)
    gather_ffn = PlaneGather(f_piece, ffn_sum, fg_sems)
    loop(0, line.count, line.issue)
    first_piece.wait()
    gather_ffn.start()
    for copy in fetches:
        copy.start()
    lag = 12
    ply = 3

    def ripple(s):
        @pl.when(s < line.count)
        def _():
            line.service(s)

        @pl.when(s >= lag)
        def _():
            line.ready(s - lag)

        @pl.when((s >= lag) & (lax.rem(s - lag, batch) == batch - 1))
        def _():
            i = (s - lag) // batch
            acts.take(i)
            act_out[lax.rem(i, 2)] = (
                mid_in[lax.rem(i, 2)].astype(F32) + total[line.batch(i, batch)].astype(F32)
            ).astype(BF16)
            acts.give(i)

    def background(s):
        @pl.when(s == 4)
        def _():
            gather_ffn.after_first()

        @pl.when(s == 11)
        def _():
            gather_ffn.after_second()

        loop(s * ply, s * ply + ply, ripple)

    dq[...] = jnp.zeros_like(dq)

    def block(head, half, keyt, mask, bias):
        h = head // 2
        cols = pl.ds(half * PB, PB)
        s = dot(ktok[h], q_ref[head, :, cols])
        if mask:
            s = causal(s)
        shift = lse_ref[head, :, cols]
        if bias is not None:
            shift = shift - bias
        p = jnp.exp2(s - shift)
        dp = dot(vtok[h], do_ref[head, :, cols])
        ds = (p * (dp - inner_ref[head, :, cols])).astype(BF16)
        dq[head, :, cols] += dot(keyt, ds)
        dv = dot_nt(do_ref[head, :, cols], p.astype(BF16))
        dk = dot_nt(q_ref[head, :, cols], ds)
        return dk, dv

    def total_of(parts):
        out = parts[0]
        for piece in parts[1:]:
            out = out + piece
        return out

    def turn_back(u, half):
        cols = pl.ds(half * PB, PB)
        cosine, sine = cos_ref[:, cols], sin_ref[:, cols]
        lower, upper = u[: HEAD_DIM // 2], u[HEAD_DIM // 2 :]
        return lower * cosine + upper * sine, upper * cosine - lower * sine

    def put_low(row, half, u, turned):
        cols = pl.ds(half * PB, PB)
        if not turned:
            low[pl.ds(row, HEAD_DIM), cols] = u.astype(BF16)
            return
        first, second = turn_back(u, half)
        low[pl.ds(row, HEAD_DIM // 2), cols] = first.astype(BF16)
        low[pl.ds(row + HEAD_DIM // 2, HEAD_DIM // 2), cols] = second.astype(BF16)

    for h in range(kvh):
        ktok[h] = kv_ref[h, :, PB : PB + CL].T
        vtok[h] = kv_ref[kvh + h, :, PB : PB + CL].T
    for h in range(kvh):
        both = [block(2 * h + r, 1, kv_ref[h, :, PB : PB + CL], True, None) for r in range(2)]
        put_low(nq + h * HEAD_DIM, 1, total_of([b[0] for b in both]) * (1.0 / LOG2E), True)
        put_low(nq + nkv + h * HEAD_DIM, 1, total_of([b[1] for b in both]), False)

    quarter = GROUP_DEVS // 2

    def slot_step(t, where, first):
        kv_load(t).wait()
        now = lax.rem(t, 2)
        for h in range(kvh):
            ktok[h] = kvs[now, h].T
            vtok[h] = kvs[now, kvh + h].T
        bias = None if first else bias_ref[lax.rem(2 * t + 1 + t // 4, GROUP_DEVS)]
        for h in range(kvh):
            background(t * 2 + h)
            both = []
            for r in range(2):
                both.append(block(2 * h + r, 1, kvs[now, h], False, None))
                both.append(block(2 * h + r, 0, kvs[now, h], first, bias))
            dkv[where, h] = (total_of([b[0] for b in both]) * (1.0 / LOG2E)).astype(BF16)
            dkv[where, kvh + h] = total_of([b[1] for b in both]).astype(BF16)

    def to_near(i):
        return remote(dkv.at[i], near.at[i], ns.at[i], nr.at[i], plane((1,))[0])

    def to_far(i):
        return remote(near.at[i], far.at[i], ps.at[i], pr.at[i], (jnp.bitwise_xor(d, 2 * i), z))

    def step(t):
        kv_load(t + 1).start()
        slot_step(t, t - t // quarter * (t - quarter), False)

        @pl.when(t < quarter)
        def _():
            to_near(t).start()

        @pl.when(t >= quarter)
        def _():
            i = t - quarter + 1
            to_near(i).wait_recv()
            near[i] = (dkv[quarter].astype(F32) + near[i].astype(F32)).astype(BF16)
            to_far(i).start()

    last = GROUP_DEVS - 1
    loop(0, last, step)
    slot_step(last, quarter, True)

    def back(j):
        group = tokens // 4
        rows = pl.ds(pl.multiple_of(j * group, group), group)
        a = [low[pl.ds(at, n), rows].T for at, n in ((0, nq), (nq, nkv), (nq + nkv, nkv))]
        size = 512
        for t in range(width // size):
            cols = pl.ds(t * size, size)
            part[rows, cols] = (
                dot_nt(a[0], wq[cols]) + dot_nt(a[1], wk[cols]) + dot_nt(a[2], wv[cols])
            ).astype(BF16)

    for copy in fetches:
        copy.wait()
    done = 2 * GROUP_DEVS * ply
    left = line.count + lag - done
    share = left // 4
    half_count = line.count // 2
    for head in range(heads):
        put_low(head * HEAD_DIM, 1, dq[head, :, PB : PB + CL] * HEAD_DIM ** (-0.5), True)
    loop(2, 4, back)
    loop(0, half_count, line_one.issue)
    loop(done, done + share, ripple)
    for head in range(heads):
        put_low(head * HEAD_DIM, 0, dq[head, :, 0:PB] * HEAD_DIM ** (-0.5), True)
    to_near(0).wait_recv()
    for i in range(1, quarter):
        to_far(i).wait_recv()
    for h in range(2 * kvh):
        home = dkv[quarter, h].astype(F32)
        home = home + near[0, h].astype(F32)
        for i in range(1, quarter):
            home = home + far[i, h].astype(F32)
        put_low(nq + h * HEAD_DIM, 0, home, h < kvh)
    loop(0, 2, back)
    loop(half_count, line.count, line_one.issue)
    loop(done + share, done + 2 * share, ripple)
    outs.prime()
    size = tile_in.shape[1]
    for t in range(width // size):
        cols = pl.ds(t * size, size)
        copy = pltpu.make_async_copy(normed_hbm.at[:, cols], tile_in, loads.at[len(pairs)])
        copy.start()
        copy.wait()
        weights[0 : nq + 2 * nkv, cols] = dot(low[...], tile_in[...]).astype(BF16)
    reduce_attn.start()
    loop(done + 2 * share, done + left, ripple)
    acts.flush()
    accum[...] = jnp.zeros_like(accum)
    gain = gain_ref[...]
    lag_one = 10

    def body(s):
        @pl.when(s < line_one.count)
        def _():
            line_one.service(s)

        @pl.when(s >= lag_one)
        def _():
            line_one.ready(s - lag_one)

        @pl.when((s >= lag_one) & (lax.rem(s - lag_one, batch) == batch - 1))
        def _():
            i = (s - lag_one) // batch
            outs.take(i)
            slot = lax.rem(i, 2)
            x = x_in[slot].astype(F32)
            inverse = lax.rsqrt(jnp.mean(x * x, axis=-1, keepdims=True) + EPSILON)
            upstream = total_one[line_one.batch(i, batch)].astype(F32)
            inner = upstream * gain
            through = inverse * inner - x * inverse**3 * jnp.mean(
                inner * x, axis=-1, keepdims=True
            )
            gt_out[slot] = (ga_in[slot].astype(F32) + through).astype(BF16)
            accum[...] += fold_rows(upstream * x * inverse)
            outs.give(i)

        @pl.when(s == 5)
        def _():
            reduce_attn.after_core()

        @pl.when(s == 18)
        def _():
            reduce_attn.after_first()

        @pl.when(s == 27)
        def _():
            reduce_attn.result(a_piece)
            gather_attn.start()

        @pl.when(s == 34)
        def _():
            gather_attn.after_first()

        @pl.when(s == 46)
        def _():
            gather_attn.after_second()

    loop(0, line_one.count + lag_one, body)
    box[member, 0:1] = jnp.sum(accum[...], axis=0, keepdims=True)
    box[member, 1:2] = gain_two[...]
    copies = [
        remote(box.at[member], box.at[member], bs.at[m], br.at[m], target)
        for m, target in zip(masks, plane(masks))
    ]
    for copy in copies:
        copy.start()
    outs.flush()
    for i in range(quarter):
        to_near(i).wait_send()
    for i in range(1, quarter):
        to_far(i).wait_send()
    line.drain()
    line_one.drain()
    reduce_attn.finish()
    gather_ffn.finish()
    gather_attn.finish()
    for copy in copies:
        copy.wait()
    result = box[0]
    for m in masks:
        result = result + box[m]
    gains[...] = result


def tail_stage(
    nz, q, kv, do, bias, lse, inner, feed, cosine, sine, gain, gain_two, kv_all, middle, ffn, normed,
    x, ga, w_query, w_key, w_value, grad_w_out, chunk=16,
):
    heads = q.shape[0]
    kvh = heads // 2
    tokens, width = feed.shape
    slot = (2 * kvh, HEAD_DIM, PB)
    n_attn = (heads + 2 * kvh) * HEAD_DIM + grad_w_out.shape[0]
    high, wide = ffn.shape
    low_high = n_attn // GROUP_DEVS
    count = tokens // chunk
    rows = 4 * chunk
    quarter = GROUP_DEVS // 2
    dma = lambda *shape: pltpu.SemaphoreType.DMA(shape)
    lines = [dma(2, count)] * 3 + [dma(count)]
    block = VM((2, rows, width), BF16)
    anywhere = pl.BlockSpec(memory_space=pl.ANY)
    vmem = pl.BlockSpec(memory_space=VM)
    return pl.pallas_call(
        functools.partial(tail_kernel, nz, chunk),
        out_shape=(
            jax.ShapeDtypeStruct(feed.shape, BF16),
            jax.ShapeDtypeStruct(feed.shape, BF16),
            jax.ShapeDtypeStruct((2, width), F32),
            jax.ShapeDtypeStruct((n_attn, width), BF16),
            jax.ShapeDtypeStruct((high * GROUP_DEVS, wide), BF16),
        ),
        in_specs=[vmem] * 3 + [pl.BlockSpec(memory_space=pltpu.SMEM)] + [vmem] * 7 + [anywhere] * 10,
        out_specs=(anywhere, anywhere, vmem, anywhere, anywhere),
        scratch_shapes=[
            VM((2,) + slot, BF16),
            VM(w_query.shape, BF16),
            VM(w_key.shape, BF16),
            VM(w_value.shape, BF16),
            VM((heads, HEAD_DIM, tokens), F32),
            VM((quarter + 1,) + slot, BF16),
            VM((quarter,) + slot, BF16),
            VM((quarter,) + slot, BF16),
            VM((kvh, PB, HEAD_DIM), BF16),
            VM((kvh, PB, HEAD_DIM), BF16),
            VM(((heads + 2 * kvh) * HEAD_DIM, tokens), BF16),
            VM(feed.shape, BF16),
            VM(feed.shape, BF16),
            VM((high, wide), BF16),
            VM(feed.shape, BF16),
            VM(feed.shape, BF16),
            VM(feed.shape, BF16),
            VM((n_attn, width), BF16),
            VM((4, low_high, width), BF16),
            VM((2, 2, low_high, width // 2), BF16),
            VM((2, low_high, width // 2), BF16),
            VM((low_high, width), BF16),
            VM((tokens, 512), BF16),
            block,
            block,
            block,
            block,
            block,
            VM((8, width), F32),
            VM((GROUP_DEVS, 2, width), F32),
        ]
        + lines * 2
        + [dma(quarter)] * 4
        + [dma(2, 11)] * 3
        + [dma(GROUP_DEVS)] * 2
        + [dma(5)]
        + [dma(2)] * 6,
        compiler_params=pltpu.CompilerParams(
            collective_id=1, has_side_effects=True, vmem_limit_bytes=60 << 20
        ),
        cost_estimate=pl.CostEstimate(
            flops=200_000_000_000, bytes_accessed=50_000_000, transcendentals=19_000_000
        ),
        name="tail_stage",
    )(
        q, kv, do, bias, lse, inner, feed, cosine, sine, gain, gain_two, kv_all, middle, ffn, normed,
        x, ga, w_query, w_key, w_value, grad_w_out,
    )


def middle_kernel(
    nz, chunk, att_hbm, wo_hbm, x_hbm, wg_hbm, wu_hbm, wd_hbm, cot_hbm, gain_ref,
    ga, mid, feed, gatt, inner_out, gwo, gain_two, gffn, piece,
    att, wo, wg, wu, wd, cot, mid32, nt2, hidden, gg, gu, part, total, accum, stage, load, store,
    r_sems, spent, held, ss, rr, fs, fr,
):
    z = lax.axis_index("tensor")
    pairs = ((x_hbm, mid), (att_hbm, att), (wg_hbm, wg), (wu_hbm, wu), (cot_hbm, cot), (wd_hbm, wd))
    loads = [pltpu.make_async_copy(src, dst, load.at[i]) for i, (src, dst) in enumerate(pairs)]
    own = gatt.shape[0]
    some = own // GROUP_DEVS

    def wo_rows(i):
        src = pl.ds(pl.multiple_of(i * some, 16), some)
        dst = pl.ds(pl.multiple_of(lax.rem(i, nz) * own + i // nz * some, 16), some)
        pltpu.make_async_copy(wo_hbm.at[src], wo.at[dst], load.at[len(pairs)]).start()

    for copy in loads[:2]:
        copy.start()
    loop(0, nz * GROUP_DEVS, wo_rows)
    for copy in loads[2:]:
        copy.start()
    greet(neighbours(nz) + plane((1, 2, 4)))
    tokens, width = mid.shape
    ff = wg.shape[1]
    heads = own // HEAD_DIM
    group = 256
    per = group // chunk
    ply = 4
    quarters = per // ply
    tile = 512
    gain = gain_ref[...]
    accum[...] = jnp.zeros_like(accum)
    line = Line(nz, chunk, part, total, held, (ss, rr, fs, fr))
    mine = pl.ds(pl.multiple_of(z * own, own), own)
    lag = 12

    def settle(c):
        rows = line.batch(c, ply)
        m = mid[rows].astype(F32)
        inverse = lax.rsqrt(jnp.mean(m * m, axis=-1, keepdims=True) + EPSILON)
        upstream = total[rows].astype(F32)
        inner = upstream * gain
        through = inverse * inner - m * inverse**3 * jnp.mean(inner * m, axis=-1, keepdims=True)
        ga[rows] = (cot[rows].astype(F32) + through).astype(BF16)
        accum[...] += fold_rows(upstream * m * inverse)

        @pl.when(lax.rem(c, quarters) == quarters - 1)
        def _():
            block = pl.ds(pl.multiple_of((c // quarters) * group, group), group)
            back = dot_nt(wo[mine], ga[block])
            gatt[:, block] = back.astype(BF16)
            for head in range(heads):
                some = pl.ds(head * HEAD_DIM, HEAD_DIM)
                there = att[pl.ds(pl.multiple_of(z * own + head * HEAD_DIM, 32), HEAD_DIM), block]
                inner_out[head, :, block] = jnp.sum(
                    gatt[some, block].astype(F32) * there.astype(F32), axis=0, keepdims=True
                )

    def ripple(s):
        @pl.when(s < line.count)
        def _():
            line.service(s)

        @pl.when(s >= lag)
        def _():
            line.ready(s - lag)

        @pl.when((s >= lag) & (lax.rem(s - lag, ply) == ply - 1))
        def _():
            settle((s - lag) // ply)

    def tick(s):
        @pl.when(s >= 0)
        def _():
            loop(s * ply, s * ply + ply, ripple)

    for copy in loads[:2]:
        copy.wait()
    pltpu.make_async_copy(wo_hbm, wo, load.at[len(pairs)]).wait()

    def forward(j):
        rows = pl.ds(pl.multiple_of(j * group, group), group)
        a = att[:, rows].T
        for t in range(width // tile):
            cols = pl.ds(t * tile, tile)
            mid32[:, cols] = mid[rows, cols].astype(F32) + dot(a, wo[:, cols])
        m = mid32[...]
        mid[rows] = m.astype(BF16)
        inverse = lax.rsqrt(jnp.mean(m * m, axis=-1, keepdims=True) + EPSILON)
        nt2[rows] = (m * inverse * gain).astype(BF16)

        @pl.when(j == 0)
        def _():
            for copy in loads[2:]:
                copy.wait()

        tick(2 * j - 3)
        for t in range(ff // tile):
            cols = pl.ds(t * tile, tile)
            gate = dot(nt2[rows], wg[:, cols])
            up = dot(nt2[rows], wu[:, cols])
            back = dot_nt(cot[rows], wd[cols])
            sig = jax.nn.sigmoid(gate)
            silu = gate * sig
            hidden[rows, cols] = (silu * up).astype(BF16)
            gu[rows, cols] = (back * silu).astype(BF16)
            gg[rows, cols] = (back * up * (sig * (1.0 + gate * (1.0 - sig)))).astype(BF16)
        for t in range(width // tile):
            cols = pl.ds(t * tile, tile)
            part[rows, cols] = (dot_nt(gg[rows], wg[cols]) + dot_nt(gu[rows], wu[cols])).astype(BF16)
        loop(j * per, j * per + per, line.issue)
        for t in range(width // tile):
            cols = pl.ds(t * tile, tile)
            feed[rows, cols] = dot(hidden[rows], wd[:, cols]).astype(BF16)
        tick(2 * j - 2)

    steps = tokens // group
    loop(0, steps, forward)
    for target in plane((1, 2, 4)):
        pl.semaphore_signal(spent, inc=1, device_id=target, device_id_type=MESH)
    high, half = width // GROUP_DEVS, ff // 2

    def rows_of(n):
        return pl.ds(pl.multiple_of(n * high, 16), high)

    def reduce_of(q):
        src = gffn.at[:, pl.ds(q * ff, ff)]
        own = stage.at[0, pl.ds(0, high), pl.ds(q * ff, ff)]
        sems = r_sems.at[q]
        if q < 2:
            room = (wg, wu)[q]
            return PlaneReduce(
                src,
                own,
                lambda i: room.at[rows_of(i)],
                lambda c, n: room.at[rows_of(4 + n), pl.ds(c * half, half)],
                lambda c: room.at[rows_of(6), pl.ds(c * half, half)],
                sems,
            )
        return PlaneReduce(
            src,
            own,
            lambda i: wd.at[rows_of(i), pl.ds(0, ff)],
            lambda c, n: wd.at[rows_of(2 * c + n), pl.ds(ff, half)],
            lambda c: wd.at[rows_of(4), pl.ds(c * half, half)],
            sems,
        )

    reduces = [reduce_of(q) for q in range(3)]
    done = 2 * steps - 3
    slabs = width // group

    def put(t):
        return pltpu.make_async_copy(
            stage.at[lax.rem(t, 2)],
            gffn.at[pl.ds(pl.multiple_of(t * group, group), group)],
            store.at[lax.rem(t, 2)],
        )

    def weights(t):
        @pl.when(t >= 2)
        def _():
            put(t - 2).wait()

        slot = lax.rem(t, 2)
        cols = pl.ds(pl.multiple_of(t * group, group), group)
        a = nt2[:, cols].T
        stage[slot, :, 0:ff] = dot(a, gg[...]).astype(BF16)
        stage[slot, :, ff : 2 * ff] = dot(a, gu[...]).astype(BF16)
        stage[slot, :, 2 * ff : 3 * ff] = dot(cot[:, cols].T, hidden[...]).astype(BF16)
        put(t).start()

        @pl.when(lax.rem(t, 2) == 1)
        def _():
            tick(done + t // 2)

    loop(0, slabs, weights)
    for t in (slabs - 2, slabs - 1):
        put(t).wait()
    pl.semaphore_wait(spent, 3)
    for reduce in reduces:
        reduce.start()
    begin, end = (done + slabs // 2) * ply, line.count + lag
    marks = (begin, begin + 9, begin + 32, end)
    loop(marks[0], marks[1], ripple)
    for reduce in reduces:
        reduce.after_core()
    loop(marks[1], marks[2], ripple)
    for reduce in reduces:
        reduce.after_first()
    loop(marks[2], marks[3], ripple)
    for t in range(width // tile):
        cols = pl.ds(t * tile, tile)
        gwo[:, cols] = dot(att[mine], ga[:, cols]).astype(BF16)
    gain_two[...] = jnp.sum(accum[...], axis=0, keepdims=True)
    for q in range(3):
        reduces[q].result(stage.at[1, pl.ds(0, high), pl.ds(q * ff, ff)])
    out = pltpu.make_async_copy(stage.at[1, pl.ds(0, high)], piece, store.at[0])
    out.start()
    for reduce in reduces:
        reduce.finish()
    line.drain()
    out.wait()


def middle_stage(nz, att_all, w_out_all, x, w_gate, w_up, w_down, cot, gain, chunk=16):
    tokens, width = x.shape
    ff = w_gate.shape[1]
    own = w_out_all.shape[0] // nz
    heads = own // HEAD_DIM
    group = 256
    wide = jax.ShapeDtypeStruct((tokens, width), BF16)
    return pl.pallas_call(
        functools.partial(middle_kernel, nz, chunk),
        out_shape=(
            wide,
            wide,
            wide,
            jax.ShapeDtypeStruct((own, tokens), BF16),
            jax.ShapeDtypeStruct((heads, 1, tokens), F32),
            jax.ShapeDtypeStruct((own, width), BF16),
            jax.ShapeDtypeStruct((1, width), F32),
            jax.ShapeDtypeStruct((width, 3 * ff), BF16),
            jax.ShapeDtypeStruct((width // GROUP_DEVS, 3 * ff), BF16),
        ),
        in_specs=[pl.BlockSpec(memory_space=pl.ANY)] * 7 + [pl.BlockSpec(memory_space=VM)],
        out_specs=(pl.BlockSpec(memory_space=VM),) * 7 + (pl.BlockSpec(memory_space=pl.ANY),) * 2,
        scratch_shapes=[
            VM(w_out_all.shape[:1] + (tokens,), BF16),
            VM(w_out_all.shape, BF16),
            VM((width, ff), BF16),
            VM((width, ff), BF16),
            VM((ff, width), BF16),
            VM((tokens, width), BF16),
            VM((group, width), F32),
            VM((tokens, width), BF16),
            VM((tokens, ff), BF16),
            VM((tokens, ff), BF16),
            VM((tokens, ff), BF16),
            VM((tokens, width), BF16),
            VM((tokens, width), BF16),
            VM((8, width), F32),
            VM((2, group, 3 * ff), BF16),
            pltpu.SemaphoreType.DMA((7,)),
            pltpu.SemaphoreType.DMA((2,)),
            pltpu.SemaphoreType.DMA((3, 2, 11)),
            pltpu.SemaphoreType.REGULAR,
        ]
        + line_scratch((tokens, width), chunk),
        compiler_params=pltpu.CompilerParams(
            collective_id=2, has_side_effects=True, vmem_limit_bytes=60 << 20
        ),
        cost_estimate=pl.CostEstimate(
            flops=100_000_000_000, bytes_accessed=50_000_000, transcendentals=1_000_000
        ),
        name="middle_stage",
    )(att_all, w_out_all, x, w_gate, w_up, w_down, cot, gain)


def finish_kernel(nq, nk, ffn, attn, gt, act, gate, up, down, q, k, v, o, gt_out, act_out):
    ff = gate.shape[1]
    gate[...] = ffn[:, 0:ff].astype(F32)
    up[...] = ffn[:, ff : 2 * ff].astype(F32)
    down[...] = ffn[:, 2 * ff : 3 * ff].astype(F32).T
    q[...] = attn[0:nq].astype(F32).T
    k[...] = attn[nq : nq + nk].astype(F32)
    v[...] = attn[nq + nk : nq + 2 * nk].astype(F32)
    o[...] = attn[nq + 2 * nk :].astype(F32)
    gt_out[...] = gt[...]
    act_out[...] = act[...]


def finish(ffn, attn, gt, act, nq, nk):
    width, ff = ffn.shape[0], ffn.shape[1] // 3
    tokens, own = gt.shape[0], attn.shape[0] - nq - 2 * nk
    tile = 256
    wide = lambda *shape: jax.ShapeDtypeStruct(shape, F32)
    down = lambda rows: pl.BlockSpec((tile, rows), lambda i: (i, 0))
    side = lambda rows: pl.BlockSpec((rows, tile), lambda i: (0, i))
    return pl.pallas_call(
        functools.partial(finish_kernel, nq, nk),
        grid=(width // tile,),
        out_shape=(
            wide(width, ff),
            wide(width, ff),
            wide(ff, width),
            wide(width, nq),
            wide(nk, width),
            wide(nk, width),
            wide(own, width),
            jax.ShapeDtypeStruct(gt.shape, gt.dtype),
            jax.ShapeDtypeStruct(act.shape, act.dtype),
        ),
        in_specs=[down(3 * ff), side(attn.shape[0]), side(tokens), side(tokens)],
        out_specs=(
            down(ff),
            down(ff),
            side(ff),
            down(nq),
            side(nk),
            side(nk),
            side(own),
            side(tokens),
            side(tokens),
        ),
        compiler_params=pltpu.CompilerParams(vmem_limit_bytes=40 << 20),
        name="finish",
    )(ffn, attn, gt, act)


def rms_inverse(inputs):
    return lax.rsqrt(jnp.mean(inputs * inputs, axis=-1, keepdims=True) + EPSILON)


def rotate(u, cosine, sine):
    half = HEAD_DIM // 2
    lower, upper = u[:, :half], u[:, half:]
    return jnp.concatenate(
        [lower * cosine - upper * sine, upper * cosine + lower * sine], axis=1
    )


def shards(
    nz,
    tokens,
    block_order,
    attn_gain,
    w_query,
    w_key,
    w_value,
    w_out,
    mlp_gain,
    w_gate,
    w_up,
    w_down,
    cotangent,
):
    device = lax.axis_index("dp")
    n_dp = lax.axis_size("dp")
    member = device % GROUP_DEVS
    order_row = lax.dynamic_index_in_dim(block_order, device // GROUP_DEVS, 0, keepdims=False)
    by_slot = order_row[jnp.bitwise_xor(jnp.arange(GROUP_DEVS), member)]
    own_block = by_slot[0]
    bias = jnp.where(by_slot <= own_block, 0.0, NEG).astype(F32)
    offsets = jnp.arange(PB, dtype=jnp.int32)
    places = jnp.concatenate([own_block * PB + offsets, GROUP_DEVS * PB + offsets])
    halfway = HEAD_DIM // 2
    frequency = ROTARY_BASE ** (-(jnp.arange(halfway, dtype=F32) * 2.0) / HEAD_DIM)
    angle = frequency[:, None] * places.astype(F32)[None, :]
    cosine, sine = jnp.cos(angle)[None], jnp.sin(angle)[None]

    count = tokens.shape[0]
    factor = HEAD_DIM ** (-0.5)
    inputs = tokens.astype(F32)
    inverse_one = rms_inverse(inputs)
    normed = (inputs * inverse_one * attn_gain).astype(BF16)

    def project(weight):
        out = lax.dot_general(
            weight, normed, (((0,), (1,)), ((), ())), preferred_element_type=F32
        )
        return out.reshape(-1, HEAD_DIM, count)

    queries = (rotate(project(w_query), cosine, sine) * (factor * LOG2E)).astype(BF16)
    keys = rotate(project(w_key), cosine, sine).astype(BF16)
    values = project(w_value).astype(BF16)
    kv = jnp.concatenate([keys, values], axis=0)
    heads, kvh = queries.shape[0], keys.shape[0]

    att_all, kv_all, lse, w_out_all = forward_attention(nz, queries, kv, w_out, bias)
    grad_attention, middle, feed_part, grad_attended, row_inner, grad_w_out, grad_gain_two, _, ffn_piece = (
        middle_stage(
            nz,
            att_all.reshape(-1, count),
            w_out_all,
            tokens,
            w_gate,
            w_up,
            w_down,
            cotangent,
            mlp_gain[None],
        )
    )
    activations, grad_tokens, gains, grad_attn, grad_ffn = tail_stage(
        nz,
        queries,
        kv,
        grad_attended.reshape(heads, HEAD_DIM, count),
        bias,
        lse,
        row_inner,
        feed_part,
        cosine[0],
        sine[0],
        attn_gain[None],
        grad_gain_two,
        kv_all,
        middle,
        ffn_piece,
        normed,
        tokens,
        grad_attention,
        w_query,
        w_key,
        w_value,
        grad_w_out,
    )
    if n_dp > GROUP_DEVS:
        gains = lax.psum(gains, "dp") * (1.0 / GROUP_DEVS)
        grad_attn = lax.psum(grad_attn.astype(F32), "dp") * (1.0 / GROUP_DEVS)
        grad_ffn = lax.psum(grad_ffn.astype(F32), "dp") * (1.0 / GROUP_DEVS)
    nq, nk = w_query.shape[1], w_key.shape[1]

    gate, up, down, query, key, value, out, grad_tokens, activations = finish(
        grad_ffn, grad_attn, grad_tokens, activations, nq, nk
    )
    return (
        activations,
        grad_tokens,
        gains[0],
        query,
        key.T,
        value.T,
        out,
        gains[1],
        gate,
        up,
        down,
    )


def solution(mesh):
    in_specs = (
        P("dp", None),
        P(),
        P(),
        P(None, "tensor"),
        P(None, "tensor"),
        P(None, "tensor"),
        P("tensor", None),
        P(),
        P(None, "tensor"),
        P(None, "tensor"),
        P("tensor", None),
        P("dp", None),
    )
    out_specs = (
        P("dp", None),
        P("dp", None),
        P(),
        P(None, "tensor"),
        P(None, "tensor"),
        P(None, "tensor"),
        P("tensor", None),
        P(),
        P(None, "tensor"),
        P(None, "tensor"),
        P("tensor", None),
    )
    return jax.shard_map(
        functools.partial(shards, mesh.shape["tensor"]),
        mesh=mesh,
        in_specs=in_specs,
        out_specs=out_specs,
        check_vma=False,
    )
```

```python
import functools

import jax
import jax.numpy as jnp
from jax import lax
from jax.experimental import pallas as pl
from jax.experimental.pallas import tpu as pltpu
from jax.sharding import PartitionSpec as P

HEAD_DIM = 96
GROUP_DEVS = 8
PB = 512
CL = 512
EPSILON = 1e-05
ROTARY_BASE = 100000.0
LOG2E = 1.4426950408889634
NEG = -1e30
MESH = pl.DeviceIdType.MESH
VM = pltpu.VMEM
F32 = jnp.float32
BF16 = jnp.bfloat16
NT = (((1,), (1,)), ((), ()))


def dot(a, b):
    return jnp.dot(a, b, preferred_element_type=F32)


def dot_nt(a, b):
    return lax.dot_general(a, b, NT, preferred_element_type=F32)


def dot_tn(a, b):
    return lax.dot_general(a, b, (((0,), (0,)), ((), ())), preferred_element_type=F32)


def causal(s):
    key = lax.broadcasted_iota(jnp.int32, s.shape, 0)
    query = lax.broadcasted_iota(jnp.int32, s.shape, 1)
    return jnp.where(key <= query, s, NEG)


def greet(targets):
    barrier = pltpu.get_barrier_semaphore()
    for target in targets:
        pl.semaphore_signal(barrier, inc=1, device_id=target, device_id_type=MESH)
    pl.semaphore_wait(barrier, len(targets))


def remote(src, dst, send, recv, target):
    return pltpu.make_async_remote_copy(
        src_ref=src, dst_ref=dst, send_sem=send, recv_sem=recv, device_id=target, device_id_type=MESH
    )


class Line:
    def __init__(self, nz, chunk, part, out, held, sems, shift=0):
        self.d, self.z = lax.axis_index("dp"), lax.axis_index("tensor")
        self.shift = shift
        self.chunk, self.part, self.out, self.held = chunk, part, out, held
        self.ss, self.rr, self.fs, self.fr = sems
        self.count = part.shape[0] // chunk
        self.root, self.last = nz // 2 - 1, nz - 1

    def rows(self, c):
        if self.shift:
            c = lax.rem(c + self.shift, self.count)
        return pl.ds(pl.multiple_of(c * self.chunk, self.chunk), self.chunk)

    def batch(self, i, n):
        if self.shift:
            i = lax.rem(i + self.shift // n, self.count // n)
        return pl.ds(pl.multiple_of(i * self.chunk * n, self.chunk * n), self.chunk * n)

    def toward(self, c, side, src):
        rows = self.rows(c)
        target = self.z + 1 if side == 0 else self.z - 1
        return remote(
            src.at[rows],
            (self.out if side == 0 else self.held).at[rows],
            self.ss.at[side, c],
            self.rr.at[side, c],
            (self.d, target),
        )

    def final(self, c, side):
        rows = self.rows(c)
        target = self.z - 1 if side == 0 else self.z + 1
        return remote(
            self.out.at[rows], self.out.at[rows], self.fs.at[side, c], self.fr.at[c], (self.d, target)
        )

    def mine(self, c, side):
        rows = self.rows(c)
        arrived = (self.out if side == 0 else self.held)[rows]
        return arrived.astype(F32) + self.part[rows].astype(F32)

    def issue(self, c):
        @pl.when(self.z == 0)
        def _():
            self.toward(c, 0, self.part).start()

        @pl.when(self.z == self.last)
        def _():
            self.toward(c, 1, self.part).start()

    def service(self, c):
        @pl.when((self.z > self.root) & (self.z < self.last))
        def _():
            rows = self.rows(c)
            self.toward(c, 1, self.held).wait_recv()
            self.held[rows] = self.mine(c, 1).astype(BF16)
            self.toward(c, 1, self.held).start()

    def ready(self, c):
        @pl.when(self.z != self.root)
        def _():
            self.final(c, 1).wait_recv()

        @pl.when((self.z > self.root) & (self.z < self.last))
        def _():
            self.final(c, 1).start()

        @pl.when(self.z == self.root)
        def _():
            rows = self.rows(c)
            self.toward(c, 0, self.out).wait_recv()
            self.toward(c, 1, self.held).wait_recv()
            self.out[rows] = (self.mine(c, 0) + self.held[rows].astype(F32)).astype(BF16)
            self.final(c, 0).start()
            self.final(c, 1).start()

    def drain(self):
        def body(c, carry):
            @pl.when(self.z < self.root + 1)
            def _():
                @pl.when(self.z == 0)
                def _():
                    self.toward(c, 0, self.part).wait_send()

                @pl.when(self.z == self.root)
                def _():
                    self.final(c, 0).wait_send()
                    self.final(c, 1).wait_send()

            @pl.when(self.z > self.root)
            def _():
                self.toward(c, 1, self.part).wait_send()

                @pl.when(self.z < self.last)
                def _():
                    self.final(c, 1).wait_send()

            return carry

        lax.fori_loop(0, self.count, body, 0)


def line_scratch(shape, chunk):
    count = shape[0] // chunk
    return [VM(shape, BF16)] + [pltpu.SemaphoreType.DMA((2, count))] * 3 + [
        pltpu.SemaphoreType.DMA((count,))
    ]


def neighbours(nz):
    d, z = lax.axis_index("dp"), lax.axis_index("tensor")
    return [(d, lax.rem(z + 1, nz)), (d, lax.rem(z + nz - 1, nz))]


def plane(masks):
    d, z = lax.axis_index("dp"), lax.axis_index("tensor")
    return [(jnp.bitwise_xor(d, m), z) for m in masks]


def loop(start, stop, body):
    def step(i, carry):
        body(i)
        return carry

    lax.fori_loop(start, stop, step, 0)


def fold_rows(values):
    return jnp.sum(values.reshape(values.shape[0] // 8, 8, values.shape[1]), axis=0)


class Plane:
    def __init__(self, height, width, sems):
        self.d, self.z = lax.axis_index("dp"), lax.axis_index("tensor")
        member = lax.rem(self.d, GROUP_DEVS)
        self.core = lax.rem(member, 2)
        self.chip = member // 2
        self.bit = (lax.rem(self.chip, 2), self.chip // 2)
        self.height, self.half, self.sems = height, width // 2, sems

    def rows(self, chip, core):
        return pl.ds(pl.multiple_of((chip * 2 + core) * self.height, 16), self.height)

    def cols(self, colour):
        return pl.ds(colour * self.half, self.half)

    def at(self, first, x, y):
        return x + 2 * y if first == 0 else y + 2 * x

    def copy(self, i, src, dst, mask):
        return remote(
            src, dst, self.sems.at[0, i], self.sems.at[1, i], (jnp.bitwise_xor(self.d, mask), self.z)
        )


class PlaneReduce(Plane):
    def __init__(self, src, mine, near, far, last, sems):
        super().__init__(src.shape[0] // GROUP_DEVS, src.shape[1], sems)
        self.src, self.mine, self.near, self.far, self.last = src, mine, near, far, last

    def to_core(self, i):
        return self.copy(i, self.src.at[self.rows(i, 1 - self.core)], self.near(i), 1)

    def fetch(self, i):
        rows = self.src.at[self.rows(i, self.core)]
        return pltpu.make_async_copy(rows, self.mine, self.sems.at[0, 10])

    def part_of(self, i, colour):
        return self.near(i).at[:, self.cols(colour)]

    def first(self, colour, k):
        i = self.at(colour, 1 - self.bit[colour], k)
        return self.copy(
            4 + 2 * colour + k, self.part_of(i, colour), self.far(colour, k), 2 << colour
        )

    def second(self, colour):
        i = self.at(colour, self.bit[colour], 1 - self.bit[1 - colour])
        return self.copy(8 + colour, self.part_of(i, colour), self.last(colour), 4 >> colour)

    def start(self):
        for i in range(4):
            self.to_core(i).start()
        if self.mine is not None:
            self.fetch(0).start()

    def after_core(self):
        for i in range(4):
            self.to_core(i).wait_recv()
            if self.mine is not None:
                self.fetch(i).wait()
                own = self.mine[...]
            else:
                own = self.src[self.rows(i, self.core)]
            near = self.near(i)
            near[...] = (own.astype(F32) + near[...].astype(F32)).astype(BF16)
            if self.mine is not None and i < 3:
                self.fetch(i + 1).start()
        for colour in range(2):
            for k in range(2):
                self.first(colour, k).start()

    def after_first(self):
        for colour in range(2):
            for k in range(2):
                self.first(colour, k).wait_recv()
                mine = self.part_of(self.at(colour, self.bit[colour], k), colour)
                mine[...] = (
                    mine[...].astype(F32) + self.far(colour, k)[...].astype(F32)
                ).astype(BF16)
        for colour in range(2):
            self.second(colour).start()

    def result(self, out):
        for colour in range(2):
            self.second(colour).wait_recv()
            out[:, self.cols(colour)] = (
                self.part_of(self.chip, colour)[...].astype(F32)
                + self.last(colour)[...].astype(F32)
            ).astype(BF16)

    def finish(self):
        for i in range(4):
            self.to_core(i).wait_send()
        for colour in range(2):
            self.second(colour).wait_send()
            for k in range(2):
                self.first(colour, k).wait_send()


class PlaneGather(Plane):
    def __init__(self, piece, out, sems):
        super().__init__(piece.shape[0], piece.shape[1], sems)
        self.piece, self.out = piece, out

    def place(self, dx, dy, colour):
        chip = jnp.bitwise_xor(self.chip, dx + 2 * dy)
        return self.out.at[self.rows(chip, self.core), self.cols(colour)]

    def keep(self):
        own = self.out.at[self.rows(self.chip, self.core)]
        return pltpu.make_async_copy(self.piece, own, self.sems.at[0, 10])

    def first(self, colour):
        dst = self.place(0, 0, colour)
        return self.copy(colour, self.piece.at[:, self.cols(colour)], dst, 4 >> colour)

    def second(self, colour, k):
        there = self.place(0, k, colour) if colour == 0 else self.place(k, 0, colour)
        src = self.piece.at[:, self.cols(colour)] if k == 0 else there
        return self.copy(2 + 2 * colour + k, src, there, 2 << colour)

    def share(self, k):
        rows = self.out.at[self.rows(jnp.bitwise_xor(self.chip, k), self.core)]
        return self.copy(6 + k, self.piece if k == 0 else rows, rows, 1)

    def start(self):
        self.keep().start()
        for colour in range(2):
            self.first(colour).start()
        self.share(0).start()

    def after_first(self):
        for colour in range(2):
            self.second(colour, 0).start()
            self.first(colour).wait_recv()
            self.second(colour, 1).start()

    def after_second(self):
        for colour in range(2):
            for k in range(2):
                self.second(colour, k).wait_recv()
        for k in (1, 2, 3):
            self.share(k).start()

    def finish(self):
        self.keep().wait()
        for k in range(4):
            self.share(k).wait()
        for colour in range(2):
            self.first(colour).wait_send()
            for k in range(2):
                self.second(colour, k).wait_send()


class LineGather:
    def __init__(self, nz, place, send, recv):
        self.d, self.z = lax.axis_index("dp"), lax.axis_index("tensor")
        self.nz, self.place, self.send, self.recv = nz, place, send, recv

    def step(self, right, s):
        index, target = (self.z - s, self.z + 1) if right else (self.z + s, self.z - 1)
        there = (index >= 0) & (index < self.nz) & (target >= 0) & (target < self.nz)
        where = self.place(index)
        way = int(right)
        return there, remote(where, where, self.send.at[way, s], self.recv.at[way, s], (self.d, target))

    def arrive(self, right, s):
        index = self.z - 1 - s if right else self.z + 1 + s
        where = self.place(index)
        way = int(right)

        @pl.when((index >= 0) & (index < self.nz))
        def _():
            remote(
                where, where, self.send.at[way, s], self.recv.at[way, s], (self.d, self.z)
            ).wait_recv()

    def start(self, s):
        for right in (True, False):
            if s > 0:
                self.arrive(right, s - 1)
            there, copy = self.step(right, s)
            pl.when(there)(copy.start)

    def last(self):
        for right in (True, False):
            self.arrive(right, self.nz - 2)

    def drain(self):
        for right in (True, False):
            for s in range(self.nz - 1):
                there, copy = self.step(right, s)
                pl.when(there)(copy.wait_send)


def forward_kernel(
    nz, q_ref, kv_ref, wo_ref, bias_ref, att_hbm, kv_hbm, lse_ref, wo_all, att, kv_all, acc, top, total, ktok, mine,
    gs, gr, zs, zr, ws, wr, wp, load, leave,
):
    heads = q_ref.shape[0]
    kvh = heads // 2
    d, z = lax.axis_index("dp"), lax.axis_index("tensor")
    some = mine.shape[0] // nz
    member = lax.rem(d, GROUP_DEVS)

    def own_place(index):
        return mine.at[pl.ds(pl.multiple_of(index * some, 16), some)]

    first_rows = pltpu.make_async_copy(
        wo_ref.at[pl.ds(pl.multiple_of(member * some, 16), some)], own_place(z), load.at[0]
    )
    first_rows.start()
    greet(plane((1, 2, 4, 6)) + neighbours(nz))
    own = kv_ref.at[:, :, pl.ds(0, PB)]
    firsts = [
        remote(own, kv_all.at[m], gs.at[m], gr.at[m], target)
        for m, target in zip((1, 2, 4, 6), plane((1, 2, 4, 6)))
    ]
    for copy in firsts:
        copy.start()
    w_line = LineGather(nz, own_place, ws, wr)
    w_plane = PlaneGather(mine, wo_all, wp)
    first_rows.wait()
    w_line.start(0)
    kv_all[0] = kv_ref[:, :, 0:PB]
    for h in range(kvh):
        ktok[8, h] = kv_ref[h, :, PB : PB + CL].T
        ktok[0, h] = kv_ref[h, :, 0:PB].T
    acc[...] = jnp.zeros_like(acc)
    top[...] = jnp.full_like(top, NEG)
    total[...] = jnp.zeros_like(total)

    def block(head, half, key, value, mask, bias):
        cols = pl.ds(half * PB, PB)
        s = dot(key, q_ref[head, :, cols])
        if mask:
            s = causal(s)
        old = top[head, :, cols]
        high = jnp.max(s, axis=0, keepdims=True)
        new = jnp.maximum(old, high if bias is None else high + bias)
        p = jnp.exp2(s - (new if bias is None else new - bias))
        shrink = jnp.exp2(old - new)
        total[head, :, cols] = total[head, :, cols] * shrink + jnp.sum(p, axis=0, keepdims=True)
        acc[head, :, cols] = acc[head, :, cols] * shrink + dot(value, p.astype(BF16))
        top[head, :, cols] = new

    def slot_step(slot, half, mask=False, bias=None):
        for head in range(heads):
            block(head, half, ktok[slot, head // 2], kv_all[slot, kvh + head // 2], mask, bias)

    for head in range(heads):
        block(head, 1, ktok[8, head // 2], kv_ref[kvh + head // 2, :, PB : PB + CL], True, None)

    def arrive(m):
        remote(kv_all.at[m], kv_all.at[m], gs.at[m], gr.at[m], (d, z)).wait_recv()

    def hand_on(m):
        return remote(kv_all.at[m], kv_all.at[m + 1], gs.at[m + 1], gr.at[m + 1], plane((1,))[0])

    def tail_slot(m):
        @pl.when(m > 0)
        def _():
            arrive(m)
            for h in range(kvh):
                ktok[m, h] = kv_all[m, h].T

        @pl.when((m > 0) & (lax.rem(m, 2) == 0))
        def _():
            hand_on(m).start()

        for s in range(1, nz - 1):

            @pl.when(m == 2 * s)
            def _():
                w_line.start(s)

        @pl.when(m == GROUP_DEVS - 1)
        def _():
            w_line.last()
            w_plane.start()

        slot_step(m, 1)

    loop(0, GROUP_DEVS, tail_slot)

    def finish(half):
        cols = pl.ds(half * PB, PB)
        for head in range(heads):
            att[z, pl.ds(head * HEAD_DIM, HEAD_DIM), cols] = (
                acc[head, :, cols] / total[head, :, cols]
            ).astype(BF16)
            lse_ref[head, :, cols] = top[head, :, cols] + jnp.log2(total[head, :, cols])

    lines = [
        LineGather(
            nz,
            lambda index, half=half: att.at[index, :, pl.ds(half * PB, PB)],
            zs.at[half],
            zr.at[half],
        )
        for half in range(2)
    ]
    kv_out = pltpu.make_async_copy(kv_all, kv_hbm, leave.at[2])
    kv_out.start()

    def att_out(half):
        there = (slice(None), slice(None), pl.ds(half * PB, PB))
        return pltpu.make_async_copy(att.at[there], att_hbm.at[there], leave.at[half])

    finish(1)
    lines[1].start(0)
    slot_step(0, 0, mask=True)

    def prompt_slot(m):
        slot_step(m, 0, bias=bias_ref[m])

        @pl.when(m == 4)
        def _():
            w_plane.after_first()
            lines[1].start(1)

    loop(1, GROUP_DEVS, prompt_slot)
    finish(0)
    lines[0].start(0)
    w_plane.after_second()
    for s in range(2, nz - 1):
        lines[1].start(s)
    for s in range(1, nz - 1):
        lines[0].start(s)
    for half in (1, 0):
        lines[half].last()
        att_out(half).start()
    for line in lines + [w_line]:
        line.drain()
    w_plane.finish()
    for copy in firsts:
        copy.wait_send()
    for m in (2, 4, 6):
        hand_on(m).wait_send()
    kv_out.wait()
    for half in range(2):
        att_out(half).wait()


def forward_attention(nz, q, kv, w_out, bias):
    heads, tokens = q.shape[0], q.shape[2]
    kvh = heads // 2
    own, width = w_out.shape
    return pl.pallas_call(
        functools.partial(forward_kernel, nz),
        out_shape=(
            jax.ShapeDtypeStruct((nz, heads * HEAD_DIM, tokens), BF16),
            jax.ShapeDtypeStruct((GROUP_DEVS, 2 * kvh, HEAD_DIM, PB), BF16),
            jax.ShapeDtypeStruct((heads, 1, tokens), F32),
            jax.ShapeDtypeStruct((nz * own, width), BF16),
        ),
        in_specs=[
            pl.BlockSpec(memory_space=VM),
            pl.BlockSpec(memory_space=VM),
            pl.BlockSpec(memory_space=pl.ANY),
            pl.BlockSpec(memory_space=pltpu.SMEM),
        ],
        out_specs=(
            pl.BlockSpec(memory_space=pl.ANY),
            pl.BlockSpec(memory_space=pl.ANY),
            pl.BlockSpec(memory_space=VM),
            pl.BlockSpec(memory_space=pl.ANY),
        ),
        scratch_shapes=[
            VM((nz, heads * HEAD_DIM, tokens), BF16),
            VM((GROUP_DEVS, 2 * kvh, HEAD_DIM, PB), BF16),
            VM((heads, HEAD_DIM, tokens), F32),
            VM((heads, 1, tokens), F32),
            VM((heads, 1, tokens), F32),
            VM((GROUP_DEVS + 1, kvh, PB, HEAD_DIM), BF16),
            VM((nz * own // GROUP_DEVS, width), BF16),
            pltpu.SemaphoreType.DMA((GROUP_DEVS,)),
            pltpu.SemaphoreType.DMA((GROUP_DEVS,)),
            pltpu.SemaphoreType.DMA((2, 2, nz - 1)),
            pltpu.SemaphoreType.DMA((2, 2, nz - 1)),
            pltpu.SemaphoreType.DMA((2, nz - 1)),
            pltpu.SemaphoreType.DMA((2, nz - 1)),
            pltpu.SemaphoreType.DMA((2, 11)),
            pltpu.SemaphoreType.DMA((1,)),
            pltpu.SemaphoreType.DMA((3,)),
        ],
        compiler_params=pltpu.CompilerParams(
            collective_id=0, has_side_effects=True, vmem_limit_bytes=60 << 20
        ),
        cost_estimate=pl.CostEstimate(
            flops=40_000_000_000, bytes_accessed=12_000_000, transcendentals=19_000_000
        ),
        name="forward_attention",
    )(q, kv, w_out, bias)


class Stream:
    def __init__(self, rows, count, ins, out):
        self.rows, self.count, self.ins, self.out = rows, count, ins, out

    def load(self, i):
        slot = lax.rem(i, 2)
        return [
            pltpu.make_async_copy(src.at[self.rows(i)], buf.at[slot], sem.at[slot])
            for src, buf, sem in self.ins
        ]

    def store(self, i):
        dst, buf, sem = self.out
        slot = lax.rem(i, 2)
        return pltpu.make_async_copy(buf.at[slot], dst.at[self.rows(i)], sem.at[slot])

    def prime(self):
        for i in range(2):
            for copy in self.load(i):
                copy.start()

    def take(self, i):
        for copy in self.load(i):
            copy.wait()

        @pl.when(i >= 2)
        def _():
            self.store(i - 2).wait()

    def give(self, i):
        self.store(i).start()

        @pl.when(i + 2 < self.count)
        def _():
            for copy in self.load(i + 2):
                copy.start()

    def flush(self):
        for i in range(self.count - 2, self.count):
            self.store(i).wait()


def tail_kernel(
    nz, chunk, q_ref, kv_ref, do_ref, bias_ref, lse_ref, inner_ref, feed, cos_ref, sin_ref,
    gain_ref, gain_two, kv_all, mid_hbm, ffn_hbm, normed_hbm, x_hbm, ga_hbm, wq_hbm, wk_hbm, wv_hbm,
    gwo_hbm,
    act, gt, gains, summed, ffn_sum,
    kvs, wq, wk, wv, dq, dkv, near, far, ktok, vtok, low, total, held, f_piece, part, total_one, held_one, weights, a_near, a_far, a_last, a_piece, tile_in,
    mid_in, act_out, x_in, ga_in, gt_out, accum, box,
    ss, rr, fs, fr, ss1, rr1, fs1, fr1, ns, nr, ps, pr, a_sems, ag_sems, fg_sems, bs, br,
    loads, kv_sem, m_sem, act_sem, x_sem, g_sem, gt_sem,
):
    heads = q_ref.shape[0]
    kvh = heads // 2
    d, z = lax.axis_index("dp"), lax.axis_index("tensor")
    member = lax.rem(d, GROUP_DEVS)
    masks = range(1, GROUP_DEVS)
    nq = heads * HEAD_DIM
    nkv = kvh * HEAD_DIM
    tokens, width = feed.shape
    pairs = (
        (wq_hbm, wq),
        (wk_hbm, wk),
        (wv_hbm, wv),
        (gwo_hbm, weights.at[pl.ds(nq + 2 * nkv, gwo_hbm.shape[0])]),
    )
    fetches = [pltpu.make_async_copy(src, dst, loads.at[i]) for i, (src, dst) in enumerate(pairs)]

    def kv_load(t):
        slot = lax.rem(2 * t + 1 + t // 4, GROUP_DEVS)
        return pltpu.make_async_copy(
            kv_all.at[slot], kvs.at[lax.rem(t, 2)], kv_sem.at[lax.rem(t, 2)]
        )

    kv_load(0).start()
    first_piece = pltpu.make_async_copy(ffn_hbm, f_piece, loads.at[len(pairs)])
    first_piece.start()
    batch = 4
    line = Line(nz, chunk, feed, total, held, (ss, rr, fs, fr))
    line_one = Line(
        nz, chunk, part, total_one, held_one, (ss1, rr1, fs1, fr1), shift=tokens // chunk // 2
    )
    batches = line.count // batch
    acts = Stream(
        lambda i: line.batch(i, batch), batches, [(mid_hbm, mid_in, m_sem)], (act, act_out, act_sem)
    )
    outs = Stream(
        lambda i: line_one.batch(i, batch),
        batches,
        [(x_hbm, x_in, x_sem), (ga_hbm, ga_in, g_sem)],
        (gt, gt_out, gt_sem),
    )
    acts.prime()
    greet(neighbours(nz) + plane(masks))
    reduce_attn = PlaneReduce(
        weights,
        None,
        lambda i: a_near.at[i],
        lambda c, k: a_far.at[c, k],
        lambda c: a_last.at[c],
        a_sems,
    )
    gather_attn = PlaneGather(a_piece, summed, ag_sems)
    gather_ffn = PlaneGather(f_piece, ffn_sum, fg_sems)
    loop(0, line.count, line.issue)
    first_piece.wait()
    gather_ffn.start()
    for copy in fetches:
        copy.start()
    lag = 12
    ply = 2

    def ripple(s):
        @pl.when(s < line.count)
        def _():
            line.service(s)

        @pl.when(s >= lag)
        def _():
            line.ready(s - lag)

        @pl.when((s >= lag) & (lax.rem(s - lag, batch) == batch - 1))
        def _():
            i = (s - lag) // batch
            acts.take(i)
            act_out[lax.rem(i, 2)] = (
                mid_in[lax.rem(i, 2)].astype(F32) + total[line.batch(i, batch)].astype(F32)
            ).astype(BF16)
            acts.give(i)

    def background(s):
        @pl.when(s == 8)
        def _():
            gather_ffn.after_first()

        @pl.when(s == 22)
        def _():
            gather_ffn.after_second()

        loop(s * ply, s * ply + ply, ripple)

    dq[...] = jnp.zeros_like(dq)

    def block(head, half, keyt, mask, bias):
        h = head // 2
        cols = pl.ds(half * PB, PB)
        s = dot(ktok[h], q_ref[head, :, cols])
        if mask:
            s = causal(s)
        shift = lse_ref[head, :, cols]
        if bias is not None:
            shift = shift - bias
        p = jnp.exp2(s - shift)
        dp = dot(vtok[h], do_ref[head, :, cols])
        ds = (p * (dp - inner_ref[head, :, cols])).astype(BF16)
        dq[head, :, cols] += dot(keyt, ds)
        dv = dot_nt(do_ref[head, :, cols], p.astype(BF16))
        dk = dot_nt(q_ref[head, :, cols], ds)
        return dk, dv

    def total_of(parts):
        out = parts[0]
        for piece in parts[1:]:
            out = out + piece
        return out

    def turn_back(u, half):
        cols = pl.ds(half * PB, PB)
        cosine, sine = cos_ref[:, cols], sin_ref[:, cols]
        lower, upper = u[: HEAD_DIM // 2], u[HEAD_DIM // 2 :]
        return lower * cosine + upper * sine, upper * cosine - lower * sine

    def put_low(row, half, u, turned):
        cols = pl.ds(half * PB, PB)
        if not turned:
            low[pl.ds(row, HEAD_DIM), cols] = u.astype(BF16)
            return
        first, second = turn_back(u, half)
        low[pl.ds(row, HEAD_DIM // 2), cols] = first.astype(BF16)
        low[pl.ds(row + HEAD_DIM // 2, HEAD_DIM // 2), cols] = second.astype(BF16)

    for h in range(kvh):
        ktok[h] = kv_ref[h, :, PB : PB + CL].T
        vtok[h] = kv_ref[kvh + h, :, PB : PB + CL].T
    for h in range(kvh):
        both = [block(2 * h + r, 1, kv_ref[h, :, PB : PB + CL], True, None) for r in range(2)]
        put_low(nq + h * HEAD_DIM, 1, total_of([b[0] for b in both]) * (1.0 / LOG2E), True)
        put_low(nq + nkv + h * HEAD_DIM, 1, total_of([b[1] for b in both]), False)

    quarter = GROUP_DEVS // 2

    def slot_step(t, where, first):
        kv_load(t).wait()
        now = lax.rem(t, 2)
        for h in range(kvh):
            ktok[h] = kvs[now, h].T
            vtok[h] = kvs[now, kvh + h].T
        bias = None if first else bias_ref[lax.rem(2 * t + 1 + t // 4, GROUP_DEVS)]
        for h in range(kvh):
            both = []
            for r in range(2):
                background(t * 4 + h * 2 + r)
                both.append(block(2 * h + r, 1, kvs[now, h], False, None))
                both.append(block(2 * h + r, 0, kvs[now, h], first, bias))
            dkv[where, h] = (total_of([b[0] for b in both]) * (1.0 / LOG2E)).astype(BF16)
            dkv[where, kvh + h] = total_of([b[1] for b in both]).astype(BF16)

    def to_near(i):
        return remote(dkv.at[i], near.at[i], ns.at[i], nr.at[i], plane((1,))[0])

    def to_far(i):
        return remote(near.at[i], far.at[i], ps.at[i], pr.at[i], (jnp.bitwise_xor(d, 2 * i), z))

    def step(t):
        kv_load(t + 1).start()
        slot_step(t, t - t // quarter * (t - quarter), False)

        @pl.when(t < quarter)
        def _():
            to_near(t).start()

        @pl.when(t >= quarter)
        def _():
            i = t - quarter + 1
            to_near(i).wait_recv()
            near[i] = (dkv[quarter].astype(F32) + near[i].astype(F32)).astype(BF16)
            to_far(i).start()

    last = GROUP_DEVS - 1
    loop(0, last, step)
    slot_step(last, quarter, True)

    def back(j):
        group = tokens // 4
        rows = pl.ds(pl.multiple_of(j * group, group), group)
        a = [low[pl.ds(at, n), rows].T for at, n in ((0, nq), (nq, nkv), (nq + nkv, nkv))]
        size = 512
        for t in range(width // size):
            cols = pl.ds(t * size, size)
            part[rows, cols] = (
                dot_nt(a[0], wq[cols]) + dot(a[1], wk[:, cols]) + dot(a[2], wv[:, cols])
            ).astype(BF16)

    for copy in fetches:
        copy.wait()
    done = 4 * GROUP_DEVS * ply
    left = line.count + lag - done
    share = left // 4
    half_count = line.count // 2
    for head in range(heads):
        put_low(head * HEAD_DIM, 1, dq[head, :, PB : PB + CL] * HEAD_DIM ** (-0.5), True)
    loop(2, 4, back)
    loop(0, half_count, line_one.issue)
    loop(done, done + share, ripple)
    for head in range(heads):
        put_low(head * HEAD_DIM, 0, dq[head, :, 0:PB] * HEAD_DIM ** (-0.5), True)
    to_near(0).wait_recv()
    for i in range(1, quarter):
        to_far(i).wait_recv()
    for h in range(2 * kvh):
        home = dkv[quarter, h].astype(F32)
        home = home + near[0, h].astype(F32)
        for i in range(1, quarter):
            home = home + far[i, h].astype(F32)
        put_low(nq + h * HEAD_DIM, 0, home, h < kvh)
    loop(0, 2, back)
    loop(half_count, line.count, line_one.issue)
    loop(done + share, done + 2 * share, ripple)
    outs.prime()
    size = tile_in.shape[1]

    def tile_load(t):
        return pltpu.make_async_copy(
            normed_hbm.at[:, pl.ds(t * size, size)], tile_in, loads.at[len(pairs)]
        )

    def tile_step(t):
        tile_load(t).wait()
        weights[0 : nq + 2 * nkv, pl.ds(t * size, size)] = dot(low[...], tile_in[...]).astype(BF16)
        if t + 1 < width // size:
            tile_load(t + 1).start()

    tile_load(0).start()
    loop(done + 2 * share, done + left, ripple)
    acts.flush()
    accum[...] = jnp.zeros_like(accum)
    gain = gain_ref[...]
    lag_one = 10

    def body(s):
        @pl.when(s < line_one.count)
        def _():
            line_one.service(s)

        @pl.when(s >= lag_one)
        def _():
            line_one.ready(s - lag_one)

        @pl.when((s >= lag_one) & (lax.rem(s - lag_one, batch) == batch - 1))
        def _():
            i = (s - lag_one) // batch
            outs.take(i)
            slot = lax.rem(i, 2)
            x = x_in[slot].astype(F32)
            inverse = lax.rsqrt(jnp.mean(x * x, axis=-1, keepdims=True) + EPSILON)
            upstream = total_one[line_one.batch(i, batch)].astype(F32)
            inner = upstream * gain
            through = inverse * inner - x * inverse**3 * jnp.mean(
                inner * x, axis=-1, keepdims=True
            )
            gt_out[slot] = (ga_in[slot].astype(F32) + through).astype(BF16)
            accum[...] += fold_rows(upstream * x * inverse)
            outs.give(i)

        for t in range(width // size):

            @pl.when(s == 4 + 5 * t)
            def _():
                tile_step(t)

        @pl.when(s == 15)
        def _():
            reduce_attn.start()

        @pl.when(s == 19)
        def _():
            reduce_attn.after_core()

        @pl.when(s == 31)
        def _():
            reduce_attn.after_first()

        @pl.when(s == 39)
        def _():
            reduce_attn.result(a_piece)
            gather_attn.start()

        @pl.when(s == 46)
        def _():
            gather_attn.after_first()

        @pl.when(s == 58)
        def _():
            gather_attn.after_second()

    loop(0, line_one.count + lag_one, body)
    box[member, 0:1] = jnp.sum(accum[...], axis=0, keepdims=True)
    box[member, 1:2] = gain_two[...]
    copies = [
        remote(box.at[member], box.at[member], bs.at[m], br.at[m], target)
        for m, target in zip(masks, plane(masks))
    ]
    for copy in copies:
        copy.start()
    outs.flush()
    for i in range(quarter):
        to_near(i).wait_send()
    for i in range(1, quarter):
        to_far(i).wait_send()
    line.drain()
    line_one.drain()
    reduce_attn.finish()
    gather_ffn.finish()
    gather_attn.finish()
    for copy in copies:
        copy.wait()
    result = box[0]
    for m in masks:
        result = result + box[m]
    gains[...] = result


def tail_stage(
    nz, q, kv, do, bias, lse, inner, feed, cosine, sine, gain, gain_two, kv_all, middle, ffn, normed,
    x, ga, w_query, w_key, w_value, grad_w_out, chunk=16,
):
    heads = q.shape[0]
    kvh = heads // 2
    tokens, width = feed.shape
    slot = (2 * kvh, HEAD_DIM, PB)
    n_attn = (heads + 2 * kvh) * HEAD_DIM + grad_w_out.shape[0]
    high, wide = ffn.shape
    low_high = n_attn // GROUP_DEVS
    count = tokens // chunk
    rows = 4 * chunk
    quarter = GROUP_DEVS // 2
    dma = lambda *shape: pltpu.SemaphoreType.DMA(shape)
    lines = [dma(2, count)] * 3 + [dma(count)]
    block = VM((2, rows, width), BF16)
    anywhere = pl.BlockSpec(memory_space=pl.ANY)
    vmem = pl.BlockSpec(memory_space=VM)
    return pl.pallas_call(
        functools.partial(tail_kernel, nz, chunk),
        out_shape=(
            jax.ShapeDtypeStruct(feed.shape, BF16),
            jax.ShapeDtypeStruct(feed.shape, BF16),
            jax.ShapeDtypeStruct((2, width), F32),
            jax.ShapeDtypeStruct((n_attn, width), BF16),
            jax.ShapeDtypeStruct((high * GROUP_DEVS, wide), BF16),
        ),
        in_specs=[vmem] * 3 + [pl.BlockSpec(memory_space=pltpu.SMEM)] + [vmem] * 7 + [anywhere] * 10,
        out_specs=(anywhere, anywhere, vmem, anywhere, anywhere),
        scratch_shapes=[
            VM((2,) + slot, BF16),
            VM(w_query.shape, BF16),
            VM(w_key.shape, BF16),
            VM(w_value.shape, BF16),
            VM((heads, HEAD_DIM, tokens), F32),
            VM((quarter + 1,) + slot, BF16),
            VM((quarter,) + slot, BF16),
            VM((quarter,) + slot, BF16),
            VM((kvh, PB, HEAD_DIM), BF16),
            VM((kvh, PB, HEAD_DIM), BF16),
            VM(((heads + 2 * kvh) * HEAD_DIM, tokens), BF16),
            VM(feed.shape, BF16),
            VM(feed.shape, BF16),
            VM((high, wide), BF16),
            VM(feed.shape, BF16),
            VM(feed.shape, BF16),
            VM(feed.shape, BF16),
            VM((n_attn, width), BF16),
            VM((4, low_high, width), BF16),
            VM((2, 2, low_high, width // 2), BF16),
            VM((2, low_high, width // 2), BF16),
            VM((low_high, width), BF16),
            VM((tokens, 512), BF16),
            block,
            block,
            block,
            block,
            block,
            VM((8, width), F32),
            VM((GROUP_DEVS, 2, width), F32),
        ]
        + lines * 2
        + [dma(quarter)] * 4
        + [dma(2, 11)] * 3
        + [dma(GROUP_DEVS)] * 2
        + [dma(5)]
        + [dma(2)] * 6,
        compiler_params=pltpu.CompilerParams(
            collective_id=1, has_side_effects=True, vmem_limit_bytes=60 << 20
        ),
        cost_estimate=pl.CostEstimate(
            flops=200_000_000_000, bytes_accessed=50_000_000, transcendentals=19_000_000
        ),
        name="tail_stage",
    )(
        q, kv, do, bias, lse, inner, feed, cosine, sine, gain, gain_two, kv_all, middle, ffn, normed,
        x, ga, w_query, w_key, w_value, grad_w_out,
    )


def middle_kernel(
    nz, chunk, att_hbm, wo_hbm, x_hbm, wg_hbm, wu_hbm, wd_hbm, cot_hbm, gain_ref,
    gatt, inner_out, gwo, gain_two, ga_hbm, mid_hbm, feed_hbm, gffn, piece,
    ga, mid, feed, att, wo, wg, wu, wd, cot, mid32, nt2, hidden, gg, gu, part, total, accum, stage,
    load, store, leave, r_sems, spent, held, ss, rr, fs, fr,
):
    z = lax.axis_index("tensor")
    group, slab = 256, 256
    tokens, width = mid.shape
    head, rest = pl.ds(0, group), pl.ds(group, tokens - group)
    pairs = (
        (x_hbm.at[head], mid.at[head]),
        (att_hbm.at[:, head], att.at[:, head]),
        (wg_hbm, wg),
        (wu_hbm, wu),
        (cot_hbm, cot),
        (wd_hbm, wd),
        (x_hbm.at[rest], mid.at[rest]),
        (att_hbm.at[:, rest], att.at[:, rest]),
    )
    loads = [pltpu.make_async_copy(src, dst, load.at[i]) for i, (src, dst) in enumerate(pairs)]
    own = gatt.shape[0]
    some = own // GROUP_DEVS

    def wo_rows(i):
        src = pl.ds(pl.multiple_of(i * some, 16), some)
        dst = pl.ds(pl.multiple_of(lax.rem(i, nz) * own + i // nz * some, 16), some)
        pltpu.make_async_copy(wo_hbm.at[src], wo.at[dst], load.at[len(pairs)]).start()

    for copy in loads[:2]:
        copy.start()
    loop(0, nz * GROUP_DEVS, wo_rows)
    for copy in loads[2:]:
        copy.start()
    greet(neighbours(nz) + plane((1, 2, 4)))
    ff = wg.shape[1]
    heads = own // HEAD_DIM
    per = group // chunk
    ply = 4
    quarters = per // ply
    tile = 512
    gain = gain_ref[...]
    accum[...] = jnp.zeros_like(accum)
    line = Line(nz, chunk, part, total, held, (ss, rr, fs, fr))
    mine = pl.ds(pl.multiple_of(z * own, own), own)
    lag = 12

    def out_of(n, g):
        src, dst = ((mid, mid_hbm), (feed, feed_hbm), (ga, ga_hbm))[n]
        rows = pl.ds(pl.multiple_of(g * group, group), group)
        return pltpu.make_async_copy(src.at[rows], dst.at[rows], leave.at[n, g])

    def settle(c):
        rows = line.batch(c, ply)
        m = mid[rows].astype(F32)
        inverse = lax.rsqrt(jnp.mean(m * m, axis=-1, keepdims=True) + EPSILON)
        upstream = total[rows].astype(F32)
        inner = upstream * gain
        through = inverse * inner - m * inverse**3 * jnp.mean(inner * m, axis=-1, keepdims=True)
        ga[rows] = (cot[rows].astype(F32) + through).astype(BF16)
        accum[...] += fold_rows(upstream * m * inverse)

        @pl.when(lax.rem(c, quarters) == quarters - 1)
        def _():
            out_of(2, c // quarters).start()
            block = pl.ds(pl.multiple_of((c // quarters) * group, group), group)
            back = dot_nt(wo[mine], ga[block])
            gatt[:, block] = back.astype(BF16)
            for head in range(heads):
                some = pl.ds(head * HEAD_DIM, HEAD_DIM)
                there = att[pl.ds(pl.multiple_of(z * own + head * HEAD_DIM, 32), HEAD_DIM), block]
                inner_out[head, :, block] = jnp.sum(
                    gatt[some, block].astype(F32) * there.astype(F32), axis=0, keepdims=True
                )

    def ripple(s):
        @pl.when(s < line.count)
        def _():
            line.service(s)

        @pl.when(s >= lag)
        def _():
            line.ready(s - lag)

        @pl.when((s >= lag) & (lax.rem(s - lag, ply) == ply - 1))
        def _():
            settle((s - lag) // ply)

    def tick(s):
        @pl.when(s >= 0)
        def _():
            loop(s * ply, s * ply + ply, ripple)

    for copy in loads[:2]:
        copy.wait()
    pltpu.make_async_copy(wo_hbm, wo, load.at[len(pairs)]).wait()

    def forward(j):
        @pl.when(j == 1)
        def _():
            for copy in loads[6:]:
                copy.wait()

        rows = pl.ds(pl.multiple_of(j * group, group), group)
        a = att[:, rows].T
        for t in range(width // tile):
            cols = pl.ds(t * tile, tile)
            mid32[:, cols] = mid[rows, cols].astype(F32) + dot(a, wo[:, cols])
        m = mid32[...]
        mid[rows] = m.astype(BF16)
        inverse = lax.rsqrt(jnp.mean(m * m, axis=-1, keepdims=True) + EPSILON)
        nt2[rows] = (m * inverse * gain).astype(BF16)

        @pl.when(j == 0)
        def _():
            for copy in loads[2:6]:
                copy.wait()

        tick(2 * j - 3)
        for t in range(ff // tile):
            cols = pl.ds(t * tile, tile)
            gate = dot(nt2[rows], wg[:, cols])
            up = dot(nt2[rows], wu[:, cols])
            back = dot_nt(cot[rows], wd[cols])
            sig = jax.nn.sigmoid(gate)
            silu = gate * sig
            hidden[rows, cols] = (silu * up).astype(BF16)
            gu[rows, cols] = (back * silu).astype(BF16)
            gg[rows, cols] = (back * up * (sig * (1.0 + gate * (1.0 - sig)))).astype(BF16)
        for t in range(width // tile):
            cols = pl.ds(t * tile, tile)
            part[rows, cols] = (dot_nt(gg[rows], wg[cols]) + dot_nt(gu[rows], wu[cols])).astype(BF16)
        loop(j * per, j * per + per, line.issue)
        for t in range(width // tile):
            cols = pl.ds(t * tile, tile)
            feed[rows, cols] = dot(hidden[rows], wd[:, cols]).astype(BF16)
        out_of(0, j).start()
        out_of(1, j).start()
        tick(2 * j - 2)

    steps = tokens // group
    loop(0, steps, forward)
    for target in plane((1, 2, 4)):
        pl.semaphore_signal(spent, inc=1, device_id=target, device_id_type=MESH)
    high, half = width // GROUP_DEVS, ff // 2

    def rows_of(n):
        return pl.ds(pl.multiple_of(n * high, 16), high)

    def reduce_of(q):
        src = gffn.at[:, pl.ds(q * ff, ff)]
        own = stage.at[0, pl.ds(0, high), pl.ds(q * ff, ff)]
        sems = r_sems.at[q]
        if q < 2:
            room = (wg, wu)[q]
            return PlaneReduce(
                src,
                own,
                lambda i: room.at[rows_of(i)],
                lambda c, n: room.at[rows_of(4 + n), pl.ds(c * half, half)],
                lambda c: room.at[rows_of(6), pl.ds(c * half, half)],
                sems,
            )
        return PlaneReduce(
            src,
            own,
            lambda i: wd.at[rows_of(i), pl.ds(0, ff)],
            lambda c, n: wd.at[rows_of(2 * c + n), pl.ds(ff, half)],
            lambda c: wd.at[rows_of(4), pl.ds(c * half, half)],
            sems,
        )

    reduces = [reduce_of(q) for q in range(3)]
    done = 2 * steps - 3
    slabs = width // slab

    def put(t):
        return pltpu.make_async_copy(
            stage.at[lax.rem(t, 2)],
            gffn.at[pl.ds(pl.multiple_of(t * slab, slab), slab)],
            store.at[lax.rem(t, 2)],
        )

    def weights(t):
        @pl.when(t >= 2)
        def _():
            put(t - 2).wait()

        slot = lax.rem(t, 2)
        cols = pl.ds(pl.multiple_of(t * slab, slab), slab)
        a = nt2[:, cols].T
        stage[slot, :, 0:ff] = dot(a, gg[...]).astype(BF16)
        stage[slot, :, ff : 2 * ff] = dot(a, gu[...]).astype(BF16)
        stage[slot, :, 2 * ff : 3 * ff] = dot(cot[:, cols].T, hidden[...]).astype(BF16)
        put(t).start()

        @pl.when(lax.rem(t, 2) == 1)
        def _():
            tick(done + t // 2)

    loop(0, slabs, weights)
    for t in (slabs - 2, slabs - 1):
        put(t).wait()
    pl.semaphore_wait(spent, 3)
    for reduce in reduces:
        reduce.start()
    begin, end = (done + slabs // 2) * ply, line.count + lag
    marks = (begin, begin + 9, begin + 32, end)
    loop(marks[0], marks[1], ripple)
    for reduce in reduces:
        reduce.after_core()
    loop(marks[1], marks[2], ripple)
    for reduce in reduces:
        reduce.after_first()
    loop(marks[2], marks[3], ripple)
    for t in range(width // tile):
        cols = pl.ds(t * tile, tile)
        gwo[:, cols] = dot(att[mine], ga[:, cols]).astype(BF16)
    gain_two[...] = jnp.sum(accum[...], axis=0, keepdims=True)
    for q in range(3):
        reduces[q].result(stage.at[1, pl.ds(0, high), pl.ds(q * ff, ff)])
    out = pltpu.make_async_copy(stage.at[1, pl.ds(0, high)], piece, store.at[0])
    out.start()
    for reduce in reduces:
        reduce.finish()
    line.drain()
    out.wait()
    for n in range(3):
        loop(0, steps, lambda g, n=n: out_of(n, g).wait())


def middle_stage(nz, att_all, w_out_all, x, w_gate, w_up, w_down, cot, gain, chunk=16):
    tokens, width = x.shape
    ff = w_gate.shape[1]
    own = w_out_all.shape[0] // nz
    heads = own // HEAD_DIM
    group, slab = 256, 256
    wide = jax.ShapeDtypeStruct((tokens, width), BF16)
    return pl.pallas_call(
        functools.partial(middle_kernel, nz, chunk),
        out_shape=(
            jax.ShapeDtypeStruct((own, tokens), BF16),
            jax.ShapeDtypeStruct((heads, 1, tokens), F32),
            jax.ShapeDtypeStruct((own, width), BF16),
            jax.ShapeDtypeStruct((1, width), F32),
            wide,
            wide,
            wide,
            jax.ShapeDtypeStruct((width, 3 * ff), BF16),
            jax.ShapeDtypeStruct((width // GROUP_DEVS, 3 * ff), BF16),
        ),
        in_specs=[pl.BlockSpec(memory_space=pl.ANY)] * 7 + [pl.BlockSpec(memory_space=VM)],
        out_specs=(pl.BlockSpec(memory_space=VM),) * 4 + (pl.BlockSpec(memory_space=pl.ANY),) * 5,
        scratch_shapes=[
            VM((tokens, width), BF16),
            VM((tokens, width), BF16),
            VM((tokens, width), BF16),
            VM(w_out_all.shape[:1] + (tokens,), BF16),
            VM(w_out_all.shape, BF16),
            VM((width, ff), BF16),
            VM((width, ff), BF16),
            VM((ff, width), BF16),
            VM((tokens, width), BF16),
            VM((group, width), F32),
            VM((tokens, width), BF16),
            VM((tokens, ff), BF16),
            VM((tokens, ff), BF16),
            VM((tokens, ff), BF16),
            VM((tokens, width), BF16),
            VM((tokens, width), BF16),
            VM((8, width), F32),
            VM((2, slab, 3 * ff), BF16),
            pltpu.SemaphoreType.DMA((9,)),
            pltpu.SemaphoreType.DMA((2,)),
            pltpu.SemaphoreType.DMA((3, tokens // group)),
            pltpu.SemaphoreType.DMA((3, 2, 11)),
            pltpu.SemaphoreType.REGULAR,
        ]
        + line_scratch((tokens, width), chunk),
        compiler_params=pltpu.CompilerParams(
            collective_id=2, has_side_effects=True, vmem_limit_bytes=60 << 20
        ),
        cost_estimate=pl.CostEstimate(
            flops=100_000_000_000, bytes_accessed=50_000_000, transcendentals=1_000_000
        ),
        name="middle_stage",
    )(att_all, w_out_all, x, w_gate, w_up, w_down, cot, gain)


def finish_kernel(nq, nk, ffn, attn, gt, act, gate, up, down, q, k, v, o, gt_out, act_out):
    ff = gate.shape[1]
    gate[...] = ffn[:, 0:ff].astype(F32)
    up[...] = ffn[:, ff : 2 * ff].astype(F32)
    down[...] = ffn[:, 2 * ff : 3 * ff].astype(F32).T
    q[...] = attn[0:nq].astype(F32).T
    k[...] = attn[nq : nq + nk].astype(F32)
    v[...] = attn[nq + nk : nq + 2 * nk].astype(F32)
    o[...] = attn[nq + 2 * nk :].astype(F32)
    gt_out[...] = gt[...]
    act_out[...] = act[...]


def finish(ffn, attn, gt, act, nq, nk):
    width, ff = ffn.shape[0], ffn.shape[1] // 3
    tokens, own = gt.shape[0], attn.shape[0] - nq - 2 * nk
    tile = 256
    wide = lambda *shape: jax.ShapeDtypeStruct(shape, F32)
    down = lambda rows: pl.BlockSpec((tile, rows), lambda i: (i, 0))
    side = lambda rows: pl.BlockSpec((rows, tile), lambda i: (0, i))
    return pl.pallas_call(
        functools.partial(finish_kernel, nq, nk),
        grid=(width // tile,),
        out_shape=(
            wide(width, ff),
            wide(width, ff),
            wide(ff, width),
            wide(width, nq),
            wide(nk, width),
            wide(nk, width),
            wide(own, width),
            jax.ShapeDtypeStruct(gt.shape, gt.dtype),
            jax.ShapeDtypeStruct(act.shape, act.dtype),
        ),
        in_specs=[down(3 * ff), side(attn.shape[0]), side(tokens), side(tokens)],
        out_specs=(
            down(ff),
            down(ff),
            side(ff),
            down(nq),
            side(nk),
            side(nk),
            side(own),
            side(tokens),
            side(tokens),
        ),
        compiler_params=pltpu.CompilerParams(vmem_limit_bytes=60 << 20),
        name="finish",
    )(ffn, attn, gt, act)


def rms_inverse(inputs):
    return lax.rsqrt(jnp.mean(inputs * inputs, axis=-1, keepdims=True) + EPSILON)


def rotate(u, cosine, sine):
    half = HEAD_DIM // 2
    lower, upper = u[:, :half], u[:, half:]
    return jnp.concatenate(
        [lower * cosine - upper * sine, upper * cosine + lower * sine], axis=1
    )


def shards(
    nz,
    tokens,
    block_order,
    attn_gain,
    w_query,
    w_key,
    w_value,
    w_out,
    mlp_gain,
    w_gate,
    w_up,
    w_down,
    cotangent,
):
    device = lax.axis_index("dp")
    n_dp = lax.axis_size("dp")
    member = device % GROUP_DEVS
    order_row = lax.dynamic_index_in_dim(block_order, device // GROUP_DEVS, 0, keepdims=False)
    by_slot = order_row[jnp.bitwise_xor(jnp.arange(GROUP_DEVS), member)]
    own_block = by_slot[0]
    bias = jnp.where(by_slot <= own_block, 0.0, NEG).astype(F32)
    offsets = jnp.arange(PB, dtype=jnp.int32)
    places = jnp.concatenate([own_block * PB + offsets, GROUP_DEVS * PB + offsets])
    halfway = HEAD_DIM // 2
    frequency = ROTARY_BASE ** (-(jnp.arange(halfway, dtype=F32) * 2.0) / HEAD_DIM)
    angle = frequency[:, None] * places.astype(F32)[None, :]
    cosine, sine = jnp.cos(angle)[None], jnp.sin(angle)[None]

    count = tokens.shape[0]
    factor = HEAD_DIM ** (-0.5)
    inputs = tokens.astype(F32)
    inverse_one = rms_inverse(inputs)
    normed = (inputs * inverse_one * attn_gain).astype(BF16)

    def project(weight):
        out = lax.dot_general(
            weight, normed, (((0,), (1,)), ((), ())), preferred_element_type=F32
        )
        return out.reshape(-1, HEAD_DIM, count)

    queries = (rotate(project(w_query), cosine, sine) * (factor * LOG2E)).astype(BF16)
    keys = rotate(project(w_key), cosine, sine).astype(BF16)
    values = project(w_value).astype(BF16)
    kv = jnp.concatenate([keys, values], axis=0)
    heads, kvh = queries.shape[0], keys.shape[0]

    att_all, kv_all, lse, w_out_all = forward_attention(nz, queries, kv, w_out, bias)
    grad_attended, row_inner, grad_w_out, grad_gain_two, grad_attention, middle, feed_part, _, ffn_piece = (
        middle_stage(
            nz,
            att_all.reshape(-1, count),
            w_out_all,
            tokens,
            w_gate,
            w_up,
            w_down,
            cotangent,
            mlp_gain[None],
        )
    )
    activations, grad_tokens, gains, grad_attn, grad_ffn = tail_stage(
        nz,
        queries,
        kv,
        grad_attended.reshape(heads, HEAD_DIM, count),
        bias,
        lse,
        row_inner,
        feed_part,
        cosine[0],
        sine[0],
        attn_gain[None],
        grad_gain_two,
        kv_all,
        middle,
        ffn_piece,
        normed,
        tokens,
        grad_attention,
        w_query,
        w_key.T,
        w_value.T,
        grad_w_out,
    )
    if n_dp > GROUP_DEVS:
        gains = lax.psum(gains, "dp") * (1.0 / GROUP_DEVS)
        grad_attn = lax.psum(grad_attn.astype(F32), "dp") * (1.0 / GROUP_DEVS)
        grad_ffn = lax.psum(grad_ffn.astype(F32), "dp") * (1.0 / GROUP_DEVS)
    nq, nk = w_query.shape[1], w_key.shape[1]

    gate, up, down, query, key, value, out, grad_tokens, activations = finish(
        grad_ffn, grad_attn, grad_tokens, activations, nq, nk
    )
    return (
        activations,
        grad_tokens,
        gains[0],
        query,
        key.T,
        value.T,
        out,
        gains[1],
        gate,
        up,
        down,
    )


def solution(mesh):
    in_specs = (
        P("dp", None),
        P(),
        P(),
        P(None, "tensor"),
        P(None, "tensor"),
        P(None, "tensor"),
        P("tensor", None),
        P(),
        P(None, "tensor"),
        P(None, "tensor"),
        P("tensor", None),
        P("dp", None),
    )
    out_specs = (
        P("dp", None),
        P("dp", None),
        P(),
        P(None, "tensor"),
        P(None, "tensor"),
        P(None, "tensor"),
        P("tensor", None),
        P(),
        P(None, "tensor"),
        P(None, "tensor"),
        P("tensor", None),
    )
    return jax.shard_map(
        functools.partial(shards, mesh.shape["tensor"]),
        mesh=mesh,
        in_specs=in_specs,
        out_specs=out_specs,
        check_vma=False,
    )
```

```python
import functools

import jax
import jax.numpy as jnp
from jax import lax
from jax.experimental import pallas as pl
from jax.experimental.pallas import tpu as pltpu
from jax.sharding import PartitionSpec as P

HEAD_DIM = 96
GROUP_DEVS = 8
PB = 512
CL = 512
EPSILON = 1e-05
ROTARY_BASE = 100000.0
LOG2E = 1.4426950408889634
NEG = -1e30
MESH = pl.DeviceIdType.MESH
VM = pltpu.VMEM
F32 = jnp.float32
BF16 = jnp.bfloat16
NT = (((1,), (1,)), ((), ()))


def dot(a, b):
    return jnp.dot(a, b, preferred_element_type=F32)


def dot_nt(a, b):
    return lax.dot_general(a, b, NT, preferred_element_type=F32)


def dot_tn(a, b):
    return lax.dot_general(a, b, (((0,), (0,)), ((), ())), preferred_element_type=F32)


def causal(s):
    key = lax.broadcasted_iota(jnp.int32, s.shape, 0)
    query = lax.broadcasted_iota(jnp.int32, s.shape, 1)
    return jnp.where(key <= query, s, NEG)


def greet(targets):
    barrier = pltpu.get_barrier_semaphore()
    for target in targets:
        pl.semaphore_signal(barrier, inc=1, device_id=target, device_id_type=MESH)
    pl.semaphore_wait(barrier, len(targets))


def remote(src, dst, send, recv, target):
    return pltpu.make_async_remote_copy(
        src_ref=src, dst_ref=dst, send_sem=send, recv_sem=recv, device_id=target, device_id_type=MESH
    )


class Line:
    def __init__(self, nz, chunk, part, out, held, sems, shift=0):
        self.d, self.z = lax.axis_index("dp"), lax.axis_index("tensor")
        self.shift = shift
        self.chunk, self.part, self.out, self.held = chunk, part, out, held
        self.ss, self.rr, self.fs, self.fr = sems
        self.count = part.shape[0] // chunk
        self.root, self.last = nz // 2 - 1, nz - 1

    def rows(self, c):
        if self.shift:
            c = lax.rem(c + self.shift, self.count)
        return pl.ds(pl.multiple_of(c * self.chunk, self.chunk), self.chunk)

    def batch(self, i, n):
        if self.shift:
            i = lax.rem(i + self.shift // n, self.count // n)
        return pl.ds(pl.multiple_of(i * self.chunk * n, self.chunk * n), self.chunk * n)

    def toward(self, c, side, src):
        rows = self.rows(c)
        target = self.z + 1 if side == 0 else self.z - 1
        return remote(
            src.at[rows],
            (self.out if side == 0 else self.held).at[rows],
            self.ss.at[side, c],
            self.rr.at[side, c],
            (self.d, target),
        )

    def final(self, c, side):
        rows = self.rows(c)
        target = self.z - 1 if side == 0 else self.z + 1
        return remote(
            self.out.at[rows], self.out.at[rows], self.fs.at[side, c], self.fr.at[c], (self.d, target)
        )

    def mine(self, c, side):
        rows = self.rows(c)
        arrived = (self.out if side == 0 else self.held)[rows]
        return arrived.astype(F32) + self.part[rows].astype(F32)

    def issue(self, c):
        @pl.when(self.z == 0)
        def _():
            self.toward(c, 0, self.part).start()

        @pl.when(self.z == self.last)
        def _():
            self.toward(c, 1, self.part).start()

    def service(self, c):
        @pl.when((self.z > self.root) & (self.z < self.last))
        def _():
            rows = self.rows(c)
            self.toward(c, 1, self.held).wait_recv()
            self.held[rows] = self.mine(c, 1).astype(BF16)
            self.toward(c, 1, self.held).start()

    def ready(self, c):
        @pl.when(self.z != self.root)
        def _():
            self.final(c, 1).wait_recv()

        @pl.when((self.z > self.root) & (self.z < self.last))
        def _():
            self.final(c, 1).start()

        @pl.when(self.z == self.root)
        def _():
            rows = self.rows(c)
            self.toward(c, 0, self.out).wait_recv()
            self.toward(c, 1, self.held).wait_recv()
            self.out[rows] = (self.mine(c, 0) + self.held[rows].astype(F32)).astype(BF16)
            self.final(c, 0).start()
            self.final(c, 1).start()

    def drain(self):
        def body(c, carry):
            @pl.when(self.z < self.root + 1)
            def _():
                @pl.when(self.z == 0)
                def _():
                    self.toward(c, 0, self.part).wait_send()

                @pl.when(self.z == self.root)
                def _():
                    self.final(c, 0).wait_send()
                    self.final(c, 1).wait_send()

            @pl.when(self.z > self.root)
            def _():
                self.toward(c, 1, self.part).wait_send()

                @pl.when(self.z < self.last)
                def _():
                    self.final(c, 1).wait_send()

            return carry

        lax.fori_loop(0, self.count, body, 0)


def line_scratch(shape, chunk):
    count = shape[0] // chunk
    return [VM(shape, BF16)] + [pltpu.SemaphoreType.DMA((2, count))] * 3 + [
        pltpu.SemaphoreType.DMA((count,))
    ]


def neighbours(nz):
    d, z = lax.axis_index("dp"), lax.axis_index("tensor")
    return [(d, lax.rem(z + 1, nz)), (d, lax.rem(z + nz - 1, nz))]


def plane(masks):
    d, z = lax.axis_index("dp"), lax.axis_index("tensor")
    return [(jnp.bitwise_xor(d, m), z) for m in masks]


def loop(start, stop, body):
    def step(i, carry):
        body(i)
        return carry

    lax.fori_loop(start, stop, step, 0)


def fold_rows(values):
    return jnp.sum(values.reshape(values.shape[0] // 8, 8, values.shape[1]), axis=0)


class Plane:
    def __init__(self, height, width, sems):
        self.d, self.z = lax.axis_index("dp"), lax.axis_index("tensor")
        member = lax.rem(self.d, GROUP_DEVS)
        self.core = lax.rem(member, 2)
        self.chip = member // 2
        self.bit = (lax.rem(self.chip, 2), self.chip // 2)
        self.height, self.half, self.sems = height, width // 2, sems

    def rows(self, chip, core):
        return pl.ds(pl.multiple_of((chip * 2 + core) * self.height, 16), self.height)

    def cols(self, colour):
        return pl.ds(colour * self.half, self.half)

    def at(self, first, x, y):
        return x + 2 * y if first == 0 else y + 2 * x

    def copy(self, i, src, dst, mask):
        return remote(
            src, dst, self.sems.at[0, i], self.sems.at[1, i], (jnp.bitwise_xor(self.d, mask), self.z)
        )


class PlaneReduce(Plane):
    def __init__(self, src, mine, near, far, last, sems):
        super().__init__(src.shape[0] // GROUP_DEVS, src.shape[1], sems)
        self.src, self.mine, self.near, self.far, self.last = src, mine, near, far, last

    def to_core(self, i):
        return self.copy(i, self.src.at[self.rows(i, 1 - self.core)], self.near(i), 1)

    def fetch(self, i):
        rows = self.src.at[self.rows(i, self.core)]
        return pltpu.make_async_copy(rows, self.mine, self.sems.at[0, 10])

    def part_of(self, i, colour):
        return self.near(i).at[:, self.cols(colour)]

    def first(self, colour, k):
        i = self.at(colour, 1 - self.bit[colour], k)
        return self.copy(
            4 + 2 * colour + k, self.part_of(i, colour), self.far(colour, k), 2 << colour
        )

    def second(self, colour):
        i = self.at(colour, self.bit[colour], 1 - self.bit[1 - colour])
        return self.copy(8 + colour, self.part_of(i, colour), self.last(colour), 4 >> colour)

    def start(self):
        for i in range(4):
            self.to_core(i).start()
        if self.mine is not None:
            self.fetch(0).start()

    def after_core(self):
        for i in range(4):
            self.to_core(i).wait_recv()
            if self.mine is not None:
                self.fetch(i).wait()
                own = self.mine[...]
            else:
                own = self.src[self.rows(i, self.core)]
            near = self.near(i)
            near[...] = (own.astype(F32) + near[...].astype(F32)).astype(BF16)
            if self.mine is not None and i < 3:
                self.fetch(i + 1).start()
        for colour in range(2):
            for k in range(2):
                self.first(colour, k).start()

    def after_first(self):
        for colour in range(2):
            for k in range(2):
                self.first(colour, k).wait_recv()
                mine = self.part_of(self.at(colour, self.bit[colour], k), colour)
                mine[...] = (
                    mine[...].astype(F32) + self.far(colour, k)[...].astype(F32)
                ).astype(BF16)
        for colour in range(2):
            self.second(colour).start()

    def result(self, out):
        for colour in range(2):
            self.second(colour).wait_recv()
            out[:, self.cols(colour)] = (
                self.part_of(self.chip, colour)[...].astype(F32)
                + self.last(colour)[...].astype(F32)
            ).astype(BF16)

    def finish(self):
        for i in range(4):
            self.to_core(i).wait_send()
        for colour in range(2):
            self.second(colour).wait_send()
            for k in range(2):
                self.first(colour, k).wait_send()


class PlaneGather(Plane):
    def __init__(self, piece, out, sems):
        super().__init__(piece.shape[0], piece.shape[1], sems)
        self.piece, self.out = piece, out

    def place(self, dx, dy, colour):
        chip = jnp.bitwise_xor(self.chip, dx + 2 * dy)
        return self.out.at[self.rows(chip, self.core), self.cols(colour)]

    def keep(self):
        own = self.out.at[self.rows(self.chip, self.core)]
        return pltpu.make_async_copy(self.piece, own, self.sems.at[0, 10])

    def first(self, colour):
        dst = self.place(0, 0, colour)
        return self.copy(colour, self.piece.at[:, self.cols(colour)], dst, 4 >> colour)

    def second(self, colour, k):
        there = self.place(0, k, colour) if colour == 0 else self.place(k, 0, colour)
        src = self.piece.at[:, self.cols(colour)] if k == 0 else there
        return self.copy(2 + 2 * colour + k, src, there, 2 << colour)

    def share(self, k):
        rows = self.out.at[self.rows(jnp.bitwise_xor(self.chip, k), self.core)]
        return self.copy(6 + k, self.piece if k == 0 else rows, rows, 1)

    def start(self):
        self.keep().start()
        for colour in range(2):
            self.first(colour).start()
        self.share(0).start()

    def after_first(self):
        for colour in range(2):
            self.second(colour, 0).start()
            self.first(colour).wait_recv()
            self.second(colour, 1).start()

    def after_second(self):
        for colour in range(2):
            for k in range(2):
                self.second(colour, k).wait_recv()
        for k in (1, 2, 3):
            self.share(k).start()

    def finish(self):
        self.keep().wait()
        for k in range(4):
            self.share(k).wait()
        for colour in range(2):
            self.first(colour).wait_send()
            for k in range(2):
                self.second(colour, k).wait_send()


class LineGather:
    def __init__(self, nz, place, send, recv):
        self.d, self.z = lax.axis_index("dp"), lax.axis_index("tensor")
        self.nz, self.place, self.send, self.recv = nz, place, send, recv

    def step(self, right, s):
        index, target = (self.z - s, self.z + 1) if right else (self.z + s, self.z - 1)
        there = (index >= 0) & (index < self.nz) & (target >= 0) & (target < self.nz)
        where = self.place(index)
        way = int(right)
        return there, remote(where, where, self.send.at[way, s], self.recv.at[way, s], (self.d, target))

    def arrive(self, right, s):
        index = self.z - 1 - s if right else self.z + 1 + s
        where = self.place(index)
        way = int(right)

        @pl.when((index >= 0) & (index < self.nz))
        def _():
            remote(
                where, where, self.send.at[way, s], self.recv.at[way, s], (self.d, self.z)
            ).wait_recv()

    def start(self, s):
        for right in (True, False):
            if s > 0:
                self.arrive(right, s - 1)
            there, copy = self.step(right, s)
            pl.when(there)(copy.start)

    def last(self):
        for right in (True, False):
            self.arrive(right, self.nz - 2)

    def drain(self):
        for right in (True, False):
            for s in range(self.nz - 1):
                there, copy = self.step(right, s)
                pl.when(there)(copy.wait_send)


def forward_kernel(
    nz, x_hbm, wq_hbm, wk_hbm, wv_hbm, cos_ref, sin_ref, gain_ref, wo_ref, bias_ref,
    q_ref, kv_ref, normed_hbm, att_hbm, kv_hbm, lse_ref, wo_all,
    x_in, normed, wq, wk, wv, att, kv_all, acc, top, total, ktok, mine,
    gs, gr, zs, zr, ws, wr, wp, load, leave, fetch, keep,
):
    heads = q_ref.shape[0]
    kvh = heads // 2
    d, z = lax.axis_index("dp"), lax.axis_index("tensor")
    some = mine.shape[0] // nz
    member = lax.rem(d, GROUP_DEVS)

    def own_place(index):
        return mine.at[pl.ds(pl.multiple_of(index * some, 16), some)]

    first_rows = pltpu.make_async_copy(
        wo_ref.at[pl.ds(pl.multiple_of(member * some, 16), some)], own_place(z), load.at[0]
    )
    first_rows.start()
    tokens = x_in.shape[0]
    group = 256
    groups = tokens // group

    def rows_of(j):
        return pl.ds(pl.multiple_of(j * group, group), group)

    x_loads = [
        pltpu.make_async_copy(x_hbm.at[rows_of(j)], x_in.at[rows_of(j)], fetch.at[j])
        for j in range(groups)
    ]
    w_loads = [
        pltpu.make_async_copy(src, dst, fetch.at[groups + n])
        for n, (src, dst) in enumerate(((wk_hbm, wk), (wv_hbm, wv), (wq_hbm, wq)))
    ]
    for copy in x_loads[:2] + w_loads[:2] + x_loads[2:] + w_loads[2:]:
        copy.start()

    def normed_out(j):
        return pltpu.make_async_copy(
            normed.at[rows_of(j)], normed_hbm.at[rows_of(j)], keep.at[j]
        )

    def turn(u, cols):
        half = HEAD_DIM // 2
        lower, upper = u[:half], u[half:]
        cosine, sine = cos_ref[:, cols], sin_ref[:, cols]
        return lower * cosine - upper * sine, upper * cosine + lower * sine

    def put_turned(ref, n, u, cols, scale):
        first, second = turn(u, cols)
        half = HEAD_DIM // 2
        ref[n, 0:half, cols] = (first * scale).astype(BF16)
        ref[n, half:HEAD_DIM, cols] = (second * scale).astype(BF16)

    def keys_values(j):
        cols = rows_of(j)
        x = x_in[cols].astype(F32)
        inverse = lax.rsqrt(jnp.mean(x * x, axis=-1, keepdims=True) + EPSILON)
        n = (x * inverse * gain_ref[...]).astype(BF16)
        normed[cols] = n
        normed_out(j).start()
        keys, values = dot_nt(wk[...], n), dot_nt(wv[...], n)
        for h in range(kvh):
            some = slice(h * HEAD_DIM, (h + 1) * HEAD_DIM)
            put_turned(kv_ref, h, keys[some], cols, 1.0)
            kv_ref[kvh + h, :, cols] = values[some].astype(BF16)

    for copy in x_loads[:2] + w_loads[:2]:
        copy.wait()
    loop(0, groups // 2, keys_values)
    greet(plane((1, 2, 4, 6)) + neighbours(nz))
    own = kv_ref.at[:, :, pl.ds(0, PB)]
    firsts = [
        remote(own, kv_all.at[m], gs.at[m], gr.at[m], target)
        for m, target in zip((1, 2, 4, 6), plane((1, 2, 4, 6)))
    ]
    for copy in firsts:
        copy.start()
    w_line = LineGather(nz, own_place, ws, wr)
    w_plane = PlaneGather(mine, wo_all, wp)
    first_rows.wait()
    w_line.start(0)
    for copy in x_loads[2:] + w_loads[2:]:
        copy.wait()
    loop(groups // 2, groups, keys_values)
    w_rows = wq[...].T

    def queries(j):
        cols = rows_of(j)
        u = dot_nt(w_rows, normed[cols])
        for head in range(heads):
            some = slice(head * HEAD_DIM, (head + 1) * HEAD_DIM)
            put_turned(q_ref, head, u[some], cols, HEAD_DIM ** (-0.5) * LOG2E)

    for j in range(groups):
        queries(j)
    kv_all[0] = kv_ref[:, :, 0:PB]
    for h in range(kvh):
        ktok[8, h] = kv_ref[h, :, PB : PB + CL].T
        ktok[0, h] = kv_ref[h, :, 0:PB].T
    acc[...] = jnp.zeros_like(acc)
    top[...] = jnp.full_like(top, NEG)
    total[...] = jnp.zeros_like(total)

    def block(head, half, key, value, mask, bias):
        cols = pl.ds(half * PB, PB)
        s = dot(key, q_ref[head, :, cols])
        if mask:
            s = causal(s)
        old = top[head, :, cols]
        high = jnp.max(s, axis=0, keepdims=True)
        new = jnp.maximum(old, high if bias is None else high + bias)
        p = jnp.exp2(s - (new if bias is None else new - bias))
        shrink = jnp.exp2(old - new)
        total[head, :, cols] = total[head, :, cols] * shrink + jnp.sum(p, axis=0, keepdims=True)
        acc[head, :, cols] = acc[head, :, cols] * shrink + dot(value, p.astype(BF16))
        top[head, :, cols] = new

    def slot_step(slot, half, mask=False, bias=None):
        for head in range(heads):
            block(head, half, ktok[slot, head // 2], kv_all[slot, kvh + head // 2], mask, bias)

    for head in range(heads):
        block(head, 1, ktok[8, head // 2], kv_ref[kvh + head // 2, :, PB : PB + CL], True, None)

    def arrive(m):
        remote(kv_all.at[m], kv_all.at[m], gs.at[m], gr.at[m], (d, z)).wait_recv()

    def hand_on(m):
        return remote(kv_all.at[m], kv_all.at[m + 1], gs.at[m + 1], gr.at[m + 1], plane((1,))[0])

    def tail_slot(m):
        @pl.when(m > 0)
        def _():
            arrive(m)
            for h in range(kvh):
                ktok[m, h] = kv_all[m, h].T

        @pl.when((m > 0) & (lax.rem(m, 2) == 0))
        def _():
            hand_on(m).start()

        for s in range(1, nz - 1):

            @pl.when(m == 2 * s)
            def _():
                w_line.start(s)

        @pl.when(m == GROUP_DEVS - 1)
        def _():
            w_line.last()
            w_plane.start()

        slot_step(m, 1)

    loop(0, GROUP_DEVS, tail_slot)

    def finish(half):
        cols = pl.ds(half * PB, PB)
        for head in range(heads):
            att[z, pl.ds(head * HEAD_DIM, HEAD_DIM), cols] = (
                acc[head, :, cols] / total[head, :, cols]
            ).astype(BF16)
            lse_ref[head, :, cols] = top[head, :, cols] + jnp.log2(total[head, :, cols])

    lines = [
        LineGather(
            nz,
            lambda index, half=half: att.at[index, :, pl.ds(half * PB, PB)],
            zs.at[half],
            zr.at[half],
        )
        for half in range(2)
    ]
    kv_out = pltpu.make_async_copy(kv_all, kv_hbm, leave.at[2])
    kv_out.start()

    def att_out(half):
        there = (slice(None), slice(None), pl.ds(half * PB, PB))
        return pltpu.make_async_copy(att.at[there], att_hbm.at[there], leave.at[half])

    finish(1)
    lines[1].start(0)
    slot_step(0, 0, mask=True)

    def prompt_slot(m):
        slot_step(m, 0, bias=bias_ref[m])

        @pl.when(m == 4)
        def _():
            w_plane.after_first()
            lines[1].start(1)

    loop(1, GROUP_DEVS, prompt_slot)
    finish(0)
    lines[0].start(0)
    w_plane.after_second()
    for s in range(2, nz - 1):
        lines[1].start(s)
    for s in range(1, nz - 1):
        lines[0].start(s)
    for half in (1, 0):
        lines[half].last()
        att_out(half).start()
    for line in lines + [w_line]:
        line.drain()
    w_plane.finish()
    for copy in firsts:
        copy.wait_send()
    for m in (2, 4, 6):
        hand_on(m).wait_send()
    kv_out.wait()
    for j in range(groups):
        normed_out(j).wait()
    for half in range(2):
        att_out(half).wait()


def forward_attention(nz, x, w_query, w_key, w_value, cosine, sine, gain, w_out, bias):
    tokens = x.shape[0]
    heads, kvh = w_query.shape[1] // HEAD_DIM, w_key.shape[0] // HEAD_DIM
    own, width = w_out.shape
    anywhere = pl.BlockSpec(memory_space=pl.ANY)
    vmem = pl.BlockSpec(memory_space=VM)
    return pl.pallas_call(
        functools.partial(forward_kernel, nz),
        out_shape=(
            jax.ShapeDtypeStruct((heads, HEAD_DIM, tokens), BF16),
            jax.ShapeDtypeStruct((2 * kvh, HEAD_DIM, tokens), BF16),
            jax.ShapeDtypeStruct(x.shape, BF16),
            jax.ShapeDtypeStruct((nz, heads * HEAD_DIM, tokens), BF16),
            jax.ShapeDtypeStruct((GROUP_DEVS, 2 * kvh, HEAD_DIM, PB), BF16),
            jax.ShapeDtypeStruct((heads, 1, tokens), F32),
            jax.ShapeDtypeStruct((nz * own, width), BF16),
        ),
        in_specs=[anywhere] * 4
        + [vmem] * 3
        + [anywhere, pl.BlockSpec(memory_space=pltpu.SMEM)],
        out_specs=(vmem, vmem, anywhere, anywhere, anywhere, vmem, anywhere),
        scratch_shapes=[
            VM(x.shape, BF16),
            VM(x.shape, BF16),
            VM(w_query.shape, BF16),
            VM(w_key.shape, BF16),
            VM(w_value.shape, BF16),
            VM((nz, heads * HEAD_DIM, tokens), BF16),
            VM((GROUP_DEVS, 2 * kvh, HEAD_DIM, PB), BF16),
            VM((heads, HEAD_DIM, tokens), F32),
            VM((heads, 1, tokens), F32),
            VM((heads, 1, tokens), F32),
            VM((GROUP_DEVS + 1, kvh, PB, HEAD_DIM), BF16),
            VM((nz * own // GROUP_DEVS, width), BF16),
            pltpu.SemaphoreType.DMA((GROUP_DEVS,)),
            pltpu.SemaphoreType.DMA((GROUP_DEVS,)),
            pltpu.SemaphoreType.DMA((2, 2, nz - 1)),
            pltpu.SemaphoreType.DMA((2, 2, nz - 1)),
            pltpu.SemaphoreType.DMA((2, nz - 1)),
            pltpu.SemaphoreType.DMA((2, nz - 1)),
            pltpu.SemaphoreType.DMA((2, 11)),
            pltpu.SemaphoreType.DMA((1,)),
            pltpu.SemaphoreType.DMA((3,)),
            pltpu.SemaphoreType.DMA((tokens // 256 + 3,)),
            pltpu.SemaphoreType.DMA((tokens // 256,)),
        ],
        compiler_params=pltpu.CompilerParams(
            collective_id=0, has_side_effects=True, vmem_limit_bytes=60 << 20
        ),
        cost_estimate=pl.CostEstimate(
            flops=40_000_000_000, bytes_accessed=12_000_000, transcendentals=19_000_000
        ),
        name="forward_attention",
    )(x, w_query, w_key, w_value, cosine, sine, gain, w_out, bias)


class Stream:
    def __init__(self, rows, count, ins, out):
        self.rows, self.count, self.ins, self.out = rows, count, ins, out

    def load(self, i):
        slot = lax.rem(i, 2)
        return [
            pltpu.make_async_copy(src.at[self.rows(i)], buf.at[slot], sem.at[slot])
            for src, buf, sem in self.ins
        ]

    def store(self, i):
        dst, buf, sem = self.out
        slot = lax.rem(i, 2)
        return pltpu.make_async_copy(buf.at[slot], dst.at[self.rows(i)], sem.at[slot])

    def prime(self):
        for i in range(2):
            for copy in self.load(i):
                copy.start()

    def take(self, i):
        for copy in self.load(i):
            copy.wait()

        @pl.when(i >= 2)
        def _():
            self.store(i - 2).wait()

    def give(self, i):
        self.store(i).start()

        @pl.when(i + 2 < self.count)
        def _():
            for copy in self.load(i + 2):
                copy.start()

    def flush(self):
        for i in range(self.count - 2, self.count):
            self.store(i).wait()


def tail_kernel(
    nz, chunk, q_ref, kv_ref, do_ref, bias_ref, lse_ref, inner_ref, feed, cos_ref, sin_ref,
    gain_ref, gain_two, kv_all, mid_hbm, ffn_hbm, normed_hbm, x_hbm, ga_hbm, wq_hbm, wk_hbm, wv_hbm,
    gwo_hbm,
    act, gt, gains, summed, ffn_sum,
    kvs, wq, wk, wv, dq, dkv, near, far, ktok, vtok, low, total, held, f_piece, part, total_one, held_one, weights, a_near, a_far, a_last, a_piece, tile_in,
    mid_in, act_out, x_in, ga_in, gt_out, accum, box,
    ss, rr, fs, fr, ss1, rr1, fs1, fr1, ns, nr, ps, pr, a_sems, ag_sems, fg_sems, bs, br,
    loads, kv_sem, m_sem, act_sem, x_sem, g_sem, gt_sem,
):
    heads = q_ref.shape[0]
    kvh = heads // 2
    d, z = lax.axis_index("dp"), lax.axis_index("tensor")
    member = lax.rem(d, GROUP_DEVS)
    masks = range(1, GROUP_DEVS)
    nq = heads * HEAD_DIM
    nkv = kvh * HEAD_DIM
    tokens, width = feed.shape
    pairs = (
        (wq_hbm, wq),
        (wk_hbm, wk),
        (wv_hbm, wv),
        (gwo_hbm, weights.at[pl.ds(nq + 2 * nkv, gwo_hbm.shape[0])]),
    )
    fetches = [pltpu.make_async_copy(src, dst, loads.at[i]) for i, (src, dst) in enumerate(pairs)]

    def kv_load(t):
        slot = lax.rem(2 * t + 1 + t // 4, GROUP_DEVS)
        return pltpu.make_async_copy(
            kv_all.at[slot], kvs.at[lax.rem(t, 2)], kv_sem.at[lax.rem(t, 2)]
        )

    kv_load(0).start()
    first_piece = pltpu.make_async_copy(ffn_hbm, f_piece, loads.at[len(pairs)])
    first_piece.start()
    batch = 4
    line = Line(nz, chunk, feed, total, held, (ss, rr, fs, fr))
    line_one = Line(
        nz, chunk, part, total_one, held_one, (ss1, rr1, fs1, fr1), shift=tokens // chunk // 2
    )
    batches = line.count // batch
    acts = Stream(
        lambda i: line.batch(i, batch), batches, [(mid_hbm, mid_in, m_sem)], (act, act_out, act_sem)
    )
    outs = Stream(
        lambda i: line_one.batch(i, batch),
        batches,
        [(x_hbm, x_in, x_sem), (ga_hbm, ga_in, g_sem)],
        (gt, gt_out, gt_sem),
    )
    acts.prime()
    greet(neighbours(nz) + plane(masks))
    reduce_attn = PlaneReduce(
        weights,
        None,
        lambda i: a_near.at[i],
        lambda c, k: a_far.at[c, k],
        lambda c: a_last.at[c],
        a_sems,
    )
    gather_attn = PlaneGather(a_piece, summed, ag_sems)
    gather_ffn = PlaneGather(f_piece, ffn_sum, fg_sems)
    loop(0, line.count, line.issue)
    first_piece.wait()
    gather_ffn.start()
    for copy in fetches:
        copy.start()
    lag = 12
    ply = 2

    def ripple(s):
        @pl.when(s < line.count)
        def _():
            line.service(s)

        @pl.when(s >= lag)
        def _():
            line.ready(s - lag)

        @pl.when((s >= lag) & (lax.rem(s - lag, batch) == batch - 1))
        def _():
            i = (s - lag) // batch
            acts.take(i)
            act_out[lax.rem(i, 2)] = (
                mid_in[lax.rem(i, 2)].astype(F32) + total[line.batch(i, batch)].astype(F32)
            ).astype(BF16)
            acts.give(i)

    def background(s):
        @pl.when(s == 8)
        def _():
            gather_ffn.after_first()

        @pl.when(s == 22)
        def _():
            gather_ffn.after_second()

        loop(s * ply, s * ply + ply, ripple)

    dq[...] = jnp.zeros_like(dq)

    def block(head, half, keyt, mask, bias):
        h = head // 2
        cols = pl.ds(half * PB, PB)
        s = dot(ktok[h], q_ref[head, :, cols])
        if mask:
            s = causal(s)
        shift = lse_ref[head, :, cols]
        if bias is not None:
            shift = shift - bias
        p = jnp.exp2(s - shift)
        dp = dot(vtok[h], do_ref[head, :, cols])
        ds = (p * (dp - inner_ref[head, :, cols])).astype(BF16)
        dq[head, :, cols] += dot(keyt, ds)
        dv = dot_nt(do_ref[head, :, cols], p.astype(BF16))
        dk = dot_nt(q_ref[head, :, cols], ds)
        return dk, dv

    def total_of(parts):
        out = parts[0]
        for piece in parts[1:]:
            out = out + piece
        return out

    def turn_back(u, half):
        cols = pl.ds(half * PB, PB)
        cosine, sine = cos_ref[:, cols], sin_ref[:, cols]
        lower, upper = u[: HEAD_DIM // 2], u[HEAD_DIM // 2 :]
        return lower * cosine + upper * sine, upper * cosine - lower * sine

    def put_low(row, half, u, turned):
        cols = pl.ds(half * PB, PB)
        if not turned:
            low[pl.ds(row, HEAD_DIM), cols] = u.astype(BF16)
            return
        first, second = turn_back(u, half)
        low[pl.ds(row, HEAD_DIM // 2), cols] = first.astype(BF16)
        low[pl.ds(row + HEAD_DIM // 2, HEAD_DIM // 2), cols] = second.astype(BF16)

    for h in range(kvh):
        ktok[h] = kv_ref[h, :, PB : PB + CL].T
        vtok[h] = kv_ref[kvh + h, :, PB : PB + CL].T
    for h in range(kvh):
        both = [block(2 * h + r, 1, kv_ref[h, :, PB : PB + CL], True, None) for r in range(2)]
        put_low(nq + h * HEAD_DIM, 1, total_of([b[0] for b in both]) * (1.0 / LOG2E), True)
        put_low(nq + nkv + h * HEAD_DIM, 1, total_of([b[1] for b in both]), False)

    quarter = GROUP_DEVS // 2

    def slot_step(t, where, first):
        kv_load(t).wait()
        now = lax.rem(t, 2)
        for h in range(kvh):
            ktok[h] = kvs[now, h].T
            vtok[h] = kvs[now, kvh + h].T
        bias = None if first else bias_ref[lax.rem(2 * t + 1 + t // 4, GROUP_DEVS)]
        for h in range(kvh):
            both = []
            for r in range(2):
                background(t * 4 + h * 2 + r)
                both.append(block(2 * h + r, 1, kvs[now, h], False, None))
                both.append(block(2 * h + r, 0, kvs[now, h], first, bias))
            dkv[where, h] = (total_of([b[0] for b in both]) * (1.0 / LOG2E)).astype(BF16)
            dkv[where, kvh + h] = total_of([b[1] for b in both]).astype(BF16)

    def to_near(i):
        return remote(dkv.at[i], near.at[i], ns.at[i], nr.at[i], plane((1,))[0])

    def to_far(i):
        return remote(near.at[i], far.at[i], ps.at[i], pr.at[i], (jnp.bitwise_xor(d, 2 * i), z))

    def step(t):
        kv_load(t + 1).start()
        slot_step(t, t - t // quarter * (t - quarter), False)

        @pl.when(t < quarter)
        def _():
            to_near(t).start()

        @pl.when(t >= quarter)
        def _():
            i = t - quarter + 1
            to_near(i).wait_recv()
            near[i] = (dkv[quarter].astype(F32) + near[i].astype(F32)).astype(BF16)
            to_far(i).start()

    last = GROUP_DEVS - 1
    loop(0, last, step)
    slot_step(last, quarter, True)

    def back(j):
        group = tokens // 4
        rows = pl.ds(pl.multiple_of(j * group, group), group)
        a = [low[pl.ds(at, n), rows].T for at, n in ((0, nq), (nq, nkv), (nq + nkv, nkv))]
        size = 512
        for t in range(width // size):
            cols = pl.ds(t * size, size)
            part[rows, cols] = (
                dot_nt(a[0], wq[cols]) + dot(a[1], wk[:, cols]) + dot(a[2], wv[:, cols])
            ).astype(BF16)

    for copy in fetches:
        copy.wait()
    done = 4 * GROUP_DEVS * ply
    left = line.count + lag - done
    share = left // 4
    half_count = line.count // 2
    for head in range(heads):
        put_low(head * HEAD_DIM, 1, dq[head, :, PB : PB + CL] * HEAD_DIM ** (-0.5), True)
    loop(2, 4, back)
    loop(0, half_count, line_one.issue)
    loop(done, done + share, ripple)
    for head in range(heads):
        put_low(head * HEAD_DIM, 0, dq[head, :, 0:PB] * HEAD_DIM ** (-0.5), True)
    to_near(0).wait_recv()
    for i in range(1, quarter):
        to_far(i).wait_recv()
    for h in range(2 * kvh):
        home = dkv[quarter, h].astype(F32)
        home = home + near[0, h].astype(F32)
        for i in range(1, quarter):
            home = home + far[i, h].astype(F32)
        put_low(nq + h * HEAD_DIM, 0, home, h < kvh)
    loop(0, 2, back)
    loop(half_count, line.count, line_one.issue)
    loop(done + share, done + 2 * share, ripple)
    outs.prime()
    size = tile_in.shape[1]

    def tile_load(t):
        return pltpu.make_async_copy(
            normed_hbm.at[:, pl.ds(t * size, size)], tile_in, loads.at[len(pairs)]
        )

    def tile_step(t):
        tile_load(t).wait()
        weights[0 : nq + 2 * nkv, pl.ds(t * size, size)] = dot(low[...], tile_in[...]).astype(BF16)
        if t + 1 < width // size:
            tile_load(t + 1).start()

    tile_load(0).start()
    loop(done + 2 * share, done + left, ripple)
    acts.flush()
    accum[...] = jnp.zeros_like(accum)
    gain = gain_ref[...]
    lag_one = 10

    def body(s):
        @pl.when(s < line_one.count)
        def _():
            line_one.service(s)

        @pl.when(s >= lag_one)
        def _():
            line_one.ready(s - lag_one)

        @pl.when((s >= lag_one) & (lax.rem(s - lag_one, batch) == batch - 1))
        def _():
            i = (s - lag_one) // batch
            outs.take(i)
            slot = lax.rem(i, 2)
            x = x_in[slot].astype(F32)
            inverse = lax.rsqrt(jnp.mean(x * x, axis=-1, keepdims=True) + EPSILON)
            upstream = total_one[line_one.batch(i, batch)].astype(F32)
            inner = upstream * gain
            through = inverse * inner - x * inverse**3 * jnp.mean(
                inner * x, axis=-1, keepdims=True
            )
            gt_out[slot] = (ga_in[slot].astype(F32) + through).astype(BF16)
            accum[...] += fold_rows(upstream * x * inverse)
            outs.give(i)

        for t in range(width // size):

            @pl.when(s == 4 + 5 * t)
            def _():
                tile_step(t)

        @pl.when(s == 15)
        def _():
            reduce_attn.start()

        @pl.when(s == 19)
        def _():
            reduce_attn.after_core()

        @pl.when(s == 31)
        def _():
            reduce_attn.after_first()

        @pl.when(s == 39)
        def _():
            reduce_attn.result(a_piece)
            gather_attn.start()

        @pl.when(s == 46)
        def _():
            gather_attn.after_first()

        @pl.when(s == 58)
        def _():
            gather_attn.after_second()

    loop(0, line_one.count + lag_one, body)
    box[member, 0:1] = jnp.sum(accum[...], axis=0, keepdims=True)
    box[member, 1:2] = gain_two[...]
    copies = [
        remote(box.at[member], box.at[member], bs.at[m], br.at[m], target)
        for m, target in zip(masks, plane(masks))
    ]
    for copy in copies:
        copy.start()
    outs.flush()
    for i in range(quarter):
        to_near(i).wait_send()
    for i in range(1, quarter):
        to_far(i).wait_send()
    line.drain()
    line_one.drain()
    reduce_attn.finish()
    gather_ffn.finish()
    gather_attn.finish()
    for copy in copies:
        copy.wait()
    result = box[0]
    for m in masks:
        result = result + box[m]
    gains[...] = result


def tail_stage(
    nz, q, kv, do, bias, lse, inner, feed, cosine, sine, gain, gain_two, kv_all, middle, ffn, normed,
    x, ga, w_query, w_key, w_value, grad_w_out, chunk=16,
):
    heads = q.shape[0]
    kvh = heads // 2
    tokens, width = feed.shape
    slot = (2 * kvh, HEAD_DIM, PB)
    n_attn = (heads + 2 * kvh) * HEAD_DIM + grad_w_out.shape[0]
    high, wide = ffn.shape
    low_high = n_attn // GROUP_DEVS
    count = tokens // chunk
    rows = 4 * chunk
    quarter = GROUP_DEVS // 2
    dma = lambda *shape: pltpu.SemaphoreType.DMA(shape)
    lines = [dma(2, count)] * 3 + [dma(count)]
    block = VM((2, rows, width), BF16)
    anywhere = pl.BlockSpec(memory_space=pl.ANY)
    vmem = pl.BlockSpec(memory_space=VM)
    return pl.pallas_call(
        functools.partial(tail_kernel, nz, chunk),
        out_shape=(
            jax.ShapeDtypeStruct(feed.shape, BF16),
            jax.ShapeDtypeStruct(feed.shape, BF16),
            jax.ShapeDtypeStruct((2, width), F32),
            jax.ShapeDtypeStruct((n_attn, width), BF16),
            jax.ShapeDtypeStruct((high * GROUP_DEVS, wide), BF16),
        ),
        in_specs=[vmem] * 3 + [pl.BlockSpec(memory_space=pltpu.SMEM)] + [vmem] * 7 + [anywhere] * 10,
        out_specs=(anywhere, anywhere, vmem, anywhere, anywhere),
        scratch_shapes=[
            VM((2,) + slot, BF16),
            VM(w_query.shape, BF16),
            VM(w_key.shape, BF16),
            VM(w_value.shape, BF16),
            VM((heads, HEAD_DIM, tokens), F32),
            VM((quarter + 1,) + slot, BF16),
            VM((quarter,) + slot, BF16),
            VM((quarter,) + slot, BF16),
            VM((kvh, PB, HEAD_DIM), BF16),
            VM((kvh, PB, HEAD_DIM), BF16),
            VM(((heads + 2 * kvh) * HEAD_DIM, tokens), BF16),
            VM(feed.shape, BF16),
            VM(feed.shape, BF16),
            VM((high, wide), BF16),
            VM(feed.shape, BF16),
            VM(feed.shape, BF16),
            VM(feed.shape, BF16),
            VM((n_attn, width), BF16),
            VM((4, low_high, width), BF16),
            VM((2, 2, low_high, width // 2), BF16),
            VM((2, low_high, width // 2), BF16),
            VM((low_high, width), BF16),
            VM((tokens, 512), BF16),
            block,
            block,
            block,
            block,
            block,
            VM((8, width), F32),
            VM((GROUP_DEVS, 2, width), F32),
        ]
        + lines * 2
        + [dma(quarter)] * 4
        + [dma(2, 11)] * 3
        + [dma(GROUP_DEVS)] * 2
        + [dma(5)]
        + [dma(2)] * 6,
        compiler_params=pltpu.CompilerParams(
            collective_id=1, has_side_effects=True, vmem_limit_bytes=60 << 20
        ),
        cost_estimate=pl.CostEstimate(
            flops=200_000_000_000, bytes_accessed=50_000_000, transcendentals=19_000_000
        ),
        name="tail_stage",
    )(
        q, kv, do, bias, lse, inner, feed, cosine, sine, gain, gain_two, kv_all, middle, ffn, normed,
        x, ga, w_query, w_key, w_value, grad_w_out,
    )


def middle_kernel(
    nz, chunk, att_hbm, wo_hbm, x_hbm, wg_hbm, wu_hbm, wd_hbm, cot_hbm, gain_ref,
    gatt, inner_out, gwo, gain_two, ga_hbm, mid_hbm, feed_hbm, gffn, piece,
    ga, mid, feed, att, wo, wg, wu, wd, cot, mid32, nt2, hidden, gg, gu, part, total, accum, stage,
    load, store, leave, r_sems, spent, held, ss, rr, fs, fr,
):
    z = lax.axis_index("tensor")
    group, slab = 256, 256
    tokens, width = mid.shape
    head, rest = pl.ds(0, group), pl.ds(group, tokens - group)
    pairs = (
        (x_hbm.at[head], mid.at[head]),
        (att_hbm.at[:, head], att.at[:, head]),
        (wg_hbm, wg),
        (wu_hbm, wu),
        (cot_hbm, cot),
        (wd_hbm, wd),
        (x_hbm.at[rest], mid.at[rest]),
        (att_hbm.at[:, rest], att.at[:, rest]),
    )
    loads = [pltpu.make_async_copy(src, dst, load.at[i]) for i, (src, dst) in enumerate(pairs)]
    own = gatt.shape[0]
    some = own // GROUP_DEVS

    def wo_rows(i):
        src = pl.ds(pl.multiple_of(i * some, 16), some)
        dst = pl.ds(pl.multiple_of(lax.rem(i, nz) * own + i // nz * some, 16), some)
        pltpu.make_async_copy(wo_hbm.at[src], wo.at[dst], load.at[len(pairs)]).start()

    for copy in loads[:2]:
        copy.start()
    loop(0, nz * GROUP_DEVS, wo_rows)
    for copy in loads[2:]:
        copy.start()
    greet(neighbours(nz) + plane((1, 2, 4)))
    ff = wg.shape[1]
    heads = own // HEAD_DIM
    per = group // chunk
    ply = 4
    quarters = per // ply
    tile = 512
    gain = gain_ref[...]
    accum[...] = jnp.zeros_like(accum)
    line = Line(nz, chunk, part, total, held, (ss, rr, fs, fr))
    mine = pl.ds(pl.multiple_of(z * own, own), own)
    lag = 12

    def out_of(n, g):
        src, dst = ((mid, mid_hbm), (feed, feed_hbm), (ga, ga_hbm))[n]
        rows = pl.ds(pl.multiple_of(g * group, group), group)
        return pltpu.make_async_copy(src.at[rows], dst.at[rows], leave.at[n, g])

    def settle(c):
        rows = line.batch(c, ply)
        m = mid[rows].astype(F32)
        inverse = lax.rsqrt(jnp.mean(m * m, axis=-1, keepdims=True) + EPSILON)
        upstream = total[rows].astype(F32)
        inner = upstream * gain
        through = inverse * inner - m * inverse**3 * jnp.mean(inner * m, axis=-1, keepdims=True)
        ga[rows] = (cot[rows].astype(F32) + through).astype(BF16)
        accum[...] += fold_rows(upstream * m * inverse)

        @pl.when(lax.rem(c, quarters) == quarters - 1)
        def _():
            out_of(2, c // quarters).start()
            block = pl.ds(pl.multiple_of((c // quarters) * group, group), group)
            back = dot_nt(wo[mine], ga[block])
            gatt[:, block] = back.astype(BF16)
            for head in range(heads):
                some = pl.ds(head * HEAD_DIM, HEAD_DIM)
                there = att[pl.ds(pl.multiple_of(z * own + head * HEAD_DIM, 32), HEAD_DIM), block]
                inner_out[head, :, block] = jnp.sum(
                    gatt[some, block].astype(F32) * there.astype(F32), axis=0, keepdims=True
                )

    def ripple(s):
        @pl.when(s < line.count)
        def _():
            line.service(s)

        @pl.when(s >= lag)
        def _():
            line.ready(s - lag)

        @pl.when((s >= lag) & (lax.rem(s - lag, ply) == ply - 1))
        def _():
            settle((s - lag) // ply)

    def tick(s):
        @pl.when(s >= 0)
        def _():
            loop(s * ply, s * ply + ply, ripple)

    for copy in loads[:2]:
        copy.wait()
    pltpu.make_async_copy(wo_hbm, wo, load.at[len(pairs)]).wait()

    def forward(j):
        @pl.when(j == 1)
        def _():
            for copy in loads[6:]:
                copy.wait()

        rows = pl.ds(pl.multiple_of(j * group, group), group)
        a = att[:, rows].T
        for t in range(width // tile):
            cols = pl.ds(t * tile, tile)
            mid32[:, cols] = mid[rows, cols].astype(F32) + dot(a, wo[:, cols])
        m = mid32[...]
        mid[rows] = m.astype(BF16)
        inverse = lax.rsqrt(jnp.mean(m * m, axis=-1, keepdims=True) + EPSILON)
        nt2[rows] = (m * inverse * gain).astype(BF16)

        @pl.when(j == 0)
        def _():
            for copy in loads[2:6]:
                copy.wait()

        tick(2 * j - 3)
        for t in range(ff // tile):
            cols = pl.ds(t * tile, tile)
            gate = dot(nt2[rows], wg[:, cols])
            up = dot(nt2[rows], wu[:, cols])
            back = dot_nt(cot[rows], wd[cols])
            sig = jax.nn.sigmoid(gate)
            silu = gate * sig
            hidden[rows, cols] = (silu * up).astype(BF16)
            gu[rows, cols] = (back * silu).astype(BF16)
            gg[rows, cols] = (back * up * (sig * (1.0 + gate * (1.0 - sig)))).astype(BF16)
        for t in range(width // tile):
            cols = pl.ds(t * tile, tile)
            part[rows, cols] = (dot_nt(gg[rows], wg[cols]) + dot_nt(gu[rows], wu[cols])).astype(BF16)
        loop(j * per, j * per + per, line.issue)
        for t in range(width // tile):
            cols = pl.ds(t * tile, tile)
            feed[rows, cols] = dot(hidden[rows], wd[:, cols]).astype(BF16)
        out_of(0, j).start()
        out_of(1, j).start()
        tick(2 * j - 2)

    steps = tokens // group
    loop(0, steps, forward)
    for target in plane((1, 2, 4)):
        pl.semaphore_signal(spent, inc=1, device_id=target, device_id_type=MESH)
    high, half = width // GROUP_DEVS, ff // 2

    def rows_of(n):
        return pl.ds(pl.multiple_of(n * high, 16), high)

    def reduce_of(q):
        src = gffn.at[:, pl.ds(q * ff, ff)]
        own = stage.at[0, pl.ds(0, high), pl.ds(q * ff, ff)]
        sems = r_sems.at[q]
        if q < 2:
            room = (wg, wu)[q]
            return PlaneReduce(
                src,
                own,
                lambda i: room.at[rows_of(i)],
                lambda c, n: room.at[rows_of(4 + n), pl.ds(c * half, half)],
                lambda c: room.at[rows_of(6), pl.ds(c * half, half)],
                sems,
            )
        return PlaneReduce(
            src,
            own,
            lambda i: wd.at[rows_of(i), pl.ds(0, ff)],
            lambda c, n: wd.at[rows_of(2 * c + n), pl.ds(ff, half)],
            lambda c: wd.at[rows_of(4), pl.ds(c * half, half)],
            sems,
        )

    reduces = [reduce_of(q) for q in range(3)]
    done = 2 * steps - 3
    slabs = width // slab

    def put(t):
        return pltpu.make_async_copy(
            stage.at[lax.rem(t, 2)],
            gffn.at[pl.ds(pl.multiple_of(t * slab, slab), slab)],
            store.at[lax.rem(t, 2)],
        )

    def weights(t):
        @pl.when(t >= 2)
        def _():
            put(t - 2).wait()

        slot = lax.rem(t, 2)
        cols = pl.ds(pl.multiple_of(t * slab, slab), slab)
        a = nt2[:, cols].T
        stage[slot, :, 0:ff] = dot(a, gg[...]).astype(BF16)
        stage[slot, :, ff : 2 * ff] = dot(a, gu[...]).astype(BF16)
        stage[slot, :, 2 * ff : 3 * ff] = dot(cot[:, cols].T, hidden[...]).astype(BF16)
        put(t).start()

        @pl.when(lax.rem(t, 2) == 1)
        def _():
            tick(done + t // 2)

    loop(0, slabs, weights)
    for t in (slabs - 2, slabs - 1):
        put(t).wait()
    pl.semaphore_wait(spent, 3)
    for reduce in reduces:
        reduce.start()
    begin, end = (done + slabs // 2) * ply, line.count + lag
    marks = (begin, begin + 9, begin + 32, end)
    loop(marks[0], marks[1], ripple)
    for reduce in reduces:
        reduce.after_core()
    loop(marks[1], marks[2], ripple)
    for reduce in reduces:
        reduce.after_first()
    loop(marks[2], marks[3], ripple)
    for t in range(width // tile):
        cols = pl.ds(t * tile, tile)
        gwo[:, cols] = dot(att[mine], ga[:, cols]).astype(BF16)
    gain_two[...] = jnp.sum(accum[...], axis=0, keepdims=True)
    for q in range(3):
        reduces[q].result(stage.at[1, pl.ds(0, high), pl.ds(q * ff, ff)])
    out = pltpu.make_async_copy(stage.at[1, pl.ds(0, high)], piece, store.at[0])
    out.start()
    for reduce in reduces:
        reduce.finish()
    line.drain()
    out.wait()
    for n in range(3):
        loop(0, steps, lambda g, n=n: out_of(n, g).wait())


def middle_stage(nz, att_all, w_out_all, x, w_gate, w_up, w_down, cot, gain, chunk=16):
    tokens, width = x.shape
    ff = w_gate.shape[1]
    own = w_out_all.shape[0] // nz
    heads = own // HEAD_DIM
    group, slab = 256, 256
    wide = jax.ShapeDtypeStruct((tokens, width), BF16)
    return pl.pallas_call(
        functools.partial(middle_kernel, nz, chunk),
        out_shape=(
            jax.ShapeDtypeStruct((own, tokens), BF16),
            jax.ShapeDtypeStruct((heads, 1, tokens), F32),
            jax.ShapeDtypeStruct((own, width), BF16),
            jax.ShapeDtypeStruct((1, width), F32),
            wide,
            wide,
            wide,
            jax.ShapeDtypeStruct((width, 3 * ff), BF16),
            jax.ShapeDtypeStruct((width // GROUP_DEVS, 3 * ff), BF16),
        ),
        in_specs=[pl.BlockSpec(memory_space=pl.ANY)] * 7 + [pl.BlockSpec(memory_space=VM)],
        out_specs=(pl.BlockSpec(memory_space=VM),) * 4 + (pl.BlockSpec(memory_space=pl.ANY),) * 5,
        scratch_shapes=[
            VM((tokens, width), BF16),
            VM((tokens, width), BF16),
            VM((tokens, width), BF16),
            VM(w_out_all.shape[:1] + (tokens,), BF16),
            VM(w_out_all.shape, BF16),
            VM((width, ff), BF16),
            VM((width, ff), BF16),
            VM((ff, width), BF16),
            VM((tokens, width), BF16),
            VM((group, width), F32),
            VM((tokens, width), BF16),
            VM((tokens, ff), BF16),
            VM((tokens, ff), BF16),
            VM((tokens, ff), BF16),
            VM((tokens, width), BF16),
            VM((tokens, width), BF16),
            VM((8, width), F32),
            VM((2, slab, 3 * ff), BF16),
            pltpu.SemaphoreType.DMA((9,)),
            pltpu.SemaphoreType.DMA((2,)),
            pltpu.SemaphoreType.DMA((3, tokens // group)),
            pltpu.SemaphoreType.DMA((3, 2, 11)),
            pltpu.SemaphoreType.REGULAR,
        ]
        + line_scratch((tokens, width), chunk),
        compiler_params=pltpu.CompilerParams(
            collective_id=2, has_side_effects=True, vmem_limit_bytes=60 << 20
        ),
        cost_estimate=pl.CostEstimate(
            flops=100_000_000_000, bytes_accessed=50_000_000, transcendentals=1_000_000
        ),
        name="middle_stage",
    )(att_all, w_out_all, x, w_gate, w_up, w_down, cot, gain)


def finish_kernel(nq, nk, ffn, attn, gt, act, gate, up, down, q, k, v, o, gt_out, act_out):
    ff = gate.shape[1]
    gate[...] = ffn[:, 0:ff].astype(F32)
    up[...] = ffn[:, ff : 2 * ff].astype(F32)
    down[...] = ffn[:, 2 * ff : 3 * ff].astype(F32).T
    q[...] = attn[0:nq].astype(F32).T
    k[...] = attn[nq : nq + nk].astype(F32)
    v[...] = attn[nq + nk : nq + 2 * nk].astype(F32)
    o[...] = attn[nq + 2 * nk :].astype(F32)
    gt_out[...] = gt[...]
    act_out[...] = act[...]


def finish(ffn, attn, gt, act, nq, nk):
    width, ff = ffn.shape[0], ffn.shape[1] // 3
    tokens, own = gt.shape[0], attn.shape[0] - nq - 2 * nk
    tile = 256
    wide = lambda *shape: jax.ShapeDtypeStruct(shape, F32)
    down = lambda rows: pl.BlockSpec((tile, rows), lambda i: (i, 0))
    side = lambda rows: pl.BlockSpec((rows, tile), lambda i: (0, i))
    return pl.pallas_call(
        functools.partial(finish_kernel, nq, nk),
        grid=(width // tile,),
        out_shape=(
            wide(width, ff),
            wide(width, ff),
            wide(ff, width),
            wide(width, nq),
            wide(nk, width),
            wide(nk, width),
            wide(own, width),
            jax.ShapeDtypeStruct(gt.shape, gt.dtype),
            jax.ShapeDtypeStruct(act.shape, act.dtype),
        ),
        in_specs=[down(3 * ff), side(attn.shape[0]), side(tokens), side(tokens)],
        out_specs=(
            down(ff),
            down(ff),
            side(ff),
            down(nq),
            side(nk),
            side(nk),
            side(own),
            side(tokens),
            side(tokens),
        ),
        compiler_params=pltpu.CompilerParams(vmem_limit_bytes=60 << 20),
        name="finish",
    )(ffn, attn, gt, act)


def shards(
    nz,
    tokens,
    block_order,
    attn_gain,
    w_query,
    w_key,
    w_value,
    w_out,
    mlp_gain,
    w_gate,
    w_up,
    w_down,
    cotangent,
):
    device = lax.axis_index("dp")
    n_dp = lax.axis_size("dp")
    member = device % GROUP_DEVS
    order_row = lax.dynamic_index_in_dim(block_order, device // GROUP_DEVS, 0, keepdims=False)
    by_slot = order_row[jnp.bitwise_xor(jnp.arange(GROUP_DEVS), member)]
    own_block = by_slot[0]
    bias = jnp.where(by_slot <= own_block, 0.0, NEG).astype(F32)
    offsets = jnp.arange(PB, dtype=jnp.int32)
    places = jnp.concatenate([own_block * PB + offsets, GROUP_DEVS * PB + offsets])
    halfway = HEAD_DIM // 2
    frequency = ROTARY_BASE ** (-(jnp.arange(halfway, dtype=F32) * 2.0) / HEAD_DIM)
    angle = frequency[:, None] * places.astype(F32)[None, :]
    cosine, sine = jnp.cos(angle), jnp.sin(angle)

    count = tokens.shape[0]
    heads = w_query.shape[1] // HEAD_DIM
    queries, kv, normed, att_all, kv_all, lse, w_out_all = forward_attention(
        nz,
        tokens,
        w_query,
        w_key.T,
        w_value.T,
        cosine,
        sine,
        attn_gain[None],
        w_out,
        bias,
    )
    grad_attended, row_inner, grad_w_out, grad_gain_two, grad_attention, middle, feed_part, _, ffn_piece = (
        middle_stage(
            nz,
            att_all.reshape(-1, count),
            w_out_all,
            tokens,
            w_gate,
            w_up,
            w_down,
            cotangent,
            mlp_gain[None],
        )
    )
    activations, grad_tokens, gains, grad_attn, grad_ffn = tail_stage(
        nz,
        queries,
        kv,
        grad_attended.reshape(heads, HEAD_DIM, count),
        bias,
        lse,
        row_inner,
        feed_part,
        cosine,
        sine,
        attn_gain[None],
        grad_gain_two,
        kv_all,
        middle,
        ffn_piece,
        normed,
        tokens,
        grad_attention,
        w_query,
        w_key.T,
        w_value.T,
        grad_w_out,
    )
    if n_dp > GROUP_DEVS:
        gains = lax.psum(gains, "dp") * (1.0 / GROUP_DEVS)
        grad_attn = lax.psum(grad_attn.astype(F32), "dp") * (1.0 / GROUP_DEVS)
        grad_ffn = lax.psum(grad_ffn.astype(F32), "dp") * (1.0 / GROUP_DEVS)
    nq, nk = w_query.shape[1], w_key.shape[1]

    gate, up, down, query, key, value, out, grad_tokens, activations = finish(
        grad_ffn, grad_attn, grad_tokens, activations, nq, nk
    )
    return (
        activations,
        grad_tokens,
        gains[0],
        query,
        key.T,
        value.T,
        out,
        gains[1],
        gate,
        up,
        down,
    )


def solution(mesh):
    in_specs = (
        P("dp", None),
        P(),
        P(),
        P(None, "tensor"),
        P(None, "tensor"),
        P(None, "tensor"),
        P("tensor", None),
        P(),
        P(None, "tensor"),
        P(None, "tensor"),
        P("tensor", None),
        P("dp", None),
    )
    out_specs = (
        P("dp", None),
        P("dp", None),
        P(),
        P(None, "tensor"),
        P(None, "tensor"),
        P(None, "tensor"),
        P("tensor", None),
        P(),
        P(None, "tensor"),
        P(None, "tensor"),
        P("tensor", None),
    )
    return jax.shard_map(
        functools.partial(shards, mesh.shape["tensor"]),
        mesh=mesh,
        in_specs=in_specs,
        out_specs=out_specs,
        check_vma=False,
    )
```

```python
import functools

import jax
import jax.numpy as jnp
from jax import lax
from jax.experimental import pallas as pl
from jax.experimental.pallas import tpu as pltpu
from jax.sharding import PartitionSpec as P

HEAD_DIM = 96
GROUP_DEVS = 8
PB = 512
CL = 512
EPSILON = 1e-05
ROTARY_BASE = 100000.0
LOG2E = 1.4426950408889634
NEG = -1e30
MESH = pl.DeviceIdType.MESH
VM = pltpu.VMEM
F32 = jnp.float32
BF16 = jnp.bfloat16
NT = (((1,), (1,)), ((), ()))


def dot(a, b):
    return jnp.dot(a, b, preferred_element_type=F32)


def dot_nt(a, b):
    return lax.dot_general(a, b, NT, preferred_element_type=F32)


def dot_tn(a, b):
    return lax.dot_general(a, b, (((0,), (0,)), ((), ())), preferred_element_type=F32)


def causal(s):
    key = lax.broadcasted_iota(jnp.int32, s.shape, 0)
    query = lax.broadcasted_iota(jnp.int32, s.shape, 1)
    return jnp.where(key <= query, s, NEG)


def greet(targets):
    barrier = pltpu.get_barrier_semaphore()
    for target in targets:
        pl.semaphore_signal(barrier, inc=1, device_id=target, device_id_type=MESH)
    pl.semaphore_wait(barrier, len(targets))


def remote(src, dst, send, recv, target):
    return pltpu.make_async_remote_copy(
        src_ref=src, dst_ref=dst, send_sem=send, recv_sem=recv, device_id=target, device_id_type=MESH
    )


class Line:
    def __init__(self, nz, chunk, part, out, held, sems, shift=0):
        self.d, self.z = lax.axis_index("dp"), lax.axis_index("tensor")
        self.shift = shift
        self.chunk, self.part, self.out, self.held = chunk, part, out, held
        self.ss, self.rr, self.fs, self.fr = sems
        self.count = part.shape[0] // chunk
        self.root, self.last = nz // 2 - 1, nz - 1

    def rows(self, c):
        if self.shift:
            c = lax.rem(c + self.shift, self.count)
        return pl.ds(pl.multiple_of(c * self.chunk, self.chunk), self.chunk)

    def batch(self, i, n):
        if self.shift:
            i = lax.rem(i + self.shift // n, self.count // n)
        return pl.ds(pl.multiple_of(i * self.chunk * n, self.chunk * n), self.chunk * n)

    def toward(self, c, side, src):
        rows = self.rows(c)
        target = self.z + 1 if side == 0 else self.z - 1
        return remote(
            src.at[rows],
            (self.out if side == 0 else self.held).at[rows],
            self.ss.at[side, c],
            self.rr.at[side, c],
            (self.d, target),
        )

    def final(self, c, side):
        rows = self.rows(c)
        target = self.z - 1 if side == 0 else self.z + 1
        return remote(
            self.out.at[rows], self.out.at[rows], self.fs.at[side, c], self.fr.at[c], (self.d, target)
        )

    def mine(self, c, side):
        rows = self.rows(c)
        arrived = (self.out if side == 0 else self.held)[rows]
        return arrived.astype(F32) + self.part[rows].astype(F32)

    def issue(self, c):
        @pl.when(self.z == 0)
        def _():
            self.toward(c, 0, self.part).start()

        @pl.when(self.z == self.last)
        def _():
            self.toward(c, 1, self.part).start()

    def service(self, c):
        @pl.when((self.z > self.root) & (self.z < self.last))
        def _():
            rows = self.rows(c)
            self.toward(c, 1, self.held).wait_recv()
            self.held[rows] = self.mine(c, 1).astype(BF16)
            self.toward(c, 1, self.held).start()

    def ready(self, c):
        @pl.when(self.z != self.root)
        def _():
            self.final(c, 1).wait_recv()

        @pl.when((self.z > self.root) & (self.z < self.last))
        def _():
            self.final(c, 1).start()

        @pl.when(self.z == self.root)
        def _():
            rows = self.rows(c)
            self.toward(c, 0, self.out).wait_recv()
            self.toward(c, 1, self.held).wait_recv()
            self.out[rows] = (self.mine(c, 0) + self.held[rows].astype(F32)).astype(BF16)
            self.final(c, 0).start()
            self.final(c, 1).start()

    def drain(self):
        def body(c, carry):
            @pl.when(self.z < self.root + 1)
            def _():
                @pl.when(self.z == 0)
                def _():
                    self.toward(c, 0, self.part).wait_send()

                @pl.when(self.z == self.root)
                def _():
                    self.final(c, 0).wait_send()
                    self.final(c, 1).wait_send()

            @pl.when(self.z > self.root)
            def _():
                self.toward(c, 1, self.part).wait_send()

                @pl.when(self.z < self.last)
                def _():
                    self.final(c, 1).wait_send()

            return carry

        lax.fori_loop(0, self.count, body, 0)


def line_scratch(shape, chunk):
    count = shape[0] // chunk
    return [VM(shape, BF16)] + [pltpu.SemaphoreType.DMA((2, count))] * 3 + [
        pltpu.SemaphoreType.DMA((count,))
    ]


def neighbours(nz):
    d, z = lax.axis_index("dp"), lax.axis_index("tensor")
    return [(d, lax.rem(z + 1, nz)), (d, lax.rem(z + nz - 1, nz))]


def plane(masks):
    d, z = lax.axis_index("dp"), lax.axis_index("tensor")
    return [(jnp.bitwise_xor(d, m), z) for m in masks]


def loop(start, stop, body):
    def step(i, carry):
        body(i)
        return carry

    lax.fori_loop(start, stop, step, 0)


def fold_rows(values):
    return jnp.sum(values.reshape(values.shape[0] // 8, 8, values.shape[1]), axis=0)


class Plane:
    def __init__(self, height, width, sems):
        self.d, self.z = lax.axis_index("dp"), lax.axis_index("tensor")
        member = lax.rem(self.d, GROUP_DEVS)
        self.core = lax.rem(member, 2)
        self.chip = member // 2
        self.bit = (lax.rem(self.chip, 2), self.chip // 2)
        self.height, self.half, self.sems = height, width // 2, sems

    def rows(self, chip, core):
        return pl.ds(pl.multiple_of((chip * 2 + core) * self.height, 16), self.height)

    def cols(self, colour):
        return pl.ds(colour * self.half, self.half)

    def at(self, first, x, y):
        return x + 2 * y if first == 0 else y + 2 * x

    def copy(self, i, src, dst, mask):
        return remote(
            src, dst, self.sems.at[0, i], self.sems.at[1, i], (jnp.bitwise_xor(self.d, mask), self.z)
        )


class PlaneReduce(Plane):
    def __init__(self, src, mine, near, far, last, sems):
        super().__init__(src.shape[0] // GROUP_DEVS, src.shape[1], sems)
        self.src, self.mine, self.near, self.far, self.last = src, mine, near, far, last

    def to_core(self, i):
        return self.copy(i, self.src.at[self.rows(i, 1 - self.core)], self.near(i), 1)

    def fetch(self, i):
        rows = self.src.at[self.rows(i, self.core)]
        return pltpu.make_async_copy(rows, self.mine, self.sems.at[0, 10])

    def part_of(self, i, colour):
        return self.near(i).at[:, self.cols(colour)]

    def first(self, colour, k):
        i = self.at(colour, 1 - self.bit[colour], k)
        return self.copy(
            4 + 2 * colour + k, self.part_of(i, colour), self.far(colour, k), 2 << colour
        )

    def second(self, colour):
        i = self.at(colour, self.bit[colour], 1 - self.bit[1 - colour])
        return self.copy(8 + colour, self.part_of(i, colour), self.last(colour), 4 >> colour)

    def start(self):
        for i in range(4):
            self.to_core(i).start()
        if self.mine is not None:
            self.fetch(0).start()

    def after_core(self):
        for i in range(4):
            self.to_core(i).wait_recv()
            if self.mine is not None:
                self.fetch(i).wait()
                own = self.mine[...]
            else:
                own = self.src[self.rows(i, self.core)]
            near = self.near(i)
            near[...] = (own.astype(F32) + near[...].astype(F32)).astype(BF16)
            if self.mine is not None and i < 3:
                self.fetch(i + 1).start()
        for colour in range(2):
            for k in range(2):
                self.first(colour, k).start()

    def after_first(self):
        for colour in range(2):
            for k in range(2):
                self.first(colour, k).wait_recv()
                mine = self.part_of(self.at(colour, self.bit[colour], k), colour)
                mine[...] = (
                    mine[...].astype(F32) + self.far(colour, k)[...].astype(F32)
                ).astype(BF16)
        for colour in range(2):
            self.second(colour).start()

    def result(self, out):
        for colour in range(2):
            self.second(colour).wait_recv()
            out[:, self.cols(colour)] = (
                self.part_of(self.chip, colour)[...].astype(F32)
                + self.last(colour)[...].astype(F32)
            ).astype(BF16)

    def finish(self):
        for i in range(4):
            self.to_core(i).wait_send()
        for colour in range(2):
            self.second(colour).wait_send()
            for k in range(2):
                self.first(colour, k).wait_send()


class PlaneGather(Plane):
    def __init__(self, piece, out, sems):
        super().__init__(piece.shape[0], piece.shape[1], sems)
        self.piece, self.out = piece, out

    def place(self, dx, dy, colour):
        chip = jnp.bitwise_xor(self.chip, dx + 2 * dy)
        return self.out.at[self.rows(chip, self.core), self.cols(colour)]

    def keep(self):
        own = self.out.at[self.rows(self.chip, self.core)]
        return pltpu.make_async_copy(self.piece, own, self.sems.at[0, 10])

    def first(self, colour):
        dst = self.place(0, 0, colour)
        return self.copy(colour, self.piece.at[:, self.cols(colour)], dst, 4 >> colour)

    def second(self, colour, k):
        there = self.place(0, k, colour) if colour == 0 else self.place(k, 0, colour)
        src = self.piece.at[:, self.cols(colour)] if k == 0 else there
        return self.copy(2 + 2 * colour + k, src, there, 2 << colour)

    def share(self, k):
        rows = self.out.at[self.rows(jnp.bitwise_xor(self.chip, k), self.core)]
        return self.copy(6 + k, self.piece if k == 0 else rows, rows, 1)

    def start(self):
        self.keep().start()
        for colour in range(2):
            self.first(colour).start()
        self.share(0).start()

    def after_first(self):
        for colour in range(2):
            self.second(colour, 0).start()
            self.first(colour).wait_recv()
            self.second(colour, 1).start()

    def after_second(self):
        for colour in range(2):
            for k in range(2):
                self.second(colour, k).wait_recv()
        for k in (1, 2, 3):
            self.share(k).start()

    def finish(self):
        self.keep().wait()
        for k in range(4):
            self.share(k).wait()
        for colour in range(2):
            self.first(colour).wait_send()
            for k in range(2):
                self.second(colour, k).wait_send()


class LineGather:
    def __init__(self, nz, place, send, recv):
        self.d, self.z = lax.axis_index("dp"), lax.axis_index("tensor")
        self.nz, self.place, self.send, self.recv = nz, place, send, recv

    def step(self, right, s):
        index, target = (self.z - s, self.z + 1) if right else (self.z + s, self.z - 1)
        there = (index >= 0) & (index < self.nz) & (target >= 0) & (target < self.nz)
        where = self.place(index)
        way = int(right)
        return there, remote(where, where, self.send.at[way, s], self.recv.at[way, s], (self.d, target))

    def arrive(self, right, s):
        index = self.z - 1 - s if right else self.z + 1 + s
        where = self.place(index)
        way = int(right)

        @pl.when((index >= 0) & (index < self.nz))
        def _():
            remote(
                where, where, self.send.at[way, s], self.recv.at[way, s], (self.d, self.z)
            ).wait_recv()

    def start(self, s):
        for right in (True, False):
            if s > 0:
                self.arrive(right, s - 1)
            there, copy = self.step(right, s)
            pl.when(there)(copy.start)

    def last(self):
        for right in (True, False):
            self.arrive(right, self.nz - 2)

    def drain(self):
        for right in (True, False):
            for s in range(self.nz - 1):
                there, copy = self.step(right, s)
                pl.when(there)(copy.wait_send)


def forward_kernel(
    nz, x_hbm, wq_hbm, wk_hbm, wv_hbm, cos_ref, sin_ref, gain_ref, wo_ref, bias_ref,
    q_ref, kv_ref, normed_hbm, att_hbm, kv_hbm, lse_ref, wo_all,
    x_in, normed, wq, wk, wv, att, kv_all, acc, top, total, ktok, mine,
    gs, gr, zs, zr, ws, wr, wp, load, leave, fetch, keep,
):
    heads = q_ref.shape[0]
    kvh = heads // 2
    d, z = lax.axis_index("dp"), lax.axis_index("tensor")
    some = mine.shape[0] // nz
    member = lax.rem(d, GROUP_DEVS)

    def own_place(index):
        return mine.at[pl.ds(pl.multiple_of(index * some, 16), some)]

    first_rows = pltpu.make_async_copy(
        wo_ref.at[pl.ds(pl.multiple_of(member * some, 16), some)], own_place(z), load.at[0]
    )
    first_rows.start()
    tokens = x_in.shape[0]
    group = 256
    groups = tokens // group

    def rows_of(j):
        return pl.ds(pl.multiple_of(j * group, group), group)

    x_loads = [
        pltpu.make_async_copy(x_hbm.at[rows_of(j)], x_in.at[rows_of(j)], fetch.at[j])
        for j in range(groups)
    ]
    w_loads = [
        pltpu.make_async_copy(src, dst, fetch.at[groups + n])
        for n, (src, dst) in enumerate(((wk_hbm, wk), (wv_hbm, wv), (wq_hbm, wq)))
    ]
    for copy in x_loads[:2] + w_loads[:2] + x_loads[2:] + w_loads[2:]:
        copy.start()

    def normed_out(j):
        return pltpu.make_async_copy(
            normed.at[rows_of(j)], normed_hbm.at[rows_of(j)], keep.at[j]
        )

    def turn(u, cols):
        half = HEAD_DIM // 2
        lower, upper = u[:half], u[half:]
        cosine, sine = cos_ref[:, cols], sin_ref[:, cols]
        return lower * cosine - upper * sine, upper * cosine + lower * sine

    def put_turned(ref, n, u, cols, scale):
        first, second = turn(u, cols)
        half = HEAD_DIM // 2
        ref[n, 0:half, cols] = (first * scale).astype(BF16)
        ref[n, half:HEAD_DIM, cols] = (second * scale).astype(BF16)

    def keys_values(j):
        cols = rows_of(j)
        x = x_in[cols].astype(F32)
        inverse = lax.rsqrt(jnp.mean(x * x, axis=-1, keepdims=True) + EPSILON)
        n = (x * inverse * gain_ref[...]).astype(BF16)
        normed[cols] = n
        normed_out(j).start()
        keys, values = dot_nt(wk[...], n), dot_nt(wv[...], n)
        for h in range(kvh):
            some = slice(h * HEAD_DIM, (h + 1) * HEAD_DIM)
            put_turned(kv_ref, h, keys[some], cols, 1.0)
            kv_ref[kvh + h, :, cols] = values[some].astype(BF16)

    for copy in x_loads[:2] + w_loads[:2]:
        copy.wait()
    loop(0, groups // 2, keys_values)
    greet(plane((1, 2, 4, 6)) + neighbours(nz))
    own = kv_ref.at[:, :, pl.ds(0, PB)]
    firsts = [
        remote(own, kv_all.at[m], gs.at[m], gr.at[m], target)
        for m, target in zip((1, 2, 4, 6), plane((1, 2, 4, 6)))
    ]
    for copy in firsts:
        copy.start()
    w_line = LineGather(nz, own_place, ws, wr)
    w_plane = PlaneGather(mine, wo_all, wp)
    first_rows.wait()
    w_line.start(0)
    for copy in x_loads[2:] + w_loads[2:]:
        copy.wait()
    loop(groups // 2, groups, keys_values)
    w_rows = wq[...].T

    def queries(j):
        cols = rows_of(j)
        u = dot_nt(w_rows, normed[cols])
        for head in range(heads):
            some = slice(head * HEAD_DIM, (head + 1) * HEAD_DIM)
            put_turned(q_ref, head, u[some], cols, HEAD_DIM ** (-0.5) * LOG2E)

    for j in range(groups):
        queries(j)
    kv_all[0] = kv_ref[:, :, 0:PB]
    for h in range(kvh):
        ktok[8, h] = kv_ref[h, :, PB : PB + CL].T
        ktok[0, h] = kv_ref[h, :, 0:PB].T
    acc[...] = jnp.zeros_like(acc)
    top[...] = jnp.full_like(top, NEG)
    total[...] = jnp.zeros_like(total)

    def block(head, half, key, value, mask, bias):
        cols = pl.ds(half * PB, PB)
        s = dot(key, q_ref[head, :, cols])
        if mask:
            s = causal(s)
        old = top[head, :, cols]
        high = jnp.max(s, axis=0, keepdims=True)
        new = jnp.maximum(old, high if bias is None else high + bias)
        p = jnp.exp2(s - (new if bias is None else new - bias))
        shrink = jnp.exp2(old - new)
        total[head, :, cols] = total[head, :, cols] * shrink + jnp.sum(p, axis=0, keepdims=True)
        acc[head, :, cols] = acc[head, :, cols] * shrink + dot(value, p.astype(BF16))
        top[head, :, cols] = new

    def slot_step(slot, half, mask=False, bias=None):
        for head in range(heads):
            block(head, half, ktok[slot, head // 2], kv_all[slot, kvh + head // 2], mask, bias)

    for head in range(heads):
        block(head, 1, ktok[8, head // 2], kv_ref[kvh + head // 2, :, PB : PB + CL], True, None)

    def arrive(m):
        remote(kv_all.at[m], kv_all.at[m], gs.at[m], gr.at[m], (d, z)).wait_recv()

    def hand_on(m):
        return remote(kv_all.at[m], kv_all.at[m + 1], gs.at[m + 1], gr.at[m + 1], plane((1,))[0])

    def tail_slot(m):
        @pl.when(m > 0)
        def _():
            arrive(m)
            for h in range(kvh):
                ktok[m, h] = kv_all[m, h].T

        @pl.when((m > 0) & (lax.rem(m, 2) == 0))
        def _():
            hand_on(m).start()

        for s in range(1, nz - 1):

            @pl.when(m == 2 * s)
            def _():
                w_line.start(s)

        @pl.when(m == GROUP_DEVS - 1)
        def _():
            w_line.last()
            w_plane.start()

        slot_step(m, 1)

    loop(0, GROUP_DEVS, tail_slot)

    def finish(half):
        cols = pl.ds(half * PB, PB)
        for head in range(heads):
            att[z, pl.ds(head * HEAD_DIM, HEAD_DIM), cols] = (
                acc[head, :, cols] / total[head, :, cols]
            ).astype(BF16)
            lse_ref[head, :, cols] = top[head, :, cols] + jnp.log2(total[head, :, cols])

    lines = [
        LineGather(
            nz,
            lambda index, half=half: att.at[index, :, pl.ds(half * PB, PB)],
            zs.at[half],
            zr.at[half],
        )
        for half in range(2)
    ]
    kv_out = pltpu.make_async_copy(kv_all, kv_hbm, leave.at[2])
    kv_out.start()

    def att_out(half):
        there = (slice(None), slice(None), pl.ds(half * PB, PB))
        return pltpu.make_async_copy(att.at[there], att_hbm.at[there], leave.at[half])

    finish(1)
    lines[1].start(0)
    slot_step(0, 0, mask=True)

    def prompt_slot(m):
        slot_step(m, 0, bias=bias_ref[m])

        @pl.when(m == 4)
        def _():
            w_plane.after_first()
            lines[1].start(1)

    loop(1, GROUP_DEVS, prompt_slot)
    finish(0)
    lines[0].start(0)
    w_plane.after_second()
    for s in range(2, nz - 1):
        lines[1].start(s)
    for s in range(1, nz - 1):
        lines[0].start(s)
    for half in (1, 0):
        lines[half].last()
        att_out(half).start()
    for line in lines + [w_line]:
        line.drain()
    w_plane.finish()
    for copy in firsts:
        copy.wait_send()
    for m in (2, 4, 6):
        hand_on(m).wait_send()
    kv_out.wait()
    for j in range(groups):
        normed_out(j).wait()
    for half in range(2):
        att_out(half).wait()


def forward_attention(nz, x, w_query, w_key, w_value, cosine, sine, gain, w_out, bias):
    tokens = x.shape[0]
    heads, kvh = w_query.shape[1] // HEAD_DIM, w_key.shape[0] // HEAD_DIM
    own, width = w_out.shape
    anywhere = pl.BlockSpec(memory_space=pl.ANY)
    vmem = pl.BlockSpec(memory_space=VM)
    return pl.pallas_call(
        functools.partial(forward_kernel, nz),
        out_shape=(
            jax.ShapeDtypeStruct((heads, HEAD_DIM, tokens), BF16),
            jax.ShapeDtypeStruct((2 * kvh, HEAD_DIM, tokens), BF16),
            jax.ShapeDtypeStruct(x.shape, BF16),
            jax.ShapeDtypeStruct((nz, heads * HEAD_DIM, tokens), BF16),
            jax.ShapeDtypeStruct((GROUP_DEVS, 2 * kvh, HEAD_DIM, PB), BF16),
            jax.ShapeDtypeStruct((heads, 1, tokens), F32),
            jax.ShapeDtypeStruct((nz * own, width), BF16),
        ),
        in_specs=[anywhere] * 4
        + [vmem] * 3
        + [anywhere, pl.BlockSpec(memory_space=pltpu.SMEM)],
        out_specs=(vmem, vmem, anywhere, anywhere, anywhere, vmem, anywhere),
        scratch_shapes=[
            VM(x.shape, BF16),
            VM(x.shape, BF16),
            VM(w_query.shape, BF16),
            VM(w_key.shape, BF16),
            VM(w_value.shape, BF16),
            VM((nz, heads * HEAD_DIM, tokens), BF16),
            VM((GROUP_DEVS, 2 * kvh, HEAD_DIM, PB), BF16),
            VM((heads, HEAD_DIM, tokens), F32),
            VM((heads, 1, tokens), F32),
            VM((heads, 1, tokens), F32),
            VM((GROUP_DEVS + 1, kvh, PB, HEAD_DIM), BF16),
            VM((nz * own // GROUP_DEVS, width), BF16),
            pltpu.SemaphoreType.DMA((GROUP_DEVS,)),
            pltpu.SemaphoreType.DMA((GROUP_DEVS,)),
            pltpu.SemaphoreType.DMA((2, 2, nz - 1)),
            pltpu.SemaphoreType.DMA((2, 2, nz - 1)),
            pltpu.SemaphoreType.DMA((2, nz - 1)),
            pltpu.SemaphoreType.DMA((2, nz - 1)),
            pltpu.SemaphoreType.DMA((2, 11)),
            pltpu.SemaphoreType.DMA((1,)),
            pltpu.SemaphoreType.DMA((3,)),
            pltpu.SemaphoreType.DMA((tokens // 256 + 3,)),
            pltpu.SemaphoreType.DMA((tokens // 256,)),
        ],
        compiler_params=pltpu.CompilerParams(
            collective_id=0, has_side_effects=True, vmem_limit_bytes=60 << 20
        ),
        cost_estimate=pl.CostEstimate(
            flops=40_000_000_000, bytes_accessed=12_000_000, transcendentals=19_000_000
        ),
        name="forward_attention",
    )(x, w_query, w_key, w_value, cosine, sine, gain, w_out, bias)


class Stream:
    def __init__(self, rows, count, ins, out):
        self.rows, self.count, self.ins, self.out = rows, count, ins, out

    def load(self, i):
        slot = lax.rem(i, 2)
        return [
            pltpu.make_async_copy(src.at[self.rows(i)], buf.at[slot], sem.at[slot])
            for src, buf, sem in self.ins
        ]

    def store(self, i):
        dst, buf, sem = self.out
        slot = lax.rem(i, 2)
        return pltpu.make_async_copy(buf.at[slot], dst.at[self.rows(i)], sem.at[slot])

    def prime(self):
        for i in range(2):
            for copy in self.load(i):
                copy.start()

    def take(self, i):
        for copy in self.load(i):
            copy.wait()

        @pl.when(i >= 2)
        def _():
            self.store(i - 2).wait()

    def give(self, i):
        self.store(i).start()

        @pl.when(i + 2 < self.count)
        def _():
            for copy in self.load(i + 2):
                copy.start()

    def flush(self):
        for i in range(self.count - 2, self.count):
            self.store(i).wait()


def tail_kernel(
    nz, chunk, q_ref, kv_ref, do_ref, bias_ref, lse_ref, inner_ref, feed, cos_ref, sin_ref,
    gain_ref, gain_two, kv_all, mid_hbm, ffn_hbm, normed_hbm, x_hbm, ga_hbm, wq_hbm, wk_hbm, wv_hbm,
    gwo_hbm,
    act, gt, gains, summed, ffn_sum,
    kvs, wq, wk, wv, dq, dkv, near, far, ktok, vtok, low, total, held, f_piece, part, total_one, held_one, weights, a_near, a_far, a_last, a_piece, tile_in,
    mid_in, act_out, x_in, ga_in, gt_out, accum, box,
    ss, rr, fs, fr, ss1, rr1, fs1, fr1, ns, nr, ps, pr, a_sems, ag_sems, fg_sems, bs, br,
    loads, kv_sem, m_sem, act_sem, x_sem, g_sem, gt_sem,
):
    heads = q_ref.shape[0]
    kvh = heads // 2
    d, z = lax.axis_index("dp"), lax.axis_index("tensor")
    member = lax.rem(d, GROUP_DEVS)
    masks = range(1, GROUP_DEVS)
    nq = heads * HEAD_DIM
    nkv = kvh * HEAD_DIM
    tokens, width = feed.shape
    pairs = (
        (wq_hbm, wq),
        (wk_hbm, wk),
        (wv_hbm, wv),
        (gwo_hbm, weights.at[pl.ds(nq + 2 * nkv, gwo_hbm.shape[0])]),
    )
    fetches = [pltpu.make_async_copy(src, dst, loads.at[i]) for i, (src, dst) in enumerate(pairs)]

    def kv_load(t):
        slot = lax.rem(2 * t + 1 + t // 4, GROUP_DEVS)
        return pltpu.make_async_copy(
            kv_all.at[slot], kvs.at[lax.rem(t, 2)], kv_sem.at[lax.rem(t, 2)]
        )

    kv_load(0).start()
    first_piece = pltpu.make_async_copy(ffn_hbm, f_piece, loads.at[len(pairs)])
    first_piece.start()
    batch = 4
    line = Line(nz, chunk, feed, total, held, (ss, rr, fs, fr))
    line_one = Line(
        nz, chunk, part, total_one, held_one, (ss1, rr1, fs1, fr1), shift=tokens // chunk // 2
    )
    batches = line.count // batch
    acts = Stream(
        lambda i: line.batch(i, batch), batches, [(mid_hbm, mid_in, m_sem)], (act, act_out, act_sem)
    )
    outs = Stream(
        lambda i: line_one.batch(i, batch),
        batches,
        [(x_hbm, x_in, x_sem), (ga_hbm, ga_in, g_sem)],
        (gt, gt_out, gt_sem),
    )
    acts.prime()
    greet(neighbours(nz) + plane(masks))
    reduce_attn = PlaneReduce(
        weights,
        None,
        lambda i: a_near.at[i],
        lambda c, k: a_far.at[c, k],
        lambda c: a_last.at[c],
        a_sems,
    )
    gather_attn = PlaneGather(a_piece, summed, ag_sems)
    gather_ffn = PlaneGather(f_piece, ffn_sum, fg_sems)
    loop(0, line.count, line.issue)
    first_piece.wait()
    gather_ffn.start()
    for copy in fetches:
        copy.start()
    lag = 12
    ply = 2

    def ripple(s):
        @pl.when(s < line.count)
        def _():
            line.service(s)

        @pl.when(s >= lag)
        def _():
            line.ready(s - lag)

        @pl.when((s >= lag) & (lax.rem(s - lag, batch) == batch - 1))
        def _():
            i = (s - lag) // batch
            acts.take(i)
            act_out[lax.rem(i, 2)] = (
                mid_in[lax.rem(i, 2)].astype(F32) + total[line.batch(i, batch)].astype(F32)
            ).astype(BF16)
            acts.give(i)

    def background(s):
        @pl.when(s == 8)
        def _():
            gather_ffn.after_first()

        @pl.when(s == 22)
        def _():
            gather_ffn.after_second()

        loop(s * ply, s * ply + ply, ripple)

    dq[...] = jnp.zeros_like(dq)

    def block(head, half, keyt, mask, bias):
        h = head // 2
        cols = pl.ds(half * PB, PB)
        s = dot(ktok[h], q_ref[head, :, cols])
        if mask:
            s = causal(s)
        shift = lse_ref[head, :, cols]
        if bias is not None:
            shift = shift - bias
        p = jnp.exp2(s - shift)
        dp = dot(vtok[h], do_ref[head, :, cols])
        ds = (p * (dp - inner_ref[head, :, cols])).astype(BF16)
        dq[head, :, cols] += dot(keyt, ds)
        dv = dot_nt(do_ref[head, :, cols], p.astype(BF16))
        dk = dot_nt(q_ref[head, :, cols], ds)
        return dk, dv

    def total_of(parts):
        out = parts[0]
        for piece in parts[1:]:
            out = out + piece
        return out

    def turn_back(u, half):
        cols = pl.ds(half * PB, PB)
        cosine, sine = cos_ref[:, cols], sin_ref[:, cols]
        lower, upper = u[: HEAD_DIM // 2], u[HEAD_DIM // 2 :]
        return lower * cosine + upper * sine, upper * cosine - lower * sine

    def put_low(row, half, u, turned):
        cols = pl.ds(half * PB, PB)
        if not turned:
            low[pl.ds(row, HEAD_DIM), cols] = u.astype(BF16)
            return
        first, second = turn_back(u, half)
        low[pl.ds(row, HEAD_DIM // 2), cols] = first.astype(BF16)
        low[pl.ds(row + HEAD_DIM // 2, HEAD_DIM // 2), cols] = second.astype(BF16)

    for h in range(kvh):
        ktok[h] = kv_ref[h, :, PB : PB + CL].T
        vtok[h] = kv_ref[kvh + h, :, PB : PB + CL].T
    for h in range(kvh):
        both = [block(2 * h + r, 1, kv_ref[h, :, PB : PB + CL], True, None) for r in range(2)]
        put_low(nq + h * HEAD_DIM, 1, total_of([b[0] for b in both]) * (1.0 / LOG2E), True)
        put_low(nq + nkv + h * HEAD_DIM, 1, total_of([b[1] for b in both]), False)

    quarter = GROUP_DEVS // 2

    def slot_step(t, where, first):
        kv_load(t).wait()
        now = lax.rem(t, 2)
        for h in range(kvh):
            ktok[h] = kvs[now, h].T
            vtok[h] = kvs[now, kvh + h].T
        bias = None if first else bias_ref[lax.rem(2 * t + 1 + t // 4, GROUP_DEVS)]
        for h in range(kvh):
            both = []
            for r in range(2):
                background(t * 4 + h * 2 + r)
                both.append(block(2 * h + r, 1, kvs[now, h], False, None))
                both.append(block(2 * h + r, 0, kvs[now, h], first, bias))
            dkv[where, h] = (total_of([b[0] for b in both]) * (1.0 / LOG2E)).astype(BF16)
            dkv[where, kvh + h] = total_of([b[1] for b in both]).astype(BF16)

    def to_near(i):
        return remote(dkv.at[i], near.at[i], ns.at[i], nr.at[i], plane((1,))[0])

    def to_far(i):
        return remote(near.at[i], far.at[i], ps.at[i], pr.at[i], (jnp.bitwise_xor(d, 2 * i), z))

    def step(t):
        kv_load(t + 1).start()
        slot_step(t, t - t // quarter * (t - quarter), False)

        @pl.when(t < quarter)
        def _():
            to_near(t).start()

        @pl.when(t >= quarter)
        def _():
            i = t - quarter + 1
            to_near(i).wait_recv()
            near[i] = (dkv[quarter].astype(F32) + near[i].astype(F32)).astype(BF16)
            to_far(i).start()

    last = GROUP_DEVS - 1
    loop(0, last, step)
    slot_step(last, quarter, True)

    def back(j):
        group = tokens // 4
        rows = pl.ds(pl.multiple_of(j * group, group), group)
        a = [low[pl.ds(at, n), rows].T for at, n in ((0, nq), (nq, nkv), (nq + nkv, nkv))]
        size = 512
        for t in range(width // size):
            cols = pl.ds(t * size, size)
            part[rows, cols] = (
                dot_nt(a[0], wq[cols]) + dot(a[1], wk[:, cols]) + dot(a[2], wv[:, cols])
            ).astype(BF16)

    for copy in fetches:
        copy.wait()
    done = 4 * GROUP_DEVS * ply
    left = line.count + lag - done
    share = left // 4
    half_count = line.count // 2
    for head in range(heads):
        put_low(head * HEAD_DIM, 1, dq[head, :, PB : PB + CL] * HEAD_DIM ** (-0.5), True)
    loop(2, 4, back)
    loop(0, half_count, line_one.issue)
    loop(done, done + share, ripple)
    for head in range(heads):
        put_low(head * HEAD_DIM, 0, dq[head, :, 0:PB] * HEAD_DIM ** (-0.5), True)
    to_near(0).wait_recv()
    for i in range(1, quarter):
        to_far(i).wait_recv()
    for h in range(2 * kvh):
        home = dkv[quarter, h].astype(F32)
        home = home + near[0, h].astype(F32)
        for i in range(1, quarter):
            home = home + far[i, h].astype(F32)
        put_low(nq + h * HEAD_DIM, 0, home, h < kvh)
    loop(0, 2, back)
    loop(half_count, line.count, line_one.issue)
    loop(done + share, done + 2 * share, ripple)
    outs.prime()
    size = tile_in.shape[1]

    def tile_load(t):
        return pltpu.make_async_copy(
            normed_hbm.at[:, pl.ds(t * size, size)], tile_in, loads.at[len(pairs)]
        )

    def tile_step(t):
        tile_load(t).wait()
        weights[0 : nq + 2 * nkv, pl.ds(t * size, size)] = dot(low[...], tile_in[...]).astype(BF16)
        if t + 1 < width // size:
            tile_load(t + 1).start()

    tile_load(0).start()
    loop(done + 2 * share, done + left, ripple)
    acts.flush()
    accum[...] = jnp.zeros_like(accum)
    gain = gain_ref[...]
    lag_one = 10

    def body(s):
        @pl.when(s < line_one.count)
        def _():
            line_one.service(s)

        @pl.when(s >= lag_one)
        def _():
            line_one.ready(s - lag_one)

        @pl.when((s >= lag_one) & (lax.rem(s - lag_one, batch) == batch - 1))
        def _():
            i = (s - lag_one) // batch
            outs.take(i)
            slot = lax.rem(i, 2)
            x = x_in[slot].astype(F32)
            inverse = lax.rsqrt(jnp.mean(x * x, axis=-1, keepdims=True) + EPSILON)
            upstream = total_one[line_one.batch(i, batch)].astype(F32)
            inner = upstream * gain
            through = inverse * inner - x * inverse**3 * jnp.mean(
                inner * x, axis=-1, keepdims=True
            )
            gt_out[slot] = (ga_in[slot].astype(F32) + through).astype(BF16)
            accum[...] += fold_rows(upstream * x * inverse)
            outs.give(i)

        for t in range(width // size):

            @pl.when(s == 4 + 5 * t)
            def _():
                tile_step(t)

        @pl.when(s == 15)
        def _():
            reduce_attn.start()

        @pl.when(s == 19)
        def _():
            reduce_attn.after_core()

        @pl.when(s == 31)
        def _():
            reduce_attn.after_first()

        @pl.when(s == 39)
        def _():
            reduce_attn.result(a_piece)
            gather_attn.start()

        @pl.when(s == 46)
        def _():
            gather_attn.after_first()

        @pl.when(s == 58)
        def _():
            gather_attn.after_second()

    loop(0, line_one.count + lag_one, body)
    box[member, 0:1] = jnp.sum(accum[...], axis=0, keepdims=True)
    box[member, 1:2] = gain_two[...]
    copies = [
        remote(box.at[member], box.at[member], bs.at[m], br.at[m], target)
        for m, target in zip(masks, plane(masks))
    ]
    for copy in copies:
        copy.start()
    outs.flush()
    for i in range(quarter):
        to_near(i).wait_send()
    for i in range(1, quarter):
        to_far(i).wait_send()
    line.drain()
    line_one.drain()
    reduce_attn.finish()
    gather_ffn.finish()
    gather_attn.finish()
    for copy in copies:
        copy.wait()
    result = box[0]
    for m in masks:
        result = result + box[m]
    gains[...] = result


def tail_stage(
    nz, q, kv, do, bias, lse, inner, feed, cosine, sine, gain, gain_two, kv_all, middle, ffn, normed,
    x, ga, w_query, w_key, w_value, grad_w_out, chunk=16,
):
    heads = q.shape[0]
    kvh = heads // 2
    tokens, width = feed.shape
    slot = (2 * kvh, HEAD_DIM, PB)
    n_attn = (heads + 2 * kvh) * HEAD_DIM + grad_w_out.shape[0]
    high, wide = ffn.shape
    low_high = n_attn // GROUP_DEVS
    count = tokens // chunk
    rows = 4 * chunk
    quarter = GROUP_DEVS // 2
    dma = lambda *shape: pltpu.SemaphoreType.DMA(shape)
    lines = [dma(2, count)] * 3 + [dma(count)]
    block = VM((2, rows, width), BF16)
    anywhere = pl.BlockSpec(memory_space=pl.ANY)
    vmem = pl.BlockSpec(memory_space=VM)
    return pl.pallas_call(
        functools.partial(tail_kernel, nz, chunk),
        out_shape=(
            jax.ShapeDtypeStruct(feed.shape, BF16),
            jax.ShapeDtypeStruct(feed.shape, BF16),
            jax.ShapeDtypeStruct((2, width), F32),
            jax.ShapeDtypeStruct((n_attn, width), BF16),
            jax.ShapeDtypeStruct((high * GROUP_DEVS, wide), BF16),
        ),
        in_specs=[vmem] * 3 + [pl.BlockSpec(memory_space=pltpu.SMEM)] + [vmem] * 7 + [anywhere] * 10,
        out_specs=(anywhere, anywhere, vmem, anywhere, anywhere),
        scratch_shapes=[
            VM((2,) + slot, BF16),
            VM(w_query.shape, BF16),
            VM(w_key.shape, BF16),
            VM(w_value.shape, BF16),
            VM((heads, HEAD_DIM, tokens), F32),
            VM((quarter + 1,) + slot, BF16),
            VM((quarter,) + slot, BF16),
            VM((quarter,) + slot, BF16),
            VM((kvh, PB, HEAD_DIM), BF16),
            VM((kvh, PB, HEAD_DIM), BF16),
            VM(((heads + 2 * kvh) * HEAD_DIM, tokens), BF16),
            VM(feed.shape, BF16),
            VM(feed.shape, BF16),
            VM((high, wide), BF16),
            VM(feed.shape, BF16),
            VM(feed.shape, BF16),
            VM(feed.shape, BF16),
            VM((n_attn, width), BF16),
            VM((4, low_high, width), BF16),
            VM((2, 2, low_high, width // 2), BF16),
            VM((2, low_high, width // 2), BF16),
            VM((low_high, width), BF16),
            VM((tokens, 512), BF16),
            block,
            block,
            block,
            block,
            block,
            VM((8, width), F32),
            VM((GROUP_DEVS, 2, width), F32),
        ]
        + lines * 2
        + [dma(quarter)] * 4
        + [dma(2, 11)] * 3
        + [dma(GROUP_DEVS)] * 2
        + [dma(5)]
        + [dma(2)] * 6,
        compiler_params=pltpu.CompilerParams(
            collective_id=1, has_side_effects=True, vmem_limit_bytes=60 << 20
        ),
        cost_estimate=pl.CostEstimate(
            flops=200_000_000_000, bytes_accessed=50_000_000, transcendentals=19_000_000
        ),
        name="tail_stage",
    )(
        q, kv, do, bias, lse, inner, feed, cosine, sine, gain, gain_two, kv_all, middle, ffn, normed,
        x, ga, w_query, w_key, w_value, grad_w_out,
    )


def middle_kernel(
    nz, chunk, att_hbm, wo_hbm, x_hbm, wg_hbm, wu_hbm, wd_hbm, cot_hbm, gain_ref,
    gatt, inner_out, gwo, gain_two, ga_hbm, mid_hbm, feed_hbm, gffn, piece,
    ga, mid, feed, att, wo, wg, wu, wd, cot, mid32, nt2, hidden, gg, gu, part, total, accum, stage,
    load, store, leave, r_sems, spent, held, ss, rr, fs, fr,
):
    z = lax.axis_index("tensor")
    group, slab = 256, 256
    tokens, width = mid.shape
    head, rest = pl.ds(0, group), pl.ds(group, tokens - group)
    pairs = (
        (x_hbm.at[head], mid.at[head]),
        (att_hbm.at[:, head], att.at[:, head]),
        (wg_hbm, wg),
        (wu_hbm, wu),
        (cot_hbm, cot),
        (wd_hbm, wd),
        (x_hbm.at[rest], mid.at[rest]),
        (att_hbm.at[:, rest], att.at[:, rest]),
    )
    loads = [pltpu.make_async_copy(src, dst, load.at[i]) for i, (src, dst) in enumerate(pairs)]
    own = gatt.shape[0]
    some = own // GROUP_DEVS

    def wo_rows(i):
        src = pl.ds(pl.multiple_of(i * some, 16), some)
        dst = pl.ds(pl.multiple_of(lax.rem(i, nz) * own + i // nz * some, 16), some)
        pltpu.make_async_copy(wo_hbm.at[src], wo.at[dst], load.at[len(pairs)]).start()

    for copy in loads[:2]:
        copy.start()
    loop(0, nz * GROUP_DEVS, wo_rows)
    for copy in loads[2:]:
        copy.start()
    greet(neighbours(nz) + plane((1, 2, 4)))
    ff = wg.shape[1]
    heads = own // HEAD_DIM
    per = group // chunk
    ply = 4
    quarters = per // ply
    tile = 512
    gain = gain_ref[...]
    accum[...] = jnp.zeros_like(accum)
    line = Line(nz, chunk, part, total, held, (ss, rr, fs, fr))
    mine = pl.ds(pl.multiple_of(z * own, own), own)
    lag = 12

    def out_of(n, g):
        src, dst = ((mid, mid_hbm), (feed, feed_hbm), (ga, ga_hbm))[n]
        rows = pl.ds(pl.multiple_of(g * group, group), group)
        return pltpu.make_async_copy(src.at[rows], dst.at[rows], leave.at[n, g])

    def settle(c):
        rows = line.batch(c, ply)
        m = mid[rows].astype(F32)
        inverse = lax.rsqrt(jnp.mean(m * m, axis=-1, keepdims=True) + EPSILON)
        upstream = total[rows].astype(F32)
        inner = upstream * gain
        through = inverse * inner - m * inverse**3 * jnp.mean(inner * m, axis=-1, keepdims=True)
        ga[rows] = (cot[rows].astype(F32) + through).astype(BF16)
        accum[...] += fold_rows(upstream * m * inverse)

        @pl.when(lax.rem(c, quarters) == quarters - 1)
        def _():
            out_of(2, c // quarters).start()
            block = pl.ds(pl.multiple_of((c // quarters) * group, group), group)
            back = dot_nt(wo[mine], ga[block])
            gatt[:, block] = back.astype(BF16)
            for head in range(heads):
                some = pl.ds(head * HEAD_DIM, HEAD_DIM)
                there = att[pl.ds(pl.multiple_of(z * own + head * HEAD_DIM, 32), HEAD_DIM), block]
                inner_out[head, :, block] = jnp.sum(
                    gatt[some, block].astype(F32) * there.astype(F32), axis=0, keepdims=True
                )

    def ripple(s):
        @pl.when(s < line.count)
        def _():
            line.service(s)

        @pl.when(s >= lag)
        def _():
            line.ready(s - lag)

        @pl.when((s >= lag) & (lax.rem(s - lag, ply) == ply - 1))
        def _():
            settle((s - lag) // ply)

    def tick(s):
        @pl.when(s >= 0)
        def _():
            loop(s * ply, s * ply + ply, ripple)

    for copy in loads[:2]:
        copy.wait()
    pltpu.make_async_copy(wo_hbm, wo, load.at[len(pairs)]).wait()

    def forward(j):
        @pl.when(j == 1)
        def _():
            for copy in loads[6:]:
                copy.wait()

        rows = pl.ds(pl.multiple_of(j * group, group), group)
        a = att[:, rows].T
        for t in range(width // tile):
            cols = pl.ds(t * tile, tile)
            mid32[:, cols] = mid[rows, cols].astype(F32) + dot(a, wo[:, cols])
        m = mid32[...]
        mid[rows] = m.astype(BF16)
        inverse = lax.rsqrt(jnp.mean(m * m, axis=-1, keepdims=True) + EPSILON)
        nt2[rows] = (m * inverse * gain).astype(BF16)

        @pl.when(j == 0)
        def _():
            for copy in loads[2:6]:
                copy.wait()

        tick(2 * j - 3)
        for t in range(ff // tile):
            cols = pl.ds(t * tile, tile)
            gate = dot(nt2[rows], wg[:, cols])
            up = dot(nt2[rows], wu[:, cols])
            back = dot_nt(cot[rows], wd[cols])
            sig = jax.nn.sigmoid(gate)
            silu = gate * sig
            hidden[rows, cols] = (silu * up).astype(BF16)
            gu[rows, cols] = (back * silu).astype(BF16)
            gg[rows, cols] = (back * up * (sig * (1.0 + gate * (1.0 - sig)))).astype(BF16)
        for t in range(width // tile):
            cols = pl.ds(t * tile, tile)
            part[rows, cols] = (dot_nt(gg[rows], wg[cols]) + dot_nt(gu[rows], wu[cols])).astype(BF16)
        loop(j * per, j * per + per, line.issue)
        for t in range(width // tile):
            cols = pl.ds(t * tile, tile)
            feed[rows, cols] = dot(hidden[rows], wd[:, cols]).astype(BF16)
        out_of(0, j).start()
        out_of(1, j).start()
        tick(2 * j - 2)

    steps = tokens // group
    loop(0, steps, forward)
    for target in plane((1, 2, 4)):
        pl.semaphore_signal(spent, inc=1, device_id=target, device_id_type=MESH)
    high, half = width // GROUP_DEVS, ff // 2

    def rows_of(n):
        return pl.ds(pl.multiple_of(n * high, 16), high)

    def reduce_of(q):
        src = gffn.at[:, pl.ds(q * ff, ff)]
        own = stage.at[0, pl.ds(0, high), pl.ds(q * ff, ff)]
        sems = r_sems.at[q]
        if q < 2:
            room = (wg, wu)[q]
            return PlaneReduce(
                src,
                own,
                lambda i: room.at[rows_of(i)],
                lambda c, n: room.at[rows_of(4 + n), pl.ds(c * half, half)],
                lambda c: room.at[rows_of(6), pl.ds(c * half, half)],
                sems,
            )
        return PlaneReduce(
            src,
            own,
            lambda i: wd.at[rows_of(i), pl.ds(0, ff)],
            lambda c, n: wd.at[rows_of(2 * c + n), pl.ds(ff, half)],
            lambda c: wd.at[rows_of(4), pl.ds(c * half, half)],
            sems,
        )

    reduces = [reduce_of(q) for q in range(3)]
    done = 2 * steps - 3
    slabs = width // slab

    def put(t):
        return pltpu.make_async_copy(
            stage.at[lax.rem(t, 2)],
            gffn.at[pl.ds(pl.multiple_of(t * slab, slab), slab)],
            store.at[lax.rem(t, 2)],
        )

    def weights(t):
        @pl.when(t >= 2)
        def _():
            put(t - 2).wait()

        slot = lax.rem(t, 2)
        cols = pl.ds(pl.multiple_of(t * slab, slab), slab)
        a = nt2[:, cols].T
        stage[slot, :, 0:ff] = dot(a, gg[...]).astype(BF16)
        stage[slot, :, ff : 2 * ff] = dot(a, gu[...]).astype(BF16)
        stage[slot, :, 2 * ff : 3 * ff] = dot(cot[:, cols].T, hidden[...]).astype(BF16)
        put(t).start()

        @pl.when(lax.rem(t, 2) == 1)
        def _():
            tick(done + t // 2)

    loop(0, slabs, weights)
    for t in (slabs - 2, slabs - 1):
        put(t).wait()
    pl.semaphore_wait(spent, 3)
    for reduce in reduces:
        reduce.start()
    begin, end = (done + slabs // 2) * ply, line.count + lag
    marks = (begin, begin + 7, begin + 29, end)
    loop(marks[0], marks[1], ripple)
    for reduce in reduces:
        reduce.after_core()
    loop(marks[1], marks[2], ripple)
    for reduce in reduces:
        reduce.after_first()
    loop(marks[2], marks[3], ripple)
    for t in range(width // tile):
        cols = pl.ds(t * tile, tile)
        gwo[:, cols] = dot(att[mine], ga[:, cols]).astype(BF16)
    gain_two[...] = jnp.sum(accum[...], axis=0, keepdims=True)
    for q in range(3):
        reduces[q].result(stage.at[1, pl.ds(0, high), pl.ds(q * ff, ff)])
    out = pltpu.make_async_copy(stage.at[1, pl.ds(0, high)], piece, store.at[0])
    out.start()
    for reduce in reduces:
        reduce.finish()
    line.drain()
    out.wait()
    for n in range(3):
        loop(0, steps, lambda g, n=n: out_of(n, g).wait())


def middle_stage(nz, att_all, w_out_all, x, w_gate, w_up, w_down, cot, gain, chunk=16):
    tokens, width = x.shape
    ff = w_gate.shape[1]
    own = w_out_all.shape[0] // nz
    heads = own // HEAD_DIM
    group, slab = 256, 256
    wide = jax.ShapeDtypeStruct((tokens, width), BF16)
    return pl.pallas_call(
        functools.partial(middle_kernel, nz, chunk),
        out_shape=(
            jax.ShapeDtypeStruct((own, tokens), BF16),
            jax.ShapeDtypeStruct((heads, 1, tokens), F32),
            jax.ShapeDtypeStruct((own, width), BF16),
            jax.ShapeDtypeStruct((1, width), F32),
            wide,
            wide,
            wide,
            jax.ShapeDtypeStruct((width, 3 * ff), BF16),
            jax.ShapeDtypeStruct((width // GROUP_DEVS, 3 * ff), BF16),
        ),
        in_specs=[pl.BlockSpec(memory_space=pl.ANY)] * 7 + [pl.BlockSpec(memory_space=VM)],
        out_specs=(pl.BlockSpec(memory_space=VM),) * 4 + (pl.BlockSpec(memory_space=pl.ANY),) * 5,
        scratch_shapes=[
            VM((tokens, width), BF16),
            VM((tokens, width), BF16),
            VM((tokens, width), BF16),
            VM(w_out_all.shape[:1] + (tokens,), BF16),
            VM(w_out_all.shape, BF16),
            VM((width, ff), BF16),
            VM((width, ff), BF16),
            VM((ff, width), BF16),
            VM((tokens, width), BF16),
            VM((group, width), F32),
            VM((tokens, width), BF16),
            VM((tokens, ff), BF16),
            VM((tokens, ff), BF16),
            VM((tokens, ff), BF16),
            VM((tokens, width), BF16),
            VM((tokens, width), BF16),
            VM((8, width), F32),
            VM((2, slab, 3 * ff), BF16),
            pltpu.SemaphoreType.DMA((9,)),
            pltpu.SemaphoreType.DMA((2,)),
            pltpu.SemaphoreType.DMA((3, tokens // group)),
            pltpu.SemaphoreType.DMA((3, 2, 11)),
            pltpu.SemaphoreType.REGULAR,
        ]
        + line_scratch((tokens, width), chunk),
        compiler_params=pltpu.CompilerParams(
            collective_id=2, has_side_effects=True, vmem_limit_bytes=60 << 20
        ),
        cost_estimate=pl.CostEstimate(
            flops=100_000_000_000, bytes_accessed=50_000_000, transcendentals=1_000_000
        ),
        name="middle_stage",
    )(att_all, w_out_all, x, w_gate, w_up, w_down, cot, gain)


def finish_kernel(nq, nk, ffn, attn, gt, act, gate, up, down, q, k, v, o, gt_out, act_out):
    ff = gate.shape[1]
    gate[...] = ffn[:, 0:ff].astype(F32)
    up[...] = ffn[:, ff : 2 * ff].astype(F32)
    down[...] = ffn[:, 2 * ff : 3 * ff].astype(F32).T
    q[...] = attn[0:nq].astype(F32).T
    k[...] = attn[nq : nq + nk].astype(F32)
    v[...] = attn[nq + nk : nq + 2 * nk].astype(F32)
    o[...] = attn[nq + 2 * nk :].astype(F32)
    gt_out[...] = gt[...]
    act_out[...] = act[...]


def finish(ffn, attn, gt, act, nq, nk):
    width, ff = ffn.shape[0], ffn.shape[1] // 3
    tokens, own = gt.shape[0], attn.shape[0] - nq - 2 * nk
    tile = 256
    wide = lambda *shape: jax.ShapeDtypeStruct(shape, F32)
    down = lambda rows: pl.BlockSpec((tile, rows), lambda i: (i, 0))
    side = lambda rows: pl.BlockSpec((rows, tile), lambda i: (0, i))
    return pl.pallas_call(
        functools.partial(finish_kernel, nq, nk),
        grid=(width // tile,),
        out_shape=(
            wide(width, ff),
            wide(width, ff),
            wide(ff, width),
            wide(width, nq),
            wide(nk, width),
            wide(nk, width),
            wide(own, width),
            jax.ShapeDtypeStruct(gt.shape, gt.dtype),
            jax.ShapeDtypeStruct(act.shape, act.dtype),
        ),
        in_specs=[down(3 * ff), side(attn.shape[0]), side(tokens), side(tokens)],
        out_specs=(
            down(ff),
            down(ff),
            side(ff),
            down(nq),
            side(nk),
            side(nk),
            side(own),
            side(tokens),
            side(tokens),
        ),
        compiler_params=pltpu.CompilerParams(vmem_limit_bytes=60 << 20),
        name="finish",
    )(ffn, attn, gt, act)


def shards(
    nz,
    tokens,
    block_order,
    attn_gain,
    w_query,
    w_key,
    w_value,
    w_out,
    mlp_gain,
    w_gate,
    w_up,
    w_down,
    cotangent,
):
    device = lax.axis_index("dp")
    n_dp = lax.axis_size("dp")
    member = device % GROUP_DEVS
    order_row = lax.dynamic_index_in_dim(block_order, device // GROUP_DEVS, 0, keepdims=False)
    by_slot = order_row[jnp.bitwise_xor(jnp.arange(GROUP_DEVS), member)]
    own_block = by_slot[0]
    bias = jnp.where(by_slot <= own_block, 0.0, NEG).astype(F32)
    offsets = jnp.arange(PB, dtype=jnp.int32)
    places = jnp.concatenate([own_block * PB + offsets, GROUP_DEVS * PB + offsets])
    halfway = HEAD_DIM // 2
    frequency = ROTARY_BASE ** (-(jnp.arange(halfway, dtype=F32) * 2.0) / HEAD_DIM)
    angle = frequency[:, None] * places.astype(F32)[None, :]
    cosine, sine = jnp.cos(angle), jnp.sin(angle)

    count = tokens.shape[0]
    heads = w_query.shape[1] // HEAD_DIM
    queries, kv, normed, att_all, kv_all, lse, w_out_all = forward_attention(
        nz,
        tokens,
        w_query,
        w_key.T,
        w_value.T,
        cosine,
        sine,
        attn_gain[None],
        w_out,
        bias,
    )
    grad_attended, row_inner, grad_w_out, grad_gain_two, grad_attention, middle, feed_part, _, ffn_piece = (
        middle_stage(
            nz,
            att_all.reshape(-1, count),
            w_out_all,
            tokens,
            w_gate,
            w_up,
            w_down,
            cotangent,
            mlp_gain[None],
        )
    )
    activations, grad_tokens, gains, grad_attn, grad_ffn = tail_stage(
        nz,
        queries,
        kv,
        grad_attended.reshape(heads, HEAD_DIM, count),
        bias,
        lse,
        row_inner,
        feed_part,
        cosine,
        sine,
        attn_gain[None],
        grad_gain_two,
        kv_all,
        middle,
        ffn_piece,
        normed,
        tokens,
        grad_attention,
        w_query,
        w_key.T,
        w_value.T,
        grad_w_out,
    )
    if n_dp > GROUP_DEVS:
        gains = lax.psum(gains, "dp") * (1.0 / GROUP_DEVS)
        grad_attn = lax.psum(grad_attn.astype(F32), "dp") * (1.0 / GROUP_DEVS)
        grad_ffn = lax.psum(grad_ffn.astype(F32), "dp") * (1.0 / GROUP_DEVS)
    nq, nk = w_query.shape[1], w_key.shape[1]

    gate, up, down, query, key, value, out, grad_tokens, activations = finish(
        grad_ffn, grad_attn, grad_tokens, activations, nq, nk
    )
    return (
        activations,
        grad_tokens,
        gains[0],
        query,
        key.T,
        value.T,
        out,
        gains[1],
        gate,
        up,
        down,
    )


def solution(mesh):
    in_specs = (
        P("dp", None),
        P(),
        P(),
        P(None, "tensor"),
        P(None, "tensor"),
        P(None, "tensor"),
        P("tensor", None),
        P(),
        P(None, "tensor"),
        P(None, "tensor"),
        P("tensor", None),
        P("dp", None),
    )
    out_specs = (
        P("dp", None),
        P("dp", None),
        P(),
        P(None, "tensor"),
        P(None, "tensor"),
        P(None, "tensor"),
        P("tensor", None),
        P(),
        P(None, "tensor"),
        P(None, "tensor"),
        P("tensor", None),
    )
    return jax.shard_map(
        functools.partial(shards, mesh.shape["tensor"]),
        mesh=mesh,
        in_specs=in_specs,
        out_specs=out_specs,
        check_vma=False,
    )
```
